32 devices in a mesh: dp: 4 (over y, x), wide: 8 (over z, core).
Axes of the slice: x: 2, y: 2, z: 4, core: 2. Of those that a mesh axis runs over, the one named last changes fastest.
Arguments:
- tokens: bfloat16 [224, 196, 768], P(('dp', 'wide')), may hold values from -6 to 6
- norm1_gain: bfloat16 [768], replicated, may hold values from 0.5 to 1.5
- norm1_shift: bfloat16 [768], replicated, may hold values from -1.796875 to 1.796875
- qkv_weight: bfloat16 [768, 2304], replicated, may hold values from -0.21875 to 0.21875
- qv_bias: bfloat16 [2, 768], replicated, may hold values from -1.796875 to 1.796875
- rel_rows: bfloat16 [127, 64], replicated, may hold values from -0.8984375 to 0.8984375
- rel_cols: bfloat16 [127, 64], replicated, may hold values from -0.8984375 to 0.8984375
- out_weight: bfloat16 [768, 768], replicated, may hold values from -3.5 to 3.5
- out_bias: bfloat16 [768], replicated, may hold values from -1.796875 to 1.796875
- norm2_gain: bfloat16 [768], replicated, may hold values from 0.5 to 1.5
- norm2_shift: bfloat16 [768], replicated, may hold values from -1.796875 to 1.796875
- fc1_weight: bfloat16 [768, 3072], replicated, may hold values from -0.21875 to 0.21875
- fc1_bias: bfloat16 [3072], replicated, may hold values from -1.796875 to 1.796875
- fc2_weight: bfloat16 [3072, 768], replicated, may hold values from -0.109375 to 0.109375
- fc2_bias: bfloat16 [768], replicated, may hold values from -1.796875 to 1.796875
- window_place: int32 [200], P('dp'), may hold values from 0 to 55, as said below
- image_extent: int32 [8, 2], P('dp'), may hold values from 33 to 64, as said below
- box_mask: int32 [224, 196], P(('dp', 'wide')), may hold values 0 or 1
- out_grad: bfloat16 [224, 196, 768], P(('dp', 'wide')), may hold values from -6 to 6
Outputs:
- tokens_out: bfloat16 [224, 196, 768], P(('dp', 'wide'))
- tokens_grad: float32 [224, 196, 768], P(('dp', 'wide'))
- norm1_gain_grad: float32 [768], replicated
- norm1_shift_grad: float32 [768], replicated
- qkv_weight_grad: float32 [768, 2304], P('wide')
- qv_bias_grad: float32 [2, 768], replicated
- rel_rows_grad: float32 [127, 64], replicated
- rel_cols_grad: float32 [127, 64], replicated
- out_weight_grad: float32 [768, 768], P('wide')
- out_bias_grad: float32 [768], replicated
- norm2_gain_grad: float32 [768], replicated
- norm2_shift_grad: float32 [768], replicated
- fc1_weight_grad: float32 [768, 3072], P('wide')
- fc1_bias_grad: float32 [3072], replicated
- fc2_weight_grad: float32 [3072, 768], P('wide')
- fc2_bias_grad: float32 [768], replicated
The draws below stay inside these ranges and needn't reach their ends.
Inputs may be any that keep to these rules, and one draw needn't show every extreme that they name: `window_place`: window t = n * 25 + w of group-local image n of a group sits on device (t + s) mod 8 of wide for a shift s drawn per group (s = 7 in the first group), in one of that device's 7 slots; no two windows of a group share a slot. Counting the windows on one device a whose image is that of a pair, over each run of 3 consecutive (image, head) pairs numbered head * 2 + image, gives at most 11. `image_extent`: the first image of each group has content in all its rows and columns.
All inputs are finite; a program needn't handle non-finite values. No bound on the sum of `box_mask` on one device may be relied on, other than what follows from the above.
Results may differ from the reference program's by a relative error of at most 0.012.
Values may be sent and summed in bfloat16 or wider, within the bound.
No kernel may reach another device: no remote copies, remote signals or barrier semaphores. Data moves between devices by JAX's collectives and lax.ppermute only.
A program may use at most 320 MiB of HBM per device.

```python
import jax
import jax.numpy as jnp
from jax import lax

D = 768
HEADS = 12
HDIM = 64
MLP = 3072
GRID = 64
WIN = 14
WGRID = 5
RELS = 127
WINS = 25
WTOK = 196
IMG_GRP = 2
IMAGES = 8
WIN_DEV = 7
SLOTS = 224
N_DP = 4
N_WIDE = 8


def draw_window_place(key, part):
    window_total = IMG_GRP * WINS

    def one_group(group_key, group_id):
        turn_key, slot_key = jax.random.split(group_key)
        drawn_turn = jax.random.randint(turn_key, (), 0, N_WIDE)
        rotation = jnp.where(group_id == 0, N_WIDE - 1, drawn_turn)
        window_ids = jnp.arange(window_total, dtype=jnp.int32)
        devices = (window_ids + rotation) % N_WIDE
        rank_ids = window_ids // N_WIDE
        shuffles = jax.vmap(lambda device_key: jax.random.permutation(device_key, WIN_DEV))(jax.random.split(slot_key, N_WIDE))
        return (devices * WIN_DEV + shuffles[devices, rank_ids]).astype(jnp.int32)
    group_ids = jnp.arange(N_DP, dtype=jnp.int32)
    return jax.vmap(one_group)(jax.random.split(key, N_DP), group_ids).reshape(-1)


def draw_image_extent(key, part):
    drawn = jax.random.randint(key, (IMAGES, 2), GRID // 2 + 1, GRID + 1)
    leading = (jnp.arange(IMAGES, dtype=jnp.int32) % IMG_GRP == 0)[:, None]
    return jnp.where(leading, GRID, drawn).astype(jnp.int32)


def set_ends(values, own_key, low, largest):
    shape = values.shape
    spot = [jax.random.randint(jax.random.fold_in(own_key, axis), (), 0, shape[axis]) for axis in range(len(shape))]
    values = values.at[tuple(spot)].set(low)
    longest = shape.index(max(shape))
    spot[longest] = (spot[longest] + 1) % shape[longest]
    return values.at[tuple(spot)].set(largest)


def shard_levels(own_key, shape, shards, least, top_value):
    loudness = 1.0
    for dim, blocks in shards:
        heights = jax.random.uniform(jax.random.fold_in(jax.random.fold_in(own_key, 6), dim), (blocks,), jnp.float32, least / len(shards), top_value / len(shards))
        loudness = loudness * jnp.repeat(jnp.exp(heights), shape[dim] // blocks).reshape((-1,) + (1,) * (len(shape) - 1 - dim))
    return loudness


def gaussian(stream_key, dims, scale, most, cuts=(), kind=jnp.bfloat16):
    result = scale * jax.random.normal(stream_key, dims, jnp.float32)
    if cuts:
        result = result * shard_levels(stream_key, dims, cuts, -0.22, 0.18)
    return jnp.clip(result, -most, most).astype(kind)


def setup_inputs(seed: int = 0) -> dict:
    streams_of = jax.random.split(jax.random.key(seed), 20)
    tokens = gaussian(streams_of[0], (SLOTS, WTOK, D), 1.0, 6.0, ((0, 32),))
    norm1_gain = jnp.clip(1.0 + 0.1 * jax.random.normal(streams_of[1], (D,), jnp.float32), 0.5, 1.5).astype(jnp.bfloat16)
    norm1_shift = gaussian(streams_of[2], (D,), 0.3, 1.796875)
    qkv_weight = gaussian(streams_of[3], (D, 3 * D), D ** -0.5, 0.21875)
    qv_bias = gaussian(streams_of[4], (2, D), 0.3, 1.796875)
    rel_rows = gaussian(streams_of[5], (RELS, HDIM), 0.15, 0.8984375)
    rel_cols = gaussian(streams_of[6], (RELS, HDIM), 0.15, 0.8984375)
    out_weight = gaussian(streams_of[7], (D, D), (max(D // 256, 1)) ** -0.5, 3.5)
    out_bias = gaussian(streams_of[8], (D,), 0.3, 1.796875)
    norm2_gain = jnp.clip(1.0 + 0.1 * jax.random.normal(streams_of[9], (D,), jnp.float32), 0.5, 1.5).astype(jnp.bfloat16)
    norm2_shift = gaussian(streams_of[10], (D,), 0.3, 1.796875)
    fc1_weight = gaussian(streams_of[11], (D, MLP), D ** -0.5, 0.21875)
    fc1_bias = gaussian(streams_of[12], (MLP,), 0.3, 1.796875)
    fc2_weight = gaussian(streams_of[13], (MLP, D), MLP ** -0.5, 0.109375)
    fc2_bias = gaussian(streams_of[14], (D,), 0.3, 1.796875)
    window_place = draw_window_place(jax.random.fold_in(streams_of[19], 71), 0)
    image_extent = draw_image_extent(jax.random.fold_in(streams_of[19], 71), 0)
    box_mask = set_ends((jax.random.randint(streams_of[17], (SLOTS, WTOK), 0, 4) < 3).astype(jnp.int32), jax.random.fold_in(streams_of[17], 1), 0, 1)
    out_grad = gaussian(streams_of[18], (SLOTS, WTOK, D), 1.0, 6.0, ((0, 32),))
    return {"tokens": tokens, "norm1_gain": norm1_gain, "norm1_shift": norm1_shift, "qkv_weight": qkv_weight, "qv_bias": qv_bias, "rel_rows": rel_rows, "rel_cols": rel_cols, "out_weight": out_weight, "out_bias": out_bias, "norm2_gain": norm2_gain, "norm2_shift": norm2_shift, "fc1_weight": fc1_weight, "fc1_bias": fc1_bias, "fc2_weight": fc2_weight, "fc2_bias": fc2_bias, "window_place": window_place, "image_extent": image_extent, "box_mask": box_mask, "out_grad": out_grad}


@jax.custom_vjp
def low(v):
    return lax.optimization_barrier(v.astype(jnp.bfloat16)).astype(jnp.float32)

@jax.custom_vjp
def low_back(v):
    return v

def low_keep(v):
    return (low(v), None)

def low_pass(kept, grad):
    return (grad,)

def back_keep(v):
    return (v, None)

def back_low(kept, grad):
    return (low(grad),)
low.defvjp(low_keep, low_pass)
low_back.defvjp(back_keep, back_low)
norm_eps = 1e-06
mask_fill = -1000000000.0

def matmul(left, right):
    return jnp.dot(left, right, precision=lax.Precision.HIGHEST, preferred_element_type=jnp.float32)

def norm_rows(values, gain, shift):
    centre = values - lax.optimization_barrier(jnp.mean(values, axis=-1, keepdims=True))
    variance = lax.optimization_barrier(jnp.mean(centre * centre, axis=-1, keepdims=True))
    return centre * lax.rsqrt(variance + norm_eps) * gain + shift

def rel_table(table):
    offsets = jnp.arange(GRID, dtype=jnp.int32)[:, None] - jnp.arange(GRID, dtype=jnp.int32)[None, :] + GRID - 1
    return table[offsets]

def attend_head(queries, key_rows, values, row_position_table, column_position_table, row_bias_terms, column_bias_terms):
    patch_count = GRID * GRID
    block_rows = min(512, patch_count)
    block_count = patch_count // block_rows
    score_scale = HDIM ** (-0.5)
    exact_result = lax.Precision.HIGHEST
    patch_ids = jnp.arange(patch_count, dtype=jnp.int32)
    grid_rows = (patch_ids // GRID).reshape(block_count, block_rows)
    grid_cols = (patch_ids % GRID).reshape(block_count, block_rows)

    def one_block(pieces):
        query_tile_rows, row_block_terms, column_block_terms = pieces
        row_partial = jnp.einsum('ry,roy->ro', query_tile_rows, row_position_table[row_block_terms], precision=exact_result) + row_bias_terms[None, :]
        column_partial = jnp.einsum('ry,roy->ro', query_tile_rows, column_position_table[column_block_terms], precision=exact_result) + column_bias_terms[None, :]
        raw_scores = matmul(query_tile_rows * score_scale, key_rows.T)
        scores = raw_scores.reshape(block_rows, GRID, GRID) + row_partial[:, :, None] + column_partial[:, None, :]
        scores = low_back(scores.reshape(block_rows, patch_count))
        totals = jax.nn.logsumexp(scores, axis=-1, keepdims=True)
        weights = low(jnp.exp(scores - totals))
        return matmul(weights, values)
    outputs = lax.map(jax.checkpoint(one_block), (queries.reshape(block_count, block_rows, HDIM), grid_rows, grid_cols))
    return outputs.reshape(patch_count, HDIM)

def split_heads(matrix):
    return matrix.reshape(GRID * GRID, HEADS, HDIM).transpose(1, 0, 2)

def block_forward(patches, params, row_bias_terms, column_bias_terms):
    gain_one, shift_one, qkv_all, qv_shift, rows_rel, cols_rel, out_all, out_shift, gain_two, shift_two, first_all, first_shift, second_all, second_shift = params
    normed = low(norm_rows(patches, gain_one, shift_one))
    mixed = matmul(normed, qkv_all)
    queries = low_back(low(mixed[:, :D] + qv_shift[0]))
    key_rows = low_back(low(mixed[:, D:2 * D]))
    values = low_back(low(mixed[:, 2 * D:] + qv_shift[1]))
    row_position_table = rel_table(rows_rel)
    column_position_table = rel_table(cols_rel)

    def per_head(triple):
        return attend_head(triple[0], triple[1], triple[2], row_position_table, column_position_table, row_bias_terms, column_bias_terms)
    heads_out = lax.map(per_head, (split_heads(queries), split_heads(key_rows), split_heads(values)))
    attended = low_back(low(heads_out.transpose(1, 0, 2).reshape(GRID * GRID, D)))
    branch = low_back(matmul(attended, out_all) + out_shift)
    middle = patches + branch
    normed_two = low(norm_rows(middle, gain_two, shift_two))
    before = low_back(matmul(normed_two, first_all) + first_shift)
    activated = low(jax.nn.gelu(before, approximate=False))
    return middle + matmul(activated, second_all) + second_shift

def reference(tokens, norm1_gain, norm1_shift, qkv_weight, qv_bias, rel_rows, rel_cols, out_weight, out_bias, norm2_gain, norm2_shift, fc1_weight, fc1_bias, fc2_weight, fc2_bias, window_place, image_extent, box_mask, out_grad):
    params = tuple((weight.astype(jnp.float32) for weight in (norm1_gain, norm1_shift, qkv_weight, qv_bias, rel_rows, rel_cols, out_weight, out_bias, norm2_gain, norm2_shift, fc1_weight, fc1_bias, fc2_weight, fc2_bias)))
    slot_total = tokens.shape[0]
    flat_tokens = tokens.reshape(slot_total * WTOK, D)
    flat_grads = out_grad.reshape(slot_total * WTOK, D)
    flat_box = box_mask.reshape(slot_total * WTOK)
    group_slots = N_WIDE * WIN_DEV
    patch_ids = jnp.arange(GRID * GRID, dtype=jnp.int32)
    cell_rows = patch_ids // GRID
    cell_cols = patch_ids % GRID
    window_ids = cell_rows // WIN * WGRID + cell_cols // WIN
    cell_ids = cell_rows % WIN * WIN + cell_cols % WIN
    grid_ids = jnp.arange(GRID, dtype=jnp.int32)

    def one_image(running, image_id):
        group_id = image_id // IMG_GRP
        places = lax.dynamic_slice_in_dim(window_place, image_id * WINS, WINS)
        slot_ids = group_id * group_slots + places[window_ids]
        token_rows = (slot_ids * WTOK + cell_ids).astype(jnp.int32)
        patches = flat_tokens[token_rows].astype(jnp.float32)
        cotangent = flat_grads[token_rows].astype(jnp.float32) * flat_box[token_rows].astype(jnp.float32)[:, None]
        extent = image_extent[image_id]
        row_bias_terms = jnp.where(grid_ids < extent[0], 0.0, mask_fill).astype(jnp.float32)
        column_bias_terms = jnp.where(grid_ids < extent[1], 0.0, mask_fill).astype(jnp.float32)

        def forward(patch_values, param_values):
            return block_forward(patch_values, param_values, row_bias_terms, column_bias_terms)
        produced, pullback = jax.vjp(forward, patches, params)
        patch_grad, param_grad = pullback(cotangent)
        running = jax.tree.map(lambda first, second: first + second, running, param_grad)
        return (running, (produced, patch_grad, token_rows))
    initial = jax.tree.map(jnp.zeros_like, params)
    totals, (produced_all, grads_all, rows_all) = lax.scan(one_image, initial, jnp.arange(IMAGES, dtype=jnp.int32))
    flat_rows = rows_all.reshape(-1)
    tokens_out = jnp.zeros((slot_total * WTOK, D), jnp.float32).at[flat_rows].set(produced_all.reshape(-1, D))
    tokens_grad = jnp.zeros((slot_total * WTOK, D), jnp.float32).at[flat_rows].set(grads_all.reshape(-1, D))
    return (tokens_out.astype(jnp.bfloat16).reshape(slot_total, WTOK, D), tokens_grad.reshape(slot_total, WTOK, D), totals[0], totals[1], totals[2], totals[3], totals[4], totals[5], totals[6], totals[7], totals[8], totals[9], totals[10], totals[11], totals[12], totals[13])
```

```python
from functools import partial

import functools
import jax
import jax.numpy as jnp
from jax import lax
from jax.experimental import pallas as pl
from jax.experimental.pallas import tpu as pltpu
from jax.sharding import PartitionSpec as P

F32 = jnp.float32
BF = jnp.bfloat16
N = 4096
NEG = -1e9

D = 768
HEADS = 12
HDIM = 64
GRID = 64
WIN = 14
WGRID = 5
PAIR_DEV = 3
WINS = 25
WTOK = 196


norm_eps = 1e-06


def product(left, right):
    return jnp.dot(left, right, preferred_element_type=jnp.float32)


def product_left(left, right):
    return lax.dot_general(
        left, right, (((0,), (0,)), ((), ())), preferred_element_type=jnp.float32
    )


def product_right(left, right):
    return lax.dot_general(
        left, right, (((1,), (1,)), ((), ())), preferred_element_type=jnp.float32
    )


def head_major(matrix):
    rows = matrix.shape[0]
    return matrix.reshape(rows, 3, HEADS, HDIM).transpose(0, 2, 1, 3).reshape(rows, 3 * D)


def part_major(matrix):
    rows = matrix.shape[0]
    return matrix.reshape(rows, HEADS, 3, HDIM).transpose(0, 2, 1, 3).reshape(rows, 3 * D)


def norm_rows(values, gain, shift):
    centre = values - jnp.mean(values, axis=-1, keepdims=True)
    spread = lax.rsqrt(jnp.mean(centre * centre, axis=-1, keepdims=True) + norm_eps)
    scaled = centre * spread
    return (scaled * gain + shift, scaled, spread)


def norm_back(grad_rows, scaled, spread, gain):
    weighted = grad_rows * gain
    return spread * (
        weighted
        - jnp.mean(weighted, axis=-1, keepdims=True)
        - scaled * jnp.mean(weighted * scaled, axis=-1, keepdims=True)
    )


def send_plan(window_place, slot_count, image_count, wide_index, capacity, wide_count):
    window_total = window_place.shape[0]
    owners = window_place // slot_count
    placed = window_place % slot_count
    window_ids = jnp.arange(window_total, dtype=jnp.int32)
    slot_ids = jnp.arange(slot_count, dtype=jnp.int32)
    matches = (owners[None, :] == wide_index) & (placed[None, :] == slot_ids[:, None])
    occupied = jnp.any(matches, axis=1)
    window_of = jnp.sum(jnp.where(matches, window_ids[None, :], 0), axis=1)
    pair_of = (
        jnp.arange(HEADS, dtype=jnp.int32)[None, :] * image_count + (window_of // WINS)[:, None]
    )
    targets = (pair_of // PAIR_DEV).reshape(-1)
    ordering = (pair_of * window_total + window_of[:, None]).reshape(-1)
    live_items = jnp.repeat(occupied, HEADS)
    earlier = (
        live_items[None, :]
        & (targets[None, :] == targets[:, None])
        & (ordering[None, :] < ordering[:, None])
    )
    ranking = jnp.sum(earlier.astype(jnp.int32), axis=1)
    position = jnp.where(live_items, targets * capacity + ranking, wide_count * capacity)
    return (occupied, window_of, live_items, position)


def receive_plan(window_place, slot_count, image_count, wide_index, capacity):
    window_total = window_place.shape[0]
    owners = window_place // slot_count
    pair_ids = wide_index * PAIR_DEV + jnp.arange(PAIR_DEV, dtype=jnp.int32)
    pair_image = pair_ids % image_count
    window_of = (pair_image[:, None] * WINS + jnp.arange(WINS, dtype=jnp.int32)[None, :]).reshape(
        -1
    )
    picked = window_of[:, None] == jnp.arange(window_total, dtype=jnp.int32)[None, :]
    sender = jnp.sum(jnp.where(picked, owners[None, :], 0), axis=1)
    ordering = jnp.repeat(pair_ids, WINS) * window_total + window_of
    earlier = (sender[None, :] == sender[:, None]) & (ordering[None, :] < ordering[:, None])
    ranking = jnp.sum(earlier.astype(jnp.int32), axis=1)
    return (sender * capacity + ranking, pair_image)


def patch_mask(occupied, window_of):
    cell_ids = jnp.arange(WTOK, dtype=jnp.int32)
    local_window = window_of % WINS
    grid_row = (local_window // WGRID)[:, None] * WIN + (cell_ids // WIN)[None, :]
    grid_col = (local_window % WGRID)[:, None] * WIN + (cell_ids % WIN)[None, :]
    inside = occupied[:, None] & (grid_row < GRID) & (grid_col < GRID)
    return inside.astype(jnp.float32)


def to_items(values, slot_count, part_count):
    shaped = values.reshape(slot_count, WTOK, HEADS, part_count * HDIM).transpose(0, 2, 1, 3)
    return shaped.reshape(slot_count * HEADS, WTOK * part_count * HDIM)


def from_items(item_rows, slot_count, part_count):
    shaped = item_rows.reshape(slot_count, HEADS, WTOK, part_count * HDIM).transpose(0, 2, 1, 3)
    return shaped.reshape(slot_count * WTOK, HEADS * part_count * HDIM)


def pack_items(item_rows, targets, length, wide_count):
    blank_rows = jnp.zeros((length, item_rows.shape[1]), item_rows.dtype)
    filled = blank_rows.at[targets].set(item_rows, mode="drop")
    return filled.reshape(wide_count, length // wide_count, item_rows.shape[1])


def unpack_items(arrived, position, live_items, length):
    flattened = arrived.reshape(length, -1)
    picked = flattened[jnp.minimum(position, length - 1)]
    return jnp.where(live_items[:, None], picked, jnp.zeros_like(picked))


def grid_from_items(item_rows, pair_count, part_count):
    padded_side = WGRID * WIN
    shaped = item_rows.reshape(pair_count, WGRID, WGRID, WIN, WIN, part_count * HDIM)
    shaped = shaped.transpose(0, 1, 3, 2, 4, 5).reshape(
        pair_count, padded_side, padded_side, part_count * HDIM
    )
    return shaped[:, :GRID, :GRID].reshape(pair_count, GRID * GRID, part_count, HDIM)


def items_from_grid(grid_values, pair_count):
    channels = grid_values.shape[-1]
    margin = WGRID * WIN - GRID
    padded = jnp.pad(
        grid_values.reshape(pair_count, GRID, GRID, channels),
        ((0, 0), (0, margin), (0, margin), (0, 0)),
    )
    shaped = padded.reshape(pair_count, WGRID, WIN, WGRID, WIN, channels).transpose(
        0, 1, 3, 2, 4, 5
    )
    return shaped.reshape(pair_count * WINS, WTOK * channels)


def dot(a,b): return jnp.dot(a,b,preferred_element_type=F32)
def dotT(a,b): return lax.dot_general(a,b,(((1,),(1,)),((),())),preferred_element_type=F32)

def split(x):
    hi=x.astype(BF); lo=(x-hi.astype(F32)).astype(BF)
    return hi,lo

def onehots():
    f=lax.broadcasted_iota(jnp.int32,(192,2048),0)
    j=lax.broadcasted_iota(jnp.int32,(192,2048),1)
    col=(f%64)==(j%64)
    row=((f-128)%32)==(j//64)
    return jnp.where(f<128, col.astype(F32), row.astype(F32)).astype(BF)

def rel_feats(q, rel, ext_r, ext_c, row0, groups, sub=None):
    fr=dotT(q, rel[...])
    outs_r=[];outs_c=[]
    lane=lax.broadcasted_iota(jnp.int32,(64,128),1)
    mr=jnp.where(lane<ext_r,0.0,NEG); mc=jnp.where(lane<ext_c,0.0,NEG)
    for g in range(groups):
        r=row0+g
        a=pltpu.roll(fr[g*64:(g+1)*64,:128], (r+65)%128, 1)+mr
        c=pltpu.roll(fr[g*64:(g+1)*64,128:], 65, 1, stride=1, stride_axis=0)+mc
        outs_r.append(a); outs_c.append(c)
    R=jnp.concatenate(outs_r,0); C=jnp.concatenate(outs_c,0)
    return R,C

def make_lhs(q,R,C):
    rh,rl=split(R[:,:64]); ch,cl=split(C[:,:64])
    qs=(q.astype(F32)*0.125).astype(BF)
    A=jnp.concatenate([qs,ch,cl,rh[:,:32],rl[:,:32]],1)
    B=jnp.concatenate([qs,ch,cl,rh[:,32:],rl[:,32:]],1)
    return A,B

def fwd_kernel(ext_ref,q_ref,k_ref,v_ref,rel_ref,o_ref,oa_ref,kt,va,*,TQ):
    p=pl.program_id(0); t=pl.program_id(1)
    @pl.when((p==0)&(t==0))
    def _():
        oh=onehots()
        kt[64:,:2048]=oh; kt[64:,2048:]=oh
        va[:,64:]=jnp.where(lax.broadcasted_iota(jnp.int32,(N,64),1)==0,1.0,0.0).astype(BF)
    @pl.when(t==0)
    def _():
        kt[:64,:]=k_ref[0].astype(F32).T.astype(BF)
        va[:,:64]=v_ref[0]
    q=q_ref[0]
    R,C=rel_feats(q,rel_ref,ext_ref[p,0],ext_ref[p,1],t*(TQ//64),TQ//64)
    A,B=make_lhs(q,R,C)
    SA=dot(A,kt[:,:2048]); SB=dot(B,kt[:,2048:])
    m=jnp.maximum(jnp.max(SA,1,keepdims=True),jnp.max(SB,1,keepdims=True))
    PA=jnp.exp(SA-m).astype(BF); PB=jnp.exp(SB-m).astype(BF)
    acc=dot(PA,va[:2048,:])+dot(PB,va[2048:,:])
    l=acc[:,64:65]
    o=acc*(1.0/l)
    L=m+jnp.log(l)
    lane=lax.broadcasted_iota(jnp.int32,(TQ,128),1)
    oa_ref[0]=jnp.where(lane<64,o,L)
    o_ref[0]=o[:,:64].astype(BF)

def attn_fwd(ext, q, k, v, rel, TQ=256):
    Pn=q.shape[0]
    return pl.pallas_call(functools.partial(fwd_kernel,TQ=TQ),
      out_shape=(jax.ShapeDtypeStruct((Pn,N,64),BF),jax.ShapeDtypeStruct((Pn,N,128),F32)),
      grid_spec=pltpu.PrefetchScalarGridSpec(num_scalar_prefetch=1,grid=(Pn,N//TQ),
        in_specs=[pl.BlockSpec((1,TQ,64),lambda p,t,*_:(p,t,0)),
                  pl.BlockSpec((1,N,64),lambda p,t,*_:(p,0,0)),
                  pl.BlockSpec((1,N,64),lambda p,t,*_:(p,0,0)),
                  pl.BlockSpec((256,64),lambda p,t,*_:(0,0))],
        out_specs=[pl.BlockSpec((1,TQ,64),lambda p,t,*_:(p,t,0)),pl.BlockSpec((1,TQ,128),lambda p,t,*_:(p,t,0))],
        scratch_shapes=[pltpu.VMEM((256,N),BF),pltpu.VMEM((N,128),BF)]),
      compiler_params=pltpu.CompilerParams(dimension_semantics=("arbitrary","arbitrary"),vmem_limit_bytes=56<<20))(ext,q,k,v,rel)

def bwd_kernel(ext_ref,q_ref,k_ref,v_ref,oa_ref,do_ref,rel_ref,relb_ref,dq_ref,dkt_ref,dvt_ref,drel_ref,kt,vt,ka,*,TQ):
    p=pl.program_id(0); t=pl.program_id(1)
    H=2048
    @pl.when((p==0)&(t==0))
    def _():
        oh=onehots()
        kt[64:,:H]=oh; kt[64:,H:]=oh
        vt[64:,:]=jnp.where(lax.broadcasted_iota(jnp.int32,(64,N),0)<2,-1.0,0.0).astype(BF)
        j=lax.broadcasted_iota(jnp.int32,(N,128),0); f=lax.broadcasted_iota(jnp.int32,(N,128),1)
        ka[:,64:192]=jnp.where(f<64,((63-f)==j%64).astype(F32),((f-64)==j//64).astype(F32)).astype(BF)
        ka[:,192:]=jnp.zeros((N,64),BF)
        drel_ref[...]=jnp.zeros_like(drel_ref)
    @pl.when(t==0)
    def _():
        kf=k_ref[0]
        kt[:64,:]=kf.astype(F32).T.astype(BF)
        ka[:,:64]=(kf.astype(F32)*0.125).astype(BF)
        vt[:64,:]=v_ref[0].astype(F32).T.astype(BF)
        dkt_ref[...]=jnp.zeros_like(dkt_ref); dvt_ref[...]=jnp.zeros_like(dvt_ref)
    q=q_ref[0]; do=do_ref[0]; oa=oa_ref[0]
    L=oa[:,64:65]
    D=jnp.sum(do.astype(F32)*oa[:,:64],1,keepdims=True)
    g=TQ//64; row0=t*g
    R,C=rel_feats(q,rel_ref,ext_ref[p,0],ext_ref[p,1],row0,g)
    A,B=make_lhs(q,R-L,C)
    dh,dl=split(D)
    lane=lax.broadcasted_iota(jnp.int32,(TQ,64),1)
    dd=jnp.where(lane==0,dh.astype(F32),jnp.where(lane==1,dl.astype(F32),0.0)).astype(BF)
    doa=jnp.concatenate([do,dd],1)
    qt=(q.astype(F32)*0.125).T.astype(BF)
    dot_=do.astype(F32).T.astype(BF)
    dqa=None
    for h,lhs in ((0,A),(1,B)):
        sl=slice(h*H,(h+1)*H)
        P=jnp.exp(dot(lhs,kt[:,sl]))
        dS=(P*dot(doa,vt[:,sl])).astype(BF)
        dvt_ref[0,:,sl]+=dot(dot_,P.astype(BF))
        dkt_ref[0,:,sl]+=dot(qt,dS)
        x=dot(dS,ka[sl,:])
        dqa=x if dqa is None else dqa+x
    z64=jnp.zeros((64,64),F32)
    outs=[]
    for i in range(g):
        rs=slice(i*64,(i+1)*64)
        dC=jnp.concatenate([dqa[rs,64:128],z64],1)
        dR=jnp.concatenate([dqa[rs,128:192],z64],1)
        fR=pltpu.roll(dR,(63-(row0+i))%128,1)
        fC=pltpu.roll(dC,0,1,stride=1,stride_axis=0)
        outs.append(jnp.concatenate([fR,fC],1))
    f=jnp.concatenate(outs,0)
    fh,fl=split(f)
    relv=relb_ref[...]
    dq=dqa[:,:64]+dot(fh,relv)+dot(fl,relv)
    dq_ref[0]=dq.astype(BF)
    q8=q.astype(F32).T.astype(BF)
    drel_ref[...]+=dot(q8,fh)+dot(q8,fl)

def attn_bwd(ext, q, k, v, oa, do, rel, TQ=256):
    Pn=q.shape[0]
    full=lambda w:pl.BlockSpec((1,N,w),lambda p,t,*_:(p,0,0))
    tile=lambda w:pl.BlockSpec((1,TQ,w),lambda p,t,*_:(p,t,0))
    return pl.pallas_call(functools.partial(bwd_kernel,TQ=TQ),
      out_shape=(jax.ShapeDtypeStruct((Pn,N,64),BF),jax.ShapeDtypeStruct((Pn,64,N),F32),jax.ShapeDtypeStruct((Pn,64,N),F32),jax.ShapeDtypeStruct((64,256),F32)),
      grid_spec=pltpu.PrefetchScalarGridSpec(num_scalar_prefetch=1,grid=(Pn,N//TQ),
        in_specs=[tile(64),full(64),full(64),tile(128),tile(64),pl.BlockSpec((256,64),lambda p,t,*_:(0,0)),pl.BlockSpec((256,64),lambda p,t,*_:(0,0))],
        out_specs=[tile(64),pl.BlockSpec((1,64,N),lambda p,t,*_:(p,0,0)),pl.BlockSpec((1,64,N),lambda p,t,*_:(p,0,0)),pl.BlockSpec((64,256),lambda p,t,*_:(0,0))],
        scratch_shapes=[pltpu.VMEM((256,N),BF),pltpu.VMEM((128,N),BF),pltpu.VMEM((N,256),BF)]),
      compiler_params=pltpu.CompilerParams(dimension_semantics=("arbitrary","arbitrary"),vmem_limit_bytes=56<<20))(ext,q,k,v,oa,do,rel,jnp.concatenate([rel[:128],rel[128:255][::-1],rel[255:]],0))


def shards(
    tokens,
    norm1_gain,
    norm1_shift,
    qkv_weight,
    qv_bias,
    rel_rows,
    rel_cols,
    out_weight,
    out_bias,
    norm2_gain,
    norm2_shift,
    fc1_weight,
    fc1_bias,
    fc2_weight,
    fc2_bias,
    window_place,
    image_extent,
    box_mask,
    out_grad,
):
    wide_count = lax.axis_size("wide")
    wide_index = lax.axis_index("wide")
    capacity = max(2, 88 // wide_count)
    length = wide_count * capacity
    slot_count = tokens.shape[0]
    image_count = image_extent.shape[0]
    row_count = slot_count * WTOK
    occupied, window_of, live_items, position = send_plan(
        window_place, slot_count, image_count, wide_index, capacity, wide_count
    )
    gather_index, pair_image = receive_plan(
        window_place, slot_count, image_count, wide_index, capacity
    )
    present = patch_mask(occupied, window_of).reshape(row_count, 1)
    qkv_heads = head_major(qkv_weight)
    inputs = tokens.reshape(row_count, D).astype(jnp.float32)
    normed1, scaled1, spread1 = norm_rows(
        inputs, norm1_gain.astype(jnp.float32), norm1_shift.astype(jnp.float32)
    )
    normed1 = normed1.astype(jnp.bfloat16)
    bias_rows = jnp.stack([qv_bias[0], jnp.zeros((D,), qv_bias.dtype), qv_bias[1]]).astype(
        jnp.float32
    )
    bias_full = head_major(bias_rows.reshape(1, 3 * D))[0]
    qkv_values = (product(normed1, qkv_heads) + bias_full).astype(jnp.bfloat16)
    qkv_packed = pack_items(to_items(qkv_values, slot_count, 3), position, length, wide_count)
    arrived_qkv = lax.all_to_all(qkv_packed, "wide", split_axis=0, concat_axis=0, tiled=True)
    pair_grid = grid_from_items(arrived_qkv.reshape(length, -1)[gather_index], PAIR_DEV, 3)
    queries, key_rows, values = (pair_grid[:, :, 0], pair_grid[:, :, 1], pair_grid[:, :, 2])
    blank = jnp.zeros((1, HDIM), BF)
    rel = jnp.concatenate([rel_rows[::-1], blank, rel_cols[::-1], blank], 0)
    extents = image_extent[pair_image]
    attended_pairs, saved = attn_fwd(extents, queries, key_rows, values, rel)
    out_packed = pack_items(
        items_from_grid(attended_pairs, PAIR_DEV), gather_index, length, wide_count
    )
    returned = lax.all_to_all(out_packed, "wide", split_axis=0, concat_axis=0, tiled=True)
    attended = from_items(unpack_items(returned, position, live_items, length), slot_count, 1)
    branch = product(attended, out_weight) + out_bias.astype(jnp.float32)
    middle = inputs + branch
    normed2, scaled2, spread2 = norm_rows(
        middle, norm2_gain.astype(jnp.float32), norm2_shift.astype(jnp.float32)
    )
    normed2 = normed2.astype(jnp.bfloat16)
    before = product(normed2, fc1_weight) + fc1_bias.astype(jnp.float32)
    activated, gelu_pull = jax.vjp(partial(jax.nn.gelu, approximate=False), before)
    act_low = activated.astype(jnp.bfloat16)
    result = middle + product(act_low, fc2_weight) + fc2_bias.astype(jnp.float32)
    tokens_out = (result * present).astype(jnp.bfloat16).reshape(tokens.shape)
    row_weight = box_mask.reshape(row_count, 1).astype(jnp.float32) * present
    grad_result = out_grad.reshape(row_count, D).astype(jnp.float32) * row_weight
    grad_low = grad_result.astype(jnp.bfloat16)
    fc2_weight_grad = product_left(act_low, grad_low)
    fc2_bias_grad = jnp.sum(grad_result, axis=0)
    grad_before = gelu_pull(product_right(grad_low, fc2_weight))[0].astype(jnp.bfloat16)
    fc1_weight_grad = product_left(normed2, grad_before)
    fc1_bias_grad = jnp.sum(grad_before.astype(jnp.float32), axis=0)
    grad_normed2 = product_right(grad_before, fc1_weight)
    norm2_gain_grad = jnp.sum(grad_normed2 * scaled2, axis=0)
    norm2_shift_grad = jnp.sum(grad_normed2, axis=0)
    grad_middle = grad_result + norm_back(
        grad_normed2, scaled2, spread2, norm2_gain.astype(jnp.float32)
    )
    grad_branch = grad_middle.astype(jnp.bfloat16)
    out_weight_grad = product_left(attended, grad_branch)
    out_bias_grad = jnp.sum(grad_branch.astype(jnp.float32), axis=0)
    grad_attended = product_right(grad_branch, out_weight).astype(jnp.bfloat16)
    grad_packed = pack_items(to_items(grad_attended, slot_count, 1), position, length, wide_count)
    grad_arrived = lax.all_to_all(grad_packed, "wide", split_axis=0, concat_axis=0, tiled=True)
    grad_pairs = grid_from_items(grad_arrived.reshape(length, -1)[gather_index], PAIR_DEV, 1)[
        :, :, 0
    ]
    grad_query, grad_keys, grad_values, rel_grads = attn_bwd(
        extents, queries, key_rows, values, saved, grad_pairs, rel
    )
    rel_grads = rel_grads.T
    rel_rows_grad = rel_grads[:127][::-1]
    rel_cols_grad = rel_grads[128:255]
    grad_keys = grad_keys.transpose(0, 2, 1)
    grad_values = grad_values.transpose(0, 2, 1)
    stacked = jnp.concatenate(
        [grad_query, grad_keys.astype(jnp.bfloat16), grad_values.astype(jnp.bfloat16)], axis=2
    )
    back_packed = pack_items(items_from_grid(stacked, PAIR_DEV), gather_index, length, wide_count)
    grad_returned = lax.all_to_all(back_packed, "wide", split_axis=0, concat_axis=0, tiled=True)
    grad_qkv = from_items(unpack_items(grad_returned, position, live_items, length), slot_count, 3)
    qkv_weight_grad = part_major(product_left(normed1, grad_qkv))
    bias_sums = jnp.sum(grad_qkv.astype(jnp.float32), axis=0).reshape(HEADS, 3, HDIM)
    qv_bias_grad = jnp.stack([bias_sums[:, 0].reshape(D), bias_sums[:, 2].reshape(D)])
    grad_normed1 = product_right(grad_qkv, qkv_heads)
    norm1_gain_grad = jnp.sum(grad_normed1 * scaled1, axis=0)
    norm1_shift_grad = jnp.sum(grad_normed1, axis=0)
    grad_inputs = (
        grad_middle + norm_back(grad_normed1, scaled1, spread1, norm1_gain.astype(jnp.float32))
    ) * present
    tokens_grad = grad_inputs.reshape(tokens.shape)
    large_grads = (qkv_weight_grad, out_weight_grad, fc1_weight_grad, fc2_weight_grad)
    shares = (
        lax.psum_scatter(large_grads[0], "wide", scatter_dimension=0, tiled=True),
        lax.psum_scatter(large_grads[1], "wide", scatter_dimension=0, tiled=True),
        lax.psum_scatter(large_grads[2], "wide", scatter_dimension=0, tiled=True),
        lax.psum_scatter(large_grads[3], "wide", scatter_dimension=0, tiled=True),
    )
    shares = lax.psum((shares[0], shares[1], shares[2], shares[3]), "dp")
    small_grads = lax.psum(
        (
            norm1_gain_grad,
            norm1_shift_grad,
            qv_bias_grad,
            rel_rows_grad,
            rel_cols_grad,
            out_bias_grad,
            norm2_gain_grad,
            norm2_shift_grad,
            fc1_bias_grad,
            fc2_bias_grad,
        ),
        ("dp", "wide"),
    )
    return (
        tokens_out,
        tokens_grad,
        small_grads[0],
        small_grads[1],
        shares[0],
        small_grads[2],
        small_grads[3],
        small_grads[4],
        shares[1],
        small_grads[5],
        small_grads[6],
        small_grads[7],
        shares[2],
        small_grads[8],
        shares[3],
        small_grads[9],
    )


def solution(mesh):
    placed = (
        P(("dp", "wide"), None, None),
        P(),
        P(),
        P(),
        P(),
        P(),
        P(),
        P(),
        P(),
        P(),
        P(),
        P(),
        P(),
        P(),
        P(),
        P("dp"),
        P("dp", None),
        P(("dp", "wide"), None),
        P(("dp", "wide"), None, None),
    )
    return jax.shard_map(
        shards,
        mesh=mesh,
        in_specs=placed,
        out_specs=(
            P(("dp", "wide"), None, None),
            P(("dp", "wide"), None, None),
            P(),
            P(),
            P("wide", None),
            P(),
            P(),
            P(),
            P("wide", None),
            P(),
            P(),
            P(),
            P("wide", None),
            P(),
            P("wide", None),
            P(),
        ),
        check_vma=False,
    )
```

```python
from functools import partial

import jax
import jax.numpy as jnp
from jax import lax
from jax.experimental import pallas as pl
from jax.experimental.pallas import tpu as pltpu
from jax.sharding import PartitionSpec as P

F32 = jnp.float32
BF = jnp.bfloat16
D = 768
HEADS = 12
HDIM = 64
GRID = 64
N = GRID * GRID
WIN = 14
WGRID = 5
WINS = 25
WTOK = 196
HALF = 98
GROUPS = 4
CHUNKS = 3
EPS = 1e-06
NEG = -1e9
VMEM = 60 << 20


def dot(a, b):
    return jnp.dot(a, b, preferred_element_type=F32)


def dot_t(a, b):
    return lax.dot_general(a, b, (((1,), (1,)), ((), ())), preferred_element_type=F32)


def t_dot(a, b):
    return lax.dot_general(a, b, (((0,), (0,)), ((), ())), preferred_element_type=F32)


def shape(dims, kind):
    return jax.ShapeDtypeStruct(dims, kind)


def params(*semantics):
    return pltpu.CompilerParams(
        dimension_semantics=semantics or ("arbitrary",), vmem_limit_bytes=VMEM
    )


class Plan:
    def __init__(self, wide, images):
        self.wide, self.images = wide, images
        self.corner = WINS % wide == 1 and wide < WINS
        self.full = WINS // wide if self.corner else -(-WINS // wide)
        self.slots = self.full + int(self.corner)
        used = self.full * HALF + 32 * int(self.corner)
        self.rows = max(-(-used // 16) * 16, self.start(self.full - 1) + 112)
        self.corner_at = self.full * HALF

    def start(self, m):
        return m * HALF // 16 * 16

    def turn(self, places, slot_count, image):
        return (places[0] // slot_count + WINS * image) % self.wide

    def residue(self, places, slot_count, me, image):
        return (me + 2 * WINS * self.wide - self.turn(places, slot_count, image)) % self.wide

    def slot(self, places, slot_count, me, image, m):
        w = jnp.minimum(self.residue(places, slot_count, me, image) + self.wide * m, WINS - 1)
        return places[image * WINS + w] % slot_count


def norm_rows(values):
    centre = values - jnp.mean(values, axis=-1, keepdims=True)
    spread = lax.rsqrt(jnp.mean(centre * centre, axis=-1, keepdims=True) + EPS)
    return (centre * spread, spread)


def norm_back(weighted, scaled, spread):
    return spread * (
        weighted
        - jnp.mean(weighted, axis=-1, keepdims=True)
        - scaled * jnp.mean(weighted * scaled, axis=-1, keepdims=True)
    )


def place_rows(buffer, values, plan, m):
    if m < plan.full:
        for half in range(2):
            buffer[half, m * HALF : (m + 1) * HALF, :] = values[half * HALF : (half + 1) * HALF, :]
    else:
        for row in range(8):
            at = plan.corner_at + (row % 4) * 8
            buffer[row // 4, at : at + 8, :] = values[row * WIN : row * WIN + 8, :]


def cell_mask(plan, w, live):
    cell = lax.broadcasted_iota(jnp.int32, (WTOK, 1), 0)
    row_end = jnp.where(w // WGRID == WGRID - 1, 8, WIN)
    col_end = jnp.where(w % WGRID == WGRID - 1, 8, WIN)
    return ((cell // WIN < row_end) & (cell % WIN < col_end) & live).astype(F32)


def enter_kernel(plan, places, me, *refs):
    count = plan.slots
    tokens, grads = (refs[:count], refs[count : 2 * count])
    box, weight, bias, gain, shift = refs[2 * count : 2 * count + 5]
    x_out, g_out, n_out = refs[2 * count + 5 : 2 * count + 8]
    sends = refs[2 * count + 8 : 2 * count + 11]
    xbuf, gbuf, turned = refs[2 * count + 11 :]
    image = pl.program_id(0)
    slot_count = box.shape[0]

    @pl.when(image == 0)
    def _():
        xbuf[...] = jnp.zeros_like(xbuf)
        gbuf[...] = jnp.zeros_like(gbuf)
        turned[...] = box[...].astype(F32).T

    residue = plan.residue(places, slot_count, me[0], image)
    for m in range(count):
        place_rows(xbuf, tokens[m][0].astype(F32), plan, m)
        w = residue + plan.wide * m
        slot = plan.slot(places, slot_count, me[0], image, m)
        lane = lax.broadcasted_iota(jnp.int32, (WTOK, slot_count), 1)
        inside = jnp.sum(jnp.where(lane == slot, turned[...], 0.0), axis=1, keepdims=True)
        inside = inside * cell_mask(plan, w, w < WINS)
        place_rows(gbuf, grads[m][0].astype(F32) * inside, plan, m)
    x = xbuf[...].reshape(2 * plan.rows, D)
    x_out[0] = x.astype(BF)
    g_out[0] = gbuf[...].reshape(2 * plan.rows, D).astype(BF)
    scaled, _ = norm_rows(x)
    normed = (scaled * gain[...] + shift[...]).astype(BF)
    n_out[0] = normed
    for part in range(3):
        made = dot(normed, weight[:, part * D : (part + 1) * D]) + bias[:, part * D : (part + 1) * D]
        top, low = (made[: plan.rows].astype(BF), made[plan.rows :].astype(BF))
        for h in range(CHUNKS):
            for g in range(GROUPS):
                at = (h * GROUPS + g) * HDIM
                sends[h][g, :, part * 128 : (part + 1) * 128] = jnp.concatenate(
                    [top[:, at : at + HDIM], low[:, at : at + HDIM]], axis=1
                )


def enter(plan, places, me, tokens, out_grad, box_mask, weight, bias, gain, shift):
    slot_count = tokens.shape[0]

    def window(m):
        return pl.BlockSpec(
            (1, WTOK, D), lambda i, p, a: (plan.slot(p, slot_count, a[0], i, m), 0, 0)
        )

    windows = [window(m) for m in range(plan.slots)]
    fixed = [
        pl.BlockSpec(x.shape, lambda i, p, a: (0, 0)) for x in (box_mask, weight, bias, gain, shift)
    ]
    rows = pl.BlockSpec((1, 2 * plan.rows, D), lambda i, p, a: (i, 0, 0))
    send = pl.BlockSpec((GROUPS, plan.rows, 384), lambda i, p, a: (i, 0, 0))
    working = shape((plan.images, 2 * plan.rows, D), BF)
    return pl.pallas_call(
        partial(enter_kernel, plan),
        out_shape=[working] * 3 + [shape((plan.wide, plan.rows, 384), BF)] * CHUNKS,
        grid_spec=pltpu.PrefetchScalarGridSpec(
            num_scalar_prefetch=2,
            grid=(plan.images,),
            in_specs=windows + windows + fixed,
            out_specs=[rows] * 3 + [send] * CHUNKS,
            scratch_shapes=[
                pltpu.VMEM((2, plan.rows, D), F32),
                pltpu.VMEM((2, plan.rows, D), F32),
                pltpu.VMEM((WTOK, slot_count), F32),
            ],
        ),
        compiler_params=params(),
        cost_estimate=pl.CostEstimate(flops=6 * 10**9, bytes_accessed=20 << 20, transcendentals=0),
        name="enter",
    )(
        places,
        me,
        *([tokens] * plan.slots),
        *([out_grad] * plan.slots),
        box_mask,
        weight,
        bias,
        gain,
        shift,
    )


def leave_kernel(plan, places, me, values, out):
    slot = pl.program_id(0)
    slot_count = pl.num_programs(0)
    out[...] = jnp.zeros_like(out)
    for image in range(plan.images):
        residue = plan.residue(places, slot_count, me[0], image)
        for m in range(plan.slots):
            w = residue + plan.wide * m
            held = places[image * WINS + jnp.minimum(w, WINS - 1)]
            hit = (w < WINS) & (held == me[0] * slot_count + slot)

            @pl.when(hit)
            def _(image=image, m=m, w=w):
                if m < plan.full:
                    halves = []
                    for half in range(2):
                        at = half * plan.rows + m * HALF
                        halves.append(values[image, at : at + HALF, :].astype(F32))
                    keep = cell_mask(plan, w, w < WINS)
                    out[0, :HALF, :] = (halves[0] * keep[:HALF]).astype(out.dtype)
                    out[0, HALF:, :] = (halves[1] * keep[HALF:]).astype(out.dtype)
                else:
                    for row in range(8):
                        at = (row // 4) * plan.rows + plan.corner_at + (row % 4) * 8
                        piece = values[image, at : at + 8, :]
                        out[0, row * WIN : row * WIN + 8, :] = piece.astype(out.dtype)


def leave(plan, places, me, values, slot_count):
    return pl.pallas_call(
        partial(leave_kernel, plan),
        out_shape=shape((slot_count, WTOK, D), values.dtype),
        grid_spec=pltpu.PrefetchScalarGridSpec(
            num_scalar_prefetch=2,
            grid=(slot_count,),
            in_specs=[pl.BlockSpec(values.shape, lambda j, p, a: (0, 0, 0))],
            out_specs=pl.BlockSpec((1, WTOK, D), lambda j, p, a: (j, 0, 0)),
        ),
        compiler_params=params(),
        cost_estimate=pl.CostEstimate(flops=1 << 20, bytes_accessed=12 << 20, transcendentals=0),
        name="leave",
    )(places, me, values)


def spread_matrix(plan, band, flip):
    dims = (560, 448) if flip else (448, 560)
    cell = lax.broadcasted_iota(jnp.int32, dims, 1 if flip else 0)
    item = lax.broadcasted_iota(jnp.int32, dims, 0 if flip else 1)
    row, col = (cell // GRID, cell % GRID)
    block = col // WIN
    shift = jnp.zeros(dims, jnp.int32)
    for c in range(WGRID):
        m = (band * WGRID + c) // plan.wide
        if m < plan.full:
            shift = jnp.where(block == c, m * HALF - plan.start(m), shift)
        else:
            shift = jnp.where(block == c, -10000, shift)
    return (item == block * 112 + shift + row * WIN + col % WIN).astype(F32).astype(BF)


def corner_matrix(plan, flip):
    dims = (48, 256) if flip else (256, 48)
    cell = lax.broadcasted_iota(jnp.int32, dims, 1 if flip else 0)
    item = lax.broadcasted_iota(jnp.int32, dims, 0 if flip else 1)
    row, col = (cell // GRID, cell % GRID)
    at = plan.corner_at - plan.start(plan.full)
    hit = (col >= 4 * WIN) & (item == at + row * 8 + col - 4 * WIN)
    return hit.astype(F32).astype(BF)


def gather_grid(plan, turn, arrived, band):
    pieces = []
    for c in range(WGRID):
        w = band * WGRID + c
        m = w // plan.wide
        if m < plan.full:
            source = (w % plan.wide + turn) % plan.wide
            at = plan.start(m)
        else:
            source, at = (0, 0)
        pieces.append(arrived[source, at : at + 112, :])
    found = dot(spread_matrix(plan, band, False), jnp.concatenate(pieces, axis=0))
    return found


def grid_rows(plan, turn, arrived, parts, store):
    for band in range(WGRID):
        found = gather_grid(plan, turn, arrived, band)
        last = band == WGRID - 1
        if last and plan.corner:
            source = ((WINS - 1) % plan.wide + turn) % plan.wide
            at = plan.start(plan.full)
            extra = dot(corner_matrix(plan, False), arrived[source, at : at + 48, :])
        for part in range(parts):
            top = found[:, part * 128 : part * 128 + HDIM]
            low = found[:, part * 128 + HDIM : (part + 1) * 128]
            if last:
                low = low[:GRID]
            whole = jnp.concatenate([top, low], axis=0)
            if last and plan.corner:
                more = jnp.concatenate(
                    [
                        extra[:, part * 128 : part * 128 + HDIM],
                        extra[:, part * 128 + HDIM : (part + 1) * 128],
                    ],
                    axis=0,
                )
                whole = whole + more
            store(part, band * WIN * GRID, whole)


def scatter_grid(plan, turn, out, parts, load, lane=0):
    span = slice(lane, lane + parts * 128)
    out[:, :, span] = jnp.zeros((plan.wide, plan.rows, parts * 128), BF)
    for band in range(WGRID):
        last = band == WGRID - 1
        base = band * WIN * GRID
        lanes = []
        for part in range(parts):
            top = load(part, base, 448)
            if last:
                low = load(part, base + 448, GRID)
                low = jnp.concatenate([low, jnp.zeros((448 - GRID, HDIM), BF)], axis=0)
            else:
                low = load(part, base + 448, 448)
            lanes += [top, low]
        made = dot(spread_matrix(plan, band, True), jnp.concatenate(lanes, axis=1)).astype(BF)
        for c in range(WGRID):
            w = band * WGRID + c
            m = w // plan.wide
            if m < plan.full:
                dest = (w % plan.wide + turn) % plan.wide
                at = plan.start(m)
                out[dest, at : at + 112, span] += made[c * 112 : (c + 1) * 112]
        if last and plan.corner:
            lanes = []
            for part in range(parts):
                lanes += [load(part, base, 256), load(part, base + 256, 256)]
            made = dot(corner_matrix(plan, True), jnp.concatenate(lanes, axis=1)).astype(BF)
            dest = ((WINS - 1) % plan.wide + turn) % plan.wide
            at = plan.start(plan.full)
            out[dest, at : at + 48, span] += made


def split(x):
    high = x.astype(BF)
    return (high, (x - high.astype(F32)).astype(BF))


def key_marks():
    feature = lax.broadcasted_iota(jnp.int32, (192, N // 2), 0)
    key = lax.broadcasted_iota(jnp.int32, (192, N // 2), 1)
    col = (feature % GRID) == (key % GRID)
    row = ((feature - 128) % 32) == (key // GRID)
    return jnp.where(feature < 128, col.astype(F32), row.astype(F32)).astype(BF)


def rel_terms(q, table, extent_rows, extent_cols, first_row, count):
    both = dot_t(q, table)
    lane = lax.broadcasted_iota(jnp.int32, (GRID, 128), 1)
    row_mask = jnp.where(lane < extent_rows, 0.0, NEG)
    col_mask = jnp.where(lane < extent_cols, 0.0, NEG)
    rows, cols = ([], [])
    for i in range(count):
        part = both[i * GRID : (i + 1) * GRID]
        rows.append(pltpu.roll(part[:, :128], (first_row + i + 65) % 128, 1) + row_mask)
        cols.append(pltpu.roll(part[:, 128:], 65, 1, stride=1, stride_axis=0) + col_mask)
    return (jnp.concatenate(rows, 0)[:, :GRID], jnp.concatenate(cols, 0)[:, :GRID])


def query_marks(q, rows, cols):
    rh, rl = split(rows)
    ch, cl = split(cols)
    scaled = (q.astype(F32) * 0.125).astype(BF)
    return [
        jnp.concatenate([scaled, ch, cl, rh[:, i : i + 32], rl[:, i : i + 32]], 1) for i in (0, 32)
    ]


def forward_kernel(plan, tile, slot_count, places, me, extent, arrived, table, *refs):
    earlier, (send, kept, saved, kt, va, held) = (refs[:-6], refs[-6:])
    step = pl.program_id(0)
    image = me[0] // GROUPS
    turn = plan.turn(places, slot_count, image)

    @pl.when(step == 0)
    def _():
        marks = key_marks()
        kt[HDIM:, : N // 2] = marks
        kt[HDIM:, N // 2 :] = marks
        va[:, HDIM:] = (lax.broadcasted_iota(jnp.int32, (N, HDIM), 1) == 0).astype(F32).astype(BF)

        def store(part, first, values):
            kept[part, first : first + values.shape[0], :] = values.astype(BF)

        grid_rows(plan, turn, arrived, 3, store)
        kt[:HDIM, :] = kept[1].astype(F32).T.astype(BF)
        va[:, :HDIM] = kept[2]

    here = pl.ds(pl.multiple_of(step * tile, tile), tile)
    q = kept[0, here, :]
    count = tile // GRID
    rows, cols = rel_terms(q, table[...], extent[image, 0], extent[image, 1], step * count, count)
    marks = query_marks(q, rows, cols)
    scores = [dot(marks[i], kt[:, i * (N // 2) : (i + 1) * (N // 2)]) for i in range(2)]
    top = jnp.maximum(*[jnp.max(s, axis=1, keepdims=True) for s in scores])
    total = None
    for i in range(2):
        weights = jnp.exp(scores[i] - top).astype(BF)
        x = dot(weights, va[i * (N // 2) : (i + 1) * (N // 2), :])
        total = x if total is None else total + x
    mass = total[:, HDIM : HDIM + 1]
    out = total * (1.0 / mass)
    lane = lax.broadcasted_iota(jnp.int32, (tile, 128), 1)
    saved[...] = jnp.where(lane < HDIM, out, top + jnp.log(mass))
    held[here, :] = out[:, :HDIM].astype(BF)

    @pl.when(step == pl.num_programs(0) - 1)
    def _():
        load = lambda part, first, size: held[first : first + size, :]
        scatter_grid(plan, turn, send, 1, load, 128 * len(earlier))
        for i, block in enumerate(earlier):
            send[:, :, 128 * i : 128 * (i + 1)] = block[...]


def attention_forward(plan, slot_count, places, me, extent, arrived, table, *earlier, tile=256):
    lanes = 128 * (1 + len(earlier))
    whole = lambda *dims: pl.BlockSpec(dims, lambda t, *_: (0,) * len(dims))
    return pl.pallas_call(
        partial(forward_kernel, plan, tile, slot_count),
        out_shape=(
            shape((plan.wide, plan.rows, lanes), BF),
            shape((3, N, HDIM), BF),
            shape((N, 128), F32),
        ),
        grid_spec=pltpu.PrefetchScalarGridSpec(
            num_scalar_prefetch=3,
            grid=(N // tile,),
            in_specs=[whole(*x.shape) for x in (arrived, table, *earlier)],
            out_specs=[
                whole(plan.wide, plan.rows, lanes),
                whole(3, N, HDIM),
                pl.BlockSpec((tile, 128), lambda t, *_: (t, 0)),
            ],
            scratch_shapes=[
                pltpu.VMEM((256, N), BF),
                pltpu.VMEM((N, 128), BF),
                pltpu.VMEM((N, HDIM), BF),
            ],
        ),
        compiler_params=params(),
        cost_estimate=pl.CostEstimate(
            flops=4 * N * N * 256, bytes_accessed=12 << 20, transcendentals=N * N
        ),
        name="attention_forward",
    )(places, me, extent, arrived, table, *earlier)


def backward_kernel(
    plan, tile, slot_count, places, me, extent,
    arrived, kept, saved, table, table_back,
    send, rel_grad,
    kt, vt, ka, dout, dq, dk, dv,
):
    step = pl.program_id(0)
    image = me[0] // GROUPS
    turn = plan.turn(places, slot_count, image)
    side = N // 2

    @pl.when(step == 0)
    def _():
        marks = key_marks()
        kt[HDIM:, :side] = marks
        kt[HDIM:, side:] = marks
        minus = lax.broadcasted_iota(jnp.int32, (HDIM, N), 0) < 2
        vt[HDIM:, :] = jnp.where(minus, -1.0, 0.0).astype(BF)
        key = lax.broadcasted_iota(jnp.int32, (N, 128), 0)
        mark = lax.broadcasted_iota(jnp.int32, (N, 128), 1)
        col = (GRID - 1 - mark) == key % GRID
        row = (mark - GRID) == key // GRID
        ka[:, HDIM:192] = jnp.where(mark < GRID, col.astype(F32), row.astype(F32)).astype(BF)
        ka[:, 192:] = jnp.zeros((N, HDIM), BF)
        rel_grad[...] = jnp.zeros_like(rel_grad)
        dk[...] = jnp.zeros_like(dk)
        dv[...] = jnp.zeros_like(dv)
        keys = kept[1].astype(F32)
        kt[:HDIM, :] = keys.T.astype(BF)
        ka[:, :HDIM] = (keys * 0.125).astype(BF)
        vt[:HDIM, :] = kept[2].astype(F32).T.astype(BF)

        def store(part, first, values):
            dout[first : first + values.shape[0], :] = values.astype(BF)

        grid_rows(plan, turn, arrived, 1, store)

    here = pl.ds(pl.multiple_of(step * tile, tile), tile)
    q = kept[0, here, :]
    do = dout[here, :]
    old = saved[...]
    count = tile // GRID
    inner = jnp.sum(do.astype(F32) * old[:, :HDIM], axis=1, keepdims=True)
    rows, cols = rel_terms(q, table[...], extent[image, 0], extent[image, 1], step * count, count)
    marks = query_marks(q, rows - old[:, HDIM : HDIM + 1], cols)
    high, low = split(inner)
    lane = lax.broadcasted_iota(jnp.int32, (tile, HDIM), 1)
    less = jnp.where(lane == 0, high.astype(F32), jnp.where(lane == 1, low.astype(F32), 0.0))
    do_less = jnp.concatenate([do, less.astype(BF)], 1)
    q_turned = (q.astype(F32) * 0.125).T.astype(BF)
    do_turned = do.astype(F32).T.astype(BF)
    back = None
    for i in range(2):
        part = slice(i * side, (i + 1) * side)
        weights = jnp.exp(dot(marks[i], kt[:, part]))
        dscore = (weights * dot(do_less, vt[:, part])).astype(BF)
        dv[:, part] += dot(do_turned, weights.astype(BF))
        dk[:, part] += dot(q_turned, dscore)
        x = dot(dscore, ka[part, :])
        back = x if back is None else back + x
    blank = jnp.zeros((GRID, HDIM), F32)
    offsets = []
    for i in range(count):
        own = slice(i * GRID, (i + 1) * GRID)
        row_part = jnp.concatenate([back[own, 128:192], blank], 1)
        col_part = jnp.concatenate([back[own, HDIM:128], blank], 1)
        row_part = pltpu.roll(row_part, (2 * GRID - 1 + GRID - step * count - i) % 128, 1)
        col_part = pltpu.roll(col_part, 0, 1, stride=1, stride_axis=0)
        offsets.append(jnp.concatenate([row_part, col_part], 1))
    high, low = split(jnp.concatenate(offsets, 0))
    rel = table_back[...]
    both = dot(jnp.concatenate([high, low], 1), jnp.concatenate([rel, rel], 0))
    dq[here, :] = (back[:, :HDIM] + both).astype(BF)
    q_whole = q.astype(F32).T.astype(BF)
    rel_grad[...] += dot(q_whole, high) + dot(q_whole, low)

    @pl.when(step == pl.num_programs(0) - 1)
    def _():
        def load(part, first, size):
            if part == 0:
                return dq[first : first + size, :]
            return turned[part - 1][first : first + size, :]

        turned = (dk[...].T.astype(BF), dv[...].T.astype(BF))
        scatter_grid(plan, turn, send, 3, load)


def attention_backward(
    plan, slot_count, places, me, extent, arrived, lane, kept, saved, table, table_back, tile=512
):
    whole = lambda *dims: pl.BlockSpec(dims, lambda t, *_: (0,) * len(dims))
    return pl.pallas_call(
        partial(backward_kernel, plan, tile, slot_count),
        out_shape=(shape((plan.wide, plan.rows, 384), BF), shape((HDIM, 256), F32)),
        grid_spec=pltpu.PrefetchScalarGridSpec(
            num_scalar_prefetch=3,
            grid=(N // tile,),
            in_specs=[
                pl.BlockSpec((plan.wide, plan.rows, 128), lambda t, *_: (0, 0, lane)),
                whole(3, N, HDIM),
                pl.BlockSpec((tile, 128), lambda t, *_: (t, 0)),
                whole(*table.shape),
                whole(*table_back.shape),
            ],
            out_specs=[whole(plan.wide, plan.rows, 384), whole(HDIM, 256)],
            scratch_shapes=[
                pltpu.VMEM((256, N), BF),
                pltpu.VMEM((128, N), BF),
                pltpu.VMEM((N, 256), BF),
                pltpu.VMEM((N, HDIM), BF),
                pltpu.VMEM((N, HDIM), BF),
                pltpu.VMEM((HDIM, N), F32),
                pltpu.VMEM((HDIM, N), F32),
            ],
        ),
        compiler_params=params(),
        cost_estimate=pl.CostEstimate(
            flops=10 * N * N * 256, bytes_accessed=12 << 20, transcendentals=N * N
        ),
        name="attention_backward",
    )(places, me, extent, arrived, kept, saved, table, table_back)


def join_kernel(plan, first, last, x, weight, bias, attended, middle):
    returned = (first.at[:, :, :128], first.at[:, :, 128:], last)
    for half in range(2):
        lanes = [
            returned[h][g, :, half * HDIM : (half + 1) * HDIM]
            for h in range(CHUNKS)
            for g in range(GROUPS)
        ]
        attended[0, half * plan.rows : (half + 1) * plan.rows, :] = jnp.concatenate(lanes, axis=1)
    middle[0] = x[0].astype(F32) + (dot(attended[0], weight[...]) + bias[...])


def join(plan, first, last, x, weight, bias):
    rows = pl.BlockSpec((1, 2 * plan.rows, D), lambda i: (i, 0, 0))
    block = pl.BlockSpec((GROUPS, plan.rows, 128), lambda i: (i, 0, 0))
    working = (plan.images, 2 * plan.rows, D)
    return pl.pallas_call(
        partial(join_kernel, plan),
        out_shape=(shape(working, BF), shape(working, F32)),
        grid=(plan.images,),
        in_specs=[
            pl.BlockSpec((GROUPS, plan.rows, 256), lambda i: (i, 0, 0)), block, rows]
        + [pl.BlockSpec((D, D), lambda i: (0, 0)), pl.BlockSpec((1, D), lambda i: (0, 0))],
        out_specs=[rows, rows],
        compiler_params=params(),
        cost_estimate=pl.CostEstimate(flops=2 * 10**9, bytes_accessed=10 << 20, transcendentals=0),
        name="join",
    )(first, last, x, weight, bias)


def part_kernel(plan, grad, weight, first, last):
    sends = (first, last.at[:, :, :128], last.at[:, :, 128:])
    made = dot_t(grad[0], weight[...])
    top, low = (made[: plan.rows].astype(BF), made[plan.rows :].astype(BF))
    for h in range(CHUNKS):
        for g in range(GROUPS):
            at = (h * GROUPS + g) * HDIM
            made = jnp.concatenate([top[:, at : at + HDIM], low[:, at : at + HDIM]], axis=1)
            sends[h][g, :, :] = made


def part(plan, grad, weight):
    return pl.pallas_call(
        partial(part_kernel, plan),
        out_shape=[shape((plan.wide, plan.rows, lanes), BF) for lanes in (128, 256)],
        grid=(plan.images,),
        in_specs=[
            pl.BlockSpec((1, 2 * plan.rows, D), lambda i: (i, 0, 0)),
            pl.BlockSpec((D, D), lambda i: (0, 0)),
        ],
        out_specs=[
            pl.BlockSpec((GROUPS, plan.rows, lanes), lambda i: (i, 0, 0)) for lanes in (128, 256)
        ],
        compiler_params=params(),
        cost_estimate=pl.CostEstimate(flops=2 * 10**9, bytes_accessed=6 << 20, transcendentals=0),
        name="part",
    )(grad, weight)


def collect_kernel(plan, chunk, arrived, normed, wq, wk, wv, *refs):
    before, (total, weight_grad, bias_grad, held) = (refs[:-4], refs[-4:])
    image = pl.program_id(0)

    @pl.when(image == 0)
    def _():
        held[...] = jnp.zeros_like(held)
        bias_grad[...] = jnp.zeros_like(bias_grad)

    n = normed[0]
    whole = None
    for p, weight in enumerate((wq, wk, wv)):
        halves = []
        for half in range(2):
            at = p * 128 + half * HDIM
            lanes = [arrived[g, :, at : at + HDIM] for g in range(GROUPS)]
            halves.append(jnp.concatenate(lanes, axis=1))
        y = jnp.concatenate(halves, axis=0)
        x = dot_t(y, weight[...])
        whole = x if whole is None else whole + x
        span = slice(p * 256, (p + 1) * 256)
        held[:, span] += t_dot(n, y)
        bias_grad[0:1, span] += jnp.sum(y.astype(F32), axis=0, keepdims=True)
    total[0] = whole + before[0][0] if before else whole

    @pl.when(image == pl.num_programs(0) - 1)
    def _():
        weight_grad[...] = held[...].astype(weight_grad.dtype)


def collect(plan, chunk, arrived, normed, weight, before):
    rows = pl.BlockSpec((1, 2 * plan.rows, D), lambda i: (i, 0, 0))
    columns = [pl.BlockSpec((D, 256), lambda i, p=p: (0, p * 3 + chunk)) for p in range(3)]
    extra = () if before is None else (before,)
    return pl.pallas_call(
        partial(collect_kernel, plan, chunk),
        out_shape=(
            shape((plan.images, 2 * plan.rows, D), F32),
            shape((D, D), BF),
            shape((8, D), F32),
        ),
        grid=(plan.images,),
        in_specs=[pl.BlockSpec((GROUPS, plan.rows, 384), lambda i: (i, 0, 0)), rows]
        + columns
        + [rows] * len(extra),
        out_specs=[
            rows,
            pl.BlockSpec((D, D), lambda i: (0, 0)),
            pl.BlockSpec((8, D), lambda i: (0, 0)),
        ],
        scratch_shapes=[pltpu.VMEM((D, D), F32)],
        compiler_params=params(),
        cost_estimate=pl.CostEstimate(flops=8 * 10**9, bytes_accessed=20 << 20, transcendentals=0),
        name="collect",
    )(arrived, normed, weight, weight, weight, *extra)


def tie(value, *others):
    return lax.optimization_barrier((value, *others))[0]


def exchange(blocks, axis="wide"):
    return lax.all_to_all(blocks, axis, split_axis=0, concat_axis=0, tiled=True)


def share_rows(grad, wide, groups):
    piece = grad.shape[0] // wide // groups
    return grad.astype(BF).reshape(wide, groups, piece, D).transpose(1, 0, 2, 3)


def over_groups(low):
    groups = low.shape[0]
    own = lax.axis_index("dp")
    take = lambda i: lax.dynamic_index_in_dim(low, i, 0, keepdims=False)
    got = [take(own)]
    for d in range(1, groups):
        pairs = [(i, (i + d) % groups) for i in range(groups)]
        got.append(lax.ppermute(take((own + d) % groups), "dp", pairs))
    return got


def add_groups(got):
    total = got[0].astype(F32)
    for x in got[1:]:
        total = total + x.astype(F32)
    return total


def add_wide(got):
    return jnp.sum(got.astype(F32), axis=0)


def shards(
    tokens, norm1_gain, norm1_shift, qkv_weight, qv_bias, rel_rows, rel_cols, out_weight, out_bias,
    norm2_gain, norm2_shift, fc1_weight, fc1_bias, fc2_weight, fc2_bias,
    window_place, image_extent, box_mask, out_grad,
):
    wide, groups = (lax.axis_size("wide"), lax.axis_size("dp"))
    me = lax.axis_index("wide").astype(jnp.int32).reshape(1)
    plan = Plan(wide, image_extent.shape[0])
    slots = tokens.shape[0]
    wide_f = lambda v: v.astype(F32).reshape(1, -1)
    bias = jnp.concatenate([qv_bias[0], jnp.zeros((D,), BF), qv_bias[1]])
    blank = jnp.zeros((1, HDIM), BF)
    table = jnp.concatenate([rel_rows[::-1], blank, rel_cols[::-1], blank], 0)
    table_back = jnp.concatenate([rel_rows[::-1], blank, rel_cols, blank], 0)
    x, grad_out, normed1, *sends = enter(
        plan, window_place, me, tokens, out_grad, box_mask,
        qkv_weight, wide_f(bias), wide_f(norm1_gain), wide_f(norm1_shift),
    )
    forward = []
    arrived = exchange(sends[0])
    for h in range(CHUNKS):
        if h + 1 < CHUNKS:
            following, arrived = lax.optimization_barrier((sends[h + 1], arrived))
            following = exchange(tie(following, forward[h - 1][2]) if h else following)
        else:
            first, arrived = lax.optimization_barrier((forward[1][0], arrived))
            first = exchange(first)
        earlier = (forward[0][0],) if h == 1 else ()
        forward.append(
            attention_forward(
                plan, slots, window_place, me, image_extent, arrived, table, *earlier
            )
        )
        arrived = following
    last, first = lax.optimization_barrier((forward[2][0], first))
    attended, middle = join(plan, first, exchange(last), x, out_weight, wide_f(out_bias))
    rows = plan.images * 2 * plan.rows
    attended = attended.reshape(rows, D)
    middle = middle.reshape(rows, D)
    grad_low = grad_out.reshape(rows, D)
    grad_result = grad_low.astype(F32)
    scaled2, spread2 = norm_rows(middle)
    normed2 = (scaled2 * wide_f(norm2_gain) + wide_f(norm2_shift)).astype(BF)
    before = dot(normed2, fc1_weight) + wide_f(fc1_bias)
    activated, gelu_pull = jax.vjp(partial(jax.nn.gelu, approximate=False), before)
    act_low = activated.astype(BF)
    grad_before = gelu_pull(dot_t(grad_low, fc2_weight))[0].astype(BF)
    grad_normed2 = dot_t(grad_before, fc1_weight)
    grad_middle = grad_result + norm_back(grad_normed2 * wide_f(norm2_gain), scaled2, spread2)
    grad_branch = grad_middle.astype(BF)
    grad_sends = part(plan, grad_branch.reshape(plan.images, 2 * plan.rows, D), out_weight)

    grad_arrived = exchange(grad_sends[0])
    normed2, act_low, attended, _ = lax.optimization_barrier(
        (normed2, act_low, attended, grad_sends[0])
    )
    fc1_low = t_dot(normed2, grad_before).astype(BF).reshape(D, groups, D).transpose(1, 0, 2)
    shares = jnp.concatenate(
        [
            fc1_low.reshape(groups, wide, D // wide, D),
            share_rows(t_dot(act_low, grad_low), wide, groups),
            share_rows(t_dot(attended, grad_branch), wide, groups),
        ],
        axis=2,
    )
    total = lambda v: jnp.sum(v.astype(F32), axis=0)
    early = jnp.concatenate(
        [
            total(grad_branch),
            total(grad_normed2 * scaled2),
            total(grad_normed2),
            total(grad_before),
            total(grad_result),
        ]
    )
    shares, grad_arrived, early = lax.optimization_barrier((shares, grad_arrived, early))
    shares = over_groups(shares)
    following = exchange(tie(grad_sends[1], grad_arrived))

    rel_total = None
    grad_qkv = []
    for h in range(CHUNKS):
        if h == 2:
            *shares, _ = lax.optimization_barrier((*shares, send))
            shares = add_groups(shares)
            grad_arrived, shares = lax.optimization_barrier((grad_arrived, shares))
        send, rel_grad = attention_backward(
            plan, slots, window_place, me, image_extent, grad_arrived, max(h - 1, 0),
            forward[h][1], forward[h][2], table, table_back,
        )
        if h == 0:
            send, grad_arrived = lax.optimization_barrier((send, following))
        rel_total = rel_grad if h == 0 else rel_total + rel_grad
        if h > 0:
            send = tie(send, grad_qkv[-1])
        grad_qkv.append(exchange(send))
        if h + 1 < CHUNKS and h > 0:
            grad_arrived = tie(grad_arrived, grad_qkv[-2])
    shares = lax.psum_scatter(shares, "wide", scatter_dimension=0, tiled=True)[0]
    result, act_low, _ = lax.optimization_barrier((middle, act_low, send))
    shares = tie(shares, send)
    shares = lax.all_gather(shares, "dp", axis=0, tiled=False)
    result = result + dot(act_low, fc2_weight) + wide_f(fc2_bias)
    tokens_out = leave(plan, window_place, me, result.reshape(plan.images, 2 * plan.rows, D), slots)
    tokens_out = tokens_out.astype(BF)
    grad_normed1 = None
    weight_grads, bias_grads = ([], [])
    for h in range(CHUNKS):
        arrived = grad_qkv[h]
        if h == 2:
            arrived, shares, tokens_out, _ = lax.optimization_barrier(
                (arrived, shares, tokens_out, grad_normed1)
            )
        grad_normed1, weight_grad, bias_grad = collect(
            plan, h, arrived, normed1, qkv_weight, grad_normed1
        )
        weight_grads.append(
            add_groups(over_groups(share_rows(weight_grad, wide, groups))).astype(BF)
        )
        bias_grads.append(bias_grad[0].reshape(3, 256))
    weight_grads = exchange(jnp.concatenate(weight_grads, axis=2))
    bias_grad = jnp.stack(bias_grads, axis=1).reshape(3, D)
    grad_normed1 = grad_normed1.reshape(rows, D)
    scaled1, spread1 = norm_rows(x.reshape(rows, D).astype(F32))
    grad_inputs = grad_middle + norm_back(grad_normed1 * wide_f(norm1_gain), scaled1, spread1)
    sums = jnp.concatenate(
        [
            early,
            total(grad_normed1 * scaled1),
            total(grad_normed1),
            bias_grad[0],
            bias_grad[2],
            rel_total.reshape(-1),
            jnp.zeros((512,), F32),
        ]
    ).reshape(-1, D)
    sums = jnp.sum(lax.all_gather(sums, "wide", axis=0, tiled=False), axis=0)
    share = D // wide
    piece = share // groups
    last = jnp.concatenate([add_wide(weight_grads).reshape(-1, D), sums], axis=0)
    last = lax.all_gather(last, "dp", axis=0, tiled=False)
    qkv_weight_grad = last[:, : 3 * piece].reshape(share, CHUNKS, 3, 256)
    qkv_weight_grad = qkv_weight_grad.transpose(0, 2, 1, 3).reshape(share, 3 * D)
    sums = jnp.sum(last[:, 3 * piece :], axis=0).reshape(-1)
    tokens_grad = leave(
        plan, window_place, me, grad_inputs.reshape(plan.images, 2 * plan.rows, D), slots
    )
    late = sums[8 * D : 12 * D]
    rel_total = sums[12 * D : 12 * D + HDIM * 256].reshape(HDIM, 256).T
    small = sums[: 8 * D]
    return (
        tokens_out,
        tokens_grad,
        late[:D],
        late[D : 2 * D],
        qkv_weight_grad,
        late[2 * D :].reshape(2, D),
        rel_total[:127][::-1],
        rel_total[128:255],
        shares[:, 2 * share :].reshape(share, D),
        small[:D],
        small[D : 2 * D],
        small[2 * D : 3 * D],
        shares[:, :share].transpose(1, 0, 2).reshape(share, 4 * D),
        small[3 * D : 7 * D],
        shares[:, share : 2 * share].reshape(4 * share, D),
        small[7 * D :],
    )


def solution(mesh):
    tokens = P(("dp", "wide"), None, None)
    placed = (tokens,) + (P(),) * 14 + (P("dp"), P("dp", None), P(("dp", "wide"), None), tokens)
    shared = P("wide", None)
    return jax.shard_map(
        shards,
        mesh=mesh,
        in_specs=placed,
        out_specs=(
            tokens, tokens, P(), P(), shared, P(), P(), P(), shared, P(), P(), P(), shared, P(),
            shared, P(),
        ),
        check_vma=False,
    )
```

```python
from functools import partial

import jax
import jax.numpy as jnp
from jax import lax
from jax.experimental import pallas as pl
from jax.experimental.pallas import tpu as pltpu
from jax.sharding import PartitionSpec as P

F32 = jnp.float32
BF = jnp.bfloat16
D = 768
HEADS = 12
HDIM = 64
GRID = 64
N = GRID * GRID
WIN = 14
WGRID = 5
WINS = 25
WTOK = 196
HALF = 98
GROUPS = 4
CHUNKS = 3
EPS = 1e-06
NEG = -1e9
VMEM = 60 << 20
KEYS = 512
TILE = 1024


def dot(a, b):
    return jnp.dot(a, b, preferred_element_type=F32)


def dot_t(a, b):
    return lax.dot_general(a, b, (((1,), (1,)), ((), ())), preferred_element_type=F32)


def t_dot(a, b):
    return lax.dot_general(a, b, (((0,), (0,)), ((), ())), preferred_element_type=F32)


def shape(dims, kind):
    return jax.ShapeDtypeStruct(dims, kind)


def params(*semantics):
    return pltpu.CompilerParams(
        dimension_semantics=semantics or ("arbitrary",), vmem_limit_bytes=VMEM
    )


class Plan:
    def __init__(self, wide, images):
        self.wide, self.images = wide, images
        self.corner = WINS % wide == 1 and wide < WINS
        self.full = WINS // wide if self.corner else -(-WINS // wide)
        self.slots = self.full + int(self.corner)
        used = self.full * HALF + 32 * int(self.corner)
        self.rows = max(-(-used // 16) * 16, self.start(self.full - 1) + 112)
        self.corner_at = self.full * HALF

    def start(self, m):
        return m * HALF // 16 * 16

    def turn(self, places, slot_count, image):
        return (places[0] // slot_count + WINS * image) % self.wide

    def residue(self, places, slot_count, me, image):
        return (me + 2 * WINS * self.wide - self.turn(places, slot_count, image)) % self.wide

    def slot(self, places, slot_count, me, image, m):
        w = jnp.minimum(self.residue(places, slot_count, me, image) + self.wide * m, WINS - 1)
        return places[image * WINS + w] % slot_count


def norm_rows(values):
    centre = values - jnp.mean(values, axis=-1, keepdims=True)
    spread = lax.rsqrt(jnp.mean(centre * centre, axis=-1, keepdims=True) + EPS)
    return (centre * spread, spread)


def norm_back(weighted, scaled, spread):
    return spread * (
        weighted
        - jnp.mean(weighted, axis=-1, keepdims=True)
        - scaled * jnp.mean(weighted * scaled, axis=-1, keepdims=True)
    )


def place_rows(buffer, values, plan, m):
    if m < plan.full:
        for half in range(2):
            buffer[half, m * HALF : (m + 1) * HALF, :] = values[half * HALF : (half + 1) * HALF, :]
    else:
        for row in range(8):
            at = plan.corner_at + (row % 4) * 8
            buffer[row // 4, at : at + 8, :] = values[row * WIN : row * WIN + 8, :]


def cell_mask(plan, w, live):
    cell = lax.broadcasted_iota(jnp.int32, (WTOK, 1), 0)
    row_end = jnp.where(w // WGRID == WGRID - 1, 8, WIN)
    col_end = jnp.where(w % WGRID == WGRID - 1, 8, WIN)
    return ((cell // WIN < row_end) & (cell % WIN < col_end) & live).astype(F32)


def send_lanes(plan, normed, weights, bias, send):
    for part in range(3):
        at = part * 256
        made = dot(normed, weights[part][...]) + bias[part][...]
        top, low = (made[: plan.rows].astype(BF), made[plan.rows :].astype(BF))
        for g in range(GROUPS):
            own = slice(g * HDIM, (g + 1) * HDIM)
            both = jnp.concatenate([top[:, own], low[:, own]], axis=1)
            send[g, :, part * 128 : (part + 1) * 128] = both


def enter_kernel(plan, places, me, *refs):
    count = plan.slots
    tokens = refs[:count]
    weights, bias = (refs[count : count + 3], refs[count + 3 : count + 6])
    gain, shift, x_out, n_out, send, xbuf = refs[count + 6 :]

    @pl.when(pl.program_id(0) == 0)
    def _():
        xbuf[...] = jnp.zeros_like(xbuf)

    for m in range(count):
        place_rows(xbuf, tokens[m][0].astype(F32), plan, m)
    x = xbuf[...].reshape(2 * plan.rows, D)
    x_out[0] = x.astype(BF)
    scaled, _ = norm_rows(x)
    normed = (scaled * gain[...] + shift[...]).astype(BF)
    n_out[0] = normed
    send_lanes(plan, normed, weights, bias, send)


def follow_kernel(plan, places, me, *refs):
    count = plan.slots
    grads = refs[:count]
    box, normed = refs[count : count + 2]
    weights, bias = (refs[count + 2 : count + 8], refs[count + 8 : count + 14])
    g_out, *sends = refs[count + 14 : count + 17]
    gbuf, turned = refs[count + 17 :]
    image = pl.program_id(0)
    slot_count = box.shape[0]

    @pl.when(image == 0)
    def _():
        gbuf[...] = jnp.zeros_like(gbuf)
        turned[...] = box[...].astype(F32).T

    for h in range(2):
        own = slice(h * 3, h * 3 + 3)
        send_lanes(plan, normed[0], weights[own], bias[own], sends[h])
    residue = plan.residue(places, slot_count, me[0], image)
    for m in range(count):
        w = residue + plan.wide * m
        slot = plan.slot(places, slot_count, me[0], image, m)
        lane = lax.broadcasted_iota(jnp.int32, (WTOK, slot_count), 1)
        inside = jnp.sum(jnp.where(lane == slot, turned[...], 0.0), axis=1, keepdims=True)
        inside = inside * cell_mask(plan, w, w < WINS)
        place_rows(gbuf, grads[m][0].astype(F32) * inside, plan, m)
    g_out[0] = gbuf[...].reshape(2 * plan.rows, D).astype(BF)


def entry_specs(plan, slot_count):
    windows = [
        pl.BlockSpec((1, WTOK, D), lambda i, p, a, m=m: (plan.slot(p, slot_count, a[0], i, m), 0, 0))
        for m in range(plan.slots)
    ]
    column = lambda rows, h: [
        pl.BlockSpec((rows, 256), lambda i, p, a, b=part * CHUNKS + h: (0, b)) for part in range(3)
    ]
    rows = pl.BlockSpec((1, 2 * plan.rows, D), lambda i, p, a: (i, 0, 0))
    send = pl.BlockSpec((GROUPS, plan.rows, 384), lambda i, p, a: (i, 0, 0))
    return (windows, column, rows, send)


def enter(plan, places, me, tokens, weight, bias, gain, shift):
    windows, column, rows, send = entry_specs(plan, tokens.shape[0])
    fixed = pl.BlockSpec((1, D), lambda i, p, a: (0, 0))
    working = shape((plan.images, 2 * plan.rows, D), BF)
    return pl.pallas_call(
        partial(enter_kernel, plan),
        out_shape=[working, working, shape((plan.wide, plan.rows, 384), BF)],
        grid_spec=pltpu.PrefetchScalarGridSpec(
            num_scalar_prefetch=2,
            grid=(plan.images,),
            in_specs=windows + column(D, 0) + column(1, 0) + [fixed, fixed],
            out_specs=[rows, rows, send],
            scratch_shapes=[pltpu.VMEM((2, plan.rows, D), F32)],
        ),
        compiler_params=params(),
        cost_estimate=pl.CostEstimate(
            flops=2 * 10**9, bytes_accessed=10 << 20, transcendentals=0
        ),
        name="enter",
    )(places, me, *([tokens] * plan.slots), *([weight] * 3), *([bias] * 3), gain, shift)


def follow(plan, places, me, out_grad, box_mask, normed, weight, bias):
    slot_count = out_grad.shape[0]
    windows, column, rows, send = entry_specs(plan, slot_count)
    fixed = pl.BlockSpec(box_mask.shape, lambda i, p, a: (0, 0))
    block = shape((plan.wide, plan.rows, 384), BF)
    return pl.pallas_call(
        partial(follow_kernel, plan),
        out_shape=[shape((plan.images, 2 * plan.rows, D), BF), block, block],
        grid_spec=pltpu.PrefetchScalarGridSpec(
            num_scalar_prefetch=2,
            grid=(plan.images,),
            in_specs=windows
            + [fixed, rows]
            + column(D, 1)
            + column(D, 2)
            + column(1, 1)
            + column(1, 2),
            out_specs=[rows, send, send],
            scratch_shapes=[
                pltpu.VMEM((2, plan.rows, D), F32),
                pltpu.VMEM((WTOK, slot_count), F32),
            ],
        ),
        compiler_params=params(),
        cost_estimate=pl.CostEstimate(
            flops=4 * 10**9, bytes_accessed=16 << 20, transcendentals=0
        ),
        name="follow",
    )(places, me, *([out_grad] * plan.slots), box_mask, normed, *([weight] * 6), *([bias] * 6))


def leave_kernel(plan, places, me, values, out, held):
    slot = pl.program_id(0)
    slot_count = pl.num_programs(0)
    held[...] = jnp.zeros_like(held)
    for image in range(plan.images):
        residue = plan.residue(places, slot_count, me[0], image)
        for m in range(plan.slots):
            w = residue + plan.wide * m
            place = places[image * WINS + jnp.minimum(w, WINS - 1)]
            hit = (w < WINS) & (place == me[0] * slot_count + slot)

            @pl.when(hit)
            def _(image=image, m=m, w=w):
                if m < plan.full:
                    keep = cell_mask(plan, w, w < WINS)
                    for half in range(2):
                        at = half * plan.rows + m * HALF
                        part = slice(half * HALF, (half + 1) * HALF)
                        held[part, :] = values[image, at : at + HALF, :] * keep[part]
                else:
                    for row in range(8):
                        at = (row // 4) * plan.rows + plan.corner_at + (row % 4) * 8
                        held[row * WIN : row * WIN + 8, :] = values[image, at : at + 8, :]

    out[0] = held[...].astype(out.dtype)


def leave(plan, places, me, values, slot_count, kind):
    return pl.pallas_call(
        partial(leave_kernel, plan),
        out_shape=shape((slot_count, WTOK, D), kind),
        grid_spec=pltpu.PrefetchScalarGridSpec(
            num_scalar_prefetch=2,
            grid=(slot_count,),
            in_specs=[
                pl.BlockSpec(values.shape, lambda j, p, a: (0, 0, 0), pipeline_mode=pl.Buffered(1))
            ],
            out_specs=pl.BlockSpec((1, WTOK, D), lambda j, p, a: (j, 0, 0)),
            scratch_shapes=[pltpu.VMEM((WTOK, D), F32)],
        ),
        compiler_params=params(),
        cost_estimate=pl.CostEstimate(flops=1 << 20, bytes_accessed=12 << 20, transcendentals=0),
        name="leave",
    )(places, me, values)


def spread_matrix(plan, band, flip):
    dims = (560, 448) if flip else (448, 560)
    cell = lax.broadcasted_iota(jnp.int32, dims, 1 if flip else 0)
    item = lax.broadcasted_iota(jnp.int32, dims, 0 if flip else 1)
    row, col = (cell // GRID, cell % GRID)
    block = col // WIN
    shift = jnp.zeros(dims, jnp.int32)
    for c in range(WGRID):
        m = (band * WGRID + c) // plan.wide
        if m < plan.full:
            shift = jnp.where(block == c, m * HALF - plan.start(m), shift)
        else:
            shift = jnp.where(block == c, -10000, shift)
    return (item == block * 112 + shift + row * WIN + col % WIN).astype(F32).astype(BF)


def corner_matrix(plan, flip):
    dims = (48, 256) if flip else (256, 48)
    cell = lax.broadcasted_iota(jnp.int32, dims, 1 if flip else 0)
    item = lax.broadcasted_iota(jnp.int32, dims, 0 if flip else 1)
    row, col = (cell // GRID, cell % GRID)
    at = plan.corner_at - plan.start(plan.full)
    hit = (col >= 4 * WIN) & (item == at + row * 8 + col - 4 * WIN)
    return hit.astype(F32).astype(BF)


def gather_grid(plan, turn, arrived, band):
    pieces = []
    for c in range(WGRID):
        w = band * WGRID + c
        m = w // plan.wide
        if m < plan.full:
            source = (w % plan.wide + turn) % plan.wide
            at = plan.start(m)
        else:
            source, at = (0, 0)
        pieces.append(arrived[source, at : at + 112, :])
    found = dot(spread_matrix(plan, band, False), jnp.concatenate(pieces, axis=0))
    return found


def grid_rows(plan, turn, arrived, parts, store):
    for band in range(WGRID):
        found = gather_grid(plan, turn, arrived, band)
        last = band == WGRID - 1
        if last and plan.corner:
            source = ((WINS - 1) % plan.wide + turn) % plan.wide
            at = plan.start(plan.full)
            extra = dot(corner_matrix(plan, False), arrived[source, at : at + 48, :])
        for part in range(parts):
            top = found[:, part * 128 : part * 128 + HDIM]
            low = found[:, part * 128 + HDIM : (part + 1) * 128]
            if last:
                low = low[:GRID]
            whole = jnp.concatenate([top, low], axis=0)
            if last and plan.corner:
                more = jnp.concatenate(
                    [
                        extra[:, part * 128 : part * 128 + HDIM],
                        extra[:, part * 128 + HDIM : (part + 1) * 128],
                    ],
                    axis=0,
                )
                whole = whole + more
            store(part, band * WIN * GRID, whole)


def scatter_grid(plan, turn, out, parts, load, lane=0):
    span = slice(lane, lane + parts * 128)
    out[:, :, span] = jnp.zeros((plan.wide, plan.rows, parts * 128), BF)
    for band in range(WGRID):
        last = band == WGRID - 1
        base = band * WIN * GRID
        lanes = []
        for part in range(parts):
            top = load(part, base, 448)
            if last:
                low = load(part, base + 448, GRID)
                low = jnp.concatenate([low, jnp.zeros((448 - GRID, HDIM), BF)], axis=0)
            else:
                low = load(part, base + 448, 448)
            lanes += [top, low]
        made = dot(spread_matrix(plan, band, True), jnp.concatenate(lanes, axis=1)).astype(BF)
        for c in range(WGRID):
            w = band * WGRID + c
            m = w // plan.wide
            if m < plan.full:
                dest = (w % plan.wide + turn) % plan.wide
                at = plan.start(m)
                out[dest, at : at + 112, span] += made[c * 112 : (c + 1) * 112]
        if last and plan.corner:
            lanes = []
            for part in range(parts):
                lanes += [load(part, base, 256), load(part, base + 256, 256)]
            made = dot(corner_matrix(plan, True), jnp.concatenate(lanes, axis=1)).astype(BF)
            dest = ((WINS - 1) % plan.wide + turn) % plan.wide
            at = plan.start(plan.full)
            out[dest, at : at + 48, span] += made


def split(x):
    high = x.astype(BF)
    return (high, (x - high.astype(F32)).astype(BF))


def key_marks():
    feature = lax.broadcasted_iota(jnp.int32, (192, N // 2), 0)
    key = lax.broadcasted_iota(jnp.int32, (192, N // 2), 1)
    col = (feature % GRID) == (key % GRID)
    row = ((feature - 128) % 32) == (key // GRID)
    return jnp.where(feature < 128, col.astype(F32), row.astype(F32)).astype(BF)


def rel_terms(q, table, extent_rows, extent_cols, first_row, count):
    both = dot_t(q, table)
    lane = lax.broadcasted_iota(jnp.int32, (GRID, 128), 1)
    row_mask = jnp.where(lane < extent_rows, 0.0, NEG)
    col_mask = jnp.where(lane < extent_cols, 0.0, NEG)
    rows, cols = ([], [])
    for i in range(count):
        part = both[i * GRID : (i + 1) * GRID]
        rows.append(pltpu.roll(part[:, :128], (first_row + i + 65) % 128, 1) + row_mask)
        cols.append(pltpu.roll(part[:, 128:], 65, 1, stride=1, stride_axis=0) + col_mask)
    return (jnp.concatenate(rows, 0)[:, :GRID], jnp.concatenate(cols, 0)[:, :GRID])


def query_marks(q, rows, cols):
    rh, rl = split(rows)
    ch, cl = split(cols)
    scaled = (q.astype(F32) * 0.125).astype(BF)
    return [
        jnp.concatenate([scaled, ch, cl, rh[:, i : i + 32], rl[:, i : i + 32]], 1) for i in (0, 32)
    ]


def forward_kernel(plan, tile, slot_count, places, me, extent, arrived, table, *refs):
    earlier, (send, kept, saved, kt, va, held) = (refs[:-6], refs[-6:])
    step = pl.program_id(0)
    image = me[0] // GROUPS
    turn = plan.turn(places, slot_count, image)

    @pl.when(step == 0)
    def _():
        marks = key_marks()
        kt[HDIM:, : N // 2] = marks
        kt[HDIM:, N // 2 :] = marks
        va[:, HDIM:] = (lax.broadcasted_iota(jnp.int32, (N, HDIM), 1) == 0).astype(F32).astype(BF)

        def store(part, first, values):
            kept[part, first : first + values.shape[0], :] = values.astype(BF)

        grid_rows(plan, turn, arrived, 3, store)
        kt[:HDIM, :] = kept[1].astype(F32).T.astype(BF)
        va[:, :HDIM] = kept[2]

    here = pl.ds(pl.multiple_of(step * tile, tile), tile)
    q = kept[0, here, :]
    count = tile // GRID
    rows, cols = rel_terms(q, table[...], extent[image, 0], extent[image, 1], step * count, count)
    marks = query_marks(q, rows, cols)
    side = N // 2
    score = lambda c: dot(marks[c * KEYS // side], kt[:, c * KEYS : (c + 1) * KEYS])
    total, top, now = (None, None, score(0))
    for c in range(N // KEYS):
        following = score(c + 1) if c + 1 < N // KEYS else None
        higher = jnp.max(now, axis=1, keepdims=True)
        if c:
            higher = jnp.maximum(top, higher)
        weights = jnp.exp(now - higher).astype(BF)
        x = dot(weights, va[c * KEYS : (c + 1) * KEYS, :])
        total = total * jnp.exp(top - higher) + x if c else x
        top, now = (higher, following)
    mass = total[:, HDIM : HDIM + 1]
    out = total * (1.0 / mass)
    lane = lax.broadcasted_iota(jnp.int32, (tile, 128), 1)
    saved[...] = jnp.where(lane < HDIM, out, top + jnp.log(mass))
    held[here, :] = out[:, :HDIM].astype(BF)

    @pl.when(step == pl.num_programs(0) - 1)
    def _():
        load = lambda part, first, size: held[first : first + size, :]
        scatter_grid(plan, turn, send, 1, load, 128 * len(earlier))
        for i, block in enumerate(earlier):
            send[:, :, 128 * i : 128 * (i + 1)] = block[...]


def attention_forward(plan, slot_count, places, me, extent, arrived, table, *earlier, tile=TILE):
    lanes = 128 * (1 + len(earlier))
    whole = lambda *dims: pl.BlockSpec(dims, lambda t, *_: (0,) * len(dims))
    return pl.pallas_call(
        partial(forward_kernel, plan, tile, slot_count),
        out_shape=(
            shape((plan.wide, plan.rows, lanes), BF),
            shape((3, N, HDIM), BF),
            shape((N, 128), F32),
        ),
        grid_spec=pltpu.PrefetchScalarGridSpec(
            num_scalar_prefetch=3,
            grid=(N // tile,),
            in_specs=[whole(*x.shape) for x in (arrived, table, *earlier)],
            out_specs=[
                whole(plan.wide, plan.rows, lanes),
                whole(3, N, HDIM),
                pl.BlockSpec((tile, 128), lambda t, *_: (t, 0)),
            ],
            scratch_shapes=[
                pltpu.VMEM((256, N), BF),
                pltpu.VMEM((N, 128), BF),
                pltpu.VMEM((N, HDIM), BF),
            ],
        ),
        compiler_params=params(),
        cost_estimate=pl.CostEstimate(
            flops=4 * N * N * 256, bytes_accessed=12 << 20, transcendentals=N * N
        ),
        name="attention_forward",
    )(places, me, extent, arrived, table, *earlier)


def backward_kernel(
    plan, tile, slot_count, places, me, extent,
    arrived, kept, saved, table, table_back,
    send, rel_grad,
    kt, vt, ka, dout, dq, dk, dv,
):
    step = pl.program_id(0)
    image = me[0] // GROUPS
    turn = plan.turn(places, slot_count, image)
    side = N // 2

    @pl.when(step == 0)
    def _():
        marks = key_marks()
        kt[HDIM:, :side] = marks
        kt[HDIM:, side:] = marks
        minus = lax.broadcasted_iota(jnp.int32, (HDIM, N), 0) < 2
        vt[HDIM:, :] = jnp.where(minus, -1.0, 0.0).astype(BF)
        key = lax.broadcasted_iota(jnp.int32, (N, 128), 0)
        mark = lax.broadcasted_iota(jnp.int32, (N, 128), 1)
        col = (GRID - 1 - mark) == key % GRID
        row = (mark - GRID) == key // GRID
        ka[:, HDIM:192] = jnp.where(mark < GRID, col.astype(F32), row.astype(F32)).astype(BF)
        ka[:, 192:] = jnp.zeros((N, HDIM), BF)
        rel_grad[...] = jnp.zeros_like(rel_grad)
        dk[...] = jnp.zeros_like(dk)
        dv[...] = jnp.zeros_like(dv)
        keys = kept[1].astype(F32)
        kt[:HDIM, :] = keys.T.astype(BF)
        ka[:, :HDIM] = (keys * 0.125).astype(BF)
        vt[:HDIM, :] = kept[2].astype(F32).T.astype(BF)

        def store(part, first, values):
            dout[first : first + values.shape[0], :] = values.astype(BF)

        grid_rows(plan, turn, arrived, 1, store)

    here = pl.ds(pl.multiple_of(step * tile, tile), tile)
    q = kept[0, here, :]
    do = dout[here, :]
    old = saved[...]
    count = tile // GRID
    inner = jnp.sum(do.astype(F32) * old[:, :HDIM], axis=1, keepdims=True)
    rows, cols = rel_terms(q, table[...], extent[image, 0], extent[image, 1], step * count, count)
    marks = query_marks(q, rows - old[:, HDIM : HDIM + 1], cols)
    high, low = split(inner)
    lane = lax.broadcasted_iota(jnp.int32, (tile, HDIM), 1)
    less = jnp.where(lane == 0, high.astype(F32), jnp.where(lane == 1, low.astype(F32), 0.0))
    do_less = jnp.concatenate([do, less.astype(BF)], 1)
    q_turned = (q.astype(F32) * 0.125).T.astype(BF)
    do_turned = do.astype(F32).T.astype(BF)
    def products(c):
        part = slice(c * KEYS, (c + 1) * KEYS)
        return (dot(marks[c * KEYS // side], kt[:, part]), dot(do_less, vt[:, part]))

    back, now = (None, products(0))
    for c in range(N // KEYS):
        part = slice(c * KEYS, (c + 1) * KEYS)
        following = products(c + 1) if c + 1 < N // KEYS else None
        weights = jnp.exp(now[0])
        dscore = (weights * now[1]).astype(BF)
        dv[:, part] += dot(do_turned, weights.astype(BF))
        dk[:, part] += dot(q_turned, dscore)
        x = dot(dscore, ka[part, :])
        back = x if back is None else back + x
        now = following
    blank = jnp.zeros((GRID, HDIM), F32)
    offsets = []
    for i in range(count):
        own = slice(i * GRID, (i + 1) * GRID)
        row_part = jnp.concatenate([back[own, 128:192], blank], 1)
        col_part = jnp.concatenate([back[own, HDIM:128], blank], 1)
        row_part = pltpu.roll(row_part, (2 * GRID - 1 + GRID - step * count - i) % 128, 1)
        col_part = pltpu.roll(col_part, 0, 1, stride=1, stride_axis=0)
        offsets.append(jnp.concatenate([row_part, col_part], 1))
    high, low = split(jnp.concatenate(offsets, 0))
    rel = table_back[...]
    both = dot(jnp.concatenate([high, low], 1), jnp.concatenate([rel, rel], 0))
    dq[here, :] = (back[:, :HDIM] + both).astype(BF)
    q_whole = q.astype(F32).T.astype(BF)
    rel_grad[...] += dot(q_whole, high) + dot(q_whole, low)

    @pl.when(step == pl.num_programs(0) - 1)
    def _():
        def load(part, first, size):
            if part == 0:
                return dq[first : first + size, :]
            return turned[part - 1][first : first + size, :]

        turned = (dk[...].T.astype(BF), dv[...].T.astype(BF))
        scatter_grid(plan, turn, send, 3, load)


def attention_backward(
    plan, slot_count, places, me, extent, arrived, lane, kept, saved, table, table_back, tile=TILE
):
    whole = lambda *dims: pl.BlockSpec(dims, lambda t, *_: (0,) * len(dims))
    return pl.pallas_call(
        partial(backward_kernel, plan, tile, slot_count),
        out_shape=(shape((plan.wide, plan.rows, 384), BF), shape((HDIM, 256), F32)),
        grid_spec=pltpu.PrefetchScalarGridSpec(
            num_scalar_prefetch=3,
            grid=(N // tile,),
            in_specs=[
                pl.BlockSpec((plan.wide, plan.rows, 128), lambda t, *_: (0, 0, lane)),
                whole(3, N, HDIM),
                pl.BlockSpec((tile, 128), lambda t, *_: (t, 0)),
                whole(*table.shape),
                whole(*table_back.shape),
            ],
            out_specs=[whole(plan.wide, plan.rows, 384), whole(HDIM, 256)],
            scratch_shapes=[
                pltpu.VMEM((256, N), BF),
                pltpu.VMEM((128, N), BF),
                pltpu.VMEM((N, 256), BF),
                pltpu.VMEM((N, HDIM), BF),
                pltpu.VMEM((N, HDIM), BF),
                pltpu.VMEM((HDIM, N), F32),
                pltpu.VMEM((HDIM, N), F32),
            ],
        ),
        compiler_params=params(),
        cost_estimate=pl.CostEstimate(
            flops=10 * N * N * 256, bytes_accessed=12 << 20, transcendentals=N * N
        ),
        name="attention_backward",
    )(places, me, extent, arrived, kept, saved, table, table_back)


def middle_kernel(
    plan, first, last, x, g, out_weight, fc1_weight, fc2_weight,
    out_bias, fc1_bias, fc2_bias, gain, shift,
    attended, normed, act, grad_before, result, grad_middle, grad_branch, send_first, send_last, sums,
    grads,
):
    step = pl.program_id(0)
    half = step % 2
    blocks = [first.at[:, :, :128], first.at[:, :, 128:], last]
    for side in range(2):

        @pl.when(half == side)
        def _(side=side):
            lanes = [
                blocks[h][k, :, side * HDIM : (side + 1) * HDIM]
                for h in range(CHUNKS)
                for k in range(GROUPS)
            ]
            attended[0] = jnp.concatenate(lanes, axis=1)

    @pl.when(step == 0)
    def _():
        sums[...] = jnp.zeros_like(sums)

    middle = x[0].astype(F32) + (dot(attended[0], out_weight[...]) + out_bias[...])
    scaled, spread = norm_rows(middle)
    n = (scaled * gain[...] + shift[...]).astype(BF)
    normed[0] = n
    grad = g[0]
    total, grad_normed = (None, None)
    add = lambda old, new: new if old is None else old + new
    for c in range(4):
        span = slice(c * D, (c + 1) * D)
        before = dot(n, fc1_weight[:, span]) + fc1_bias[:, span]
        share = 0.5 + 0.5 * lax.erf(before * (0.5**0.5))
        low = (before * share).astype(BF)
        act[0, :, span] = low
        slope = share + before * (jnp.exp(before * before * -0.5) * 0.3989422804014327)
        back = (dot_t(grad, fc2_weight[span, :]) * slope).astype(BF)
        grad_before[0, :, span] = back
        sums[:, (3 + c) * D : (4 + c) * D] += jnp.sum(back.astype(F32), axis=0, keepdims=True)
        total = add(total, dot(low, fc2_weight[span, :]))
        grad_normed = add(grad_normed, dot_t(back, fc1_weight[:, span]))
    result[0] = middle + total + fc2_bias[...]
    full = grad.astype(F32) + norm_back(grad_normed * gain[...], scaled, spread)
    grad_middle[0] = full
    branch = full.astype(BF)
    grad_branch[0] = branch
    for place, value in (
        (0, branch.astype(F32)), (1, grad_normed * scaled), (2, grad_normed), (7, grad.astype(F32))
    ):
        sums[:, place * D : (place + 1) * D] += jnp.sum(value, axis=0, keepdims=True)
    grads[...] = dot_t(branch, out_weight[...]).astype(BF)
    targets = [send_first, send_last.at[:, :, :128], send_last.at[:, :, 128:]]
    for side in range(2):

        @pl.when(half == side)
        def _(side=side):
            for h in range(CHUNKS):
                for k in range(GROUPS):
                    at = (h * GROUPS + k) * HDIM
                    made = grads[:, at : at + HDIM]
                    targets[h][k, :, side * HDIM : (side + 1) * HDIM] = made


def middle_part(plan, first, last, x, g, out_weight, fc1_weight, fc2_weight, *vectors):
    rows, hidden = (plan.rows, fc1_weight.shape[1])
    halves = 2 * plan.images
    x, g = (v.reshape(halves, rows, D) for v in (x, g))
    row = lambda width: pl.BlockSpec((1, rows, width), lambda i: (i, 0, 0))
    whole = lambda v: pl.BlockSpec(v.shape, lambda i: (0, 0), pipeline_mode=pl.Buffered(1))
    block = lambda lanes: pl.BlockSpec((GROUPS, rows, lanes), lambda i: (i // 2, 0, 0))
    made = lambda width, kind: shape((halves, rows, width), kind)
    fixed = (out_weight, fc1_weight, fc2_weight, *vectors)
    return pl.pallas_call(
        partial(middle_kernel, plan),
        out_shape=(
            made(D, BF), made(D, BF), made(hidden, BF), made(hidden, BF),
            made(D, F32), made(D, F32), made(D, BF),
            shape((plan.wide, rows, 128), BF), shape((plan.wide, rows, 256), BF),
            shape((1, 8 * D), F32),
        ),
        grid=(halves,),
        in_specs=[block(256), block(128), row(D), row(D)] + [whole(v) for v in fixed],
        out_specs=(
            row(D), row(D), row(hidden), row(hidden), row(D), row(D), row(D),
            block(128), block(256), pl.BlockSpec((1, 8 * D), lambda i: (0, 0)),
        ),
        scratch_shapes=[pltpu.VMEM((rows, D), BF)],
        compiler_params=params(),
        cost_estimate=pl.CostEstimate(
            flops=30 * 10**9, bytes_accessed=40 << 20, transcendentals=8 << 20
        ),
        name="middle",
    )(first, last, x, g, *fixed)


def shares_kernel(
    plan, groups, own, normed, grad_before, g, act, attended, branch,
    o0, o1, o2, o3, fc1, fc2, out, ready, turned_n, turned_g, sem,
):
    step, image = (pl.program_id(0), pl.program_id(1))
    finished = image == pl.num_programs(1) - 1
    outs = (o0, o1, o2, o3)
    d = (own[0] + step) % groups
    piece = D // plan.wide
    part = piece // groups
    width = D // groups

    @pl.when(image == 0)
    def _():
        fc1[...] = jnp.zeros_like(fc1)
        fc2[...] = jnp.zeros_like(fc2)

    @pl.when((image == 0) & (step == 0))
    def _():
        out[...] = jnp.zeros_like(out)

    @pl.when(step == 0)
    def _():
        turned_n[image] = normed[0].astype(F32).T.astype(BF)
        turned_g[image] = g[0].astype(F32).T.astype(BF)
        out[...] += t_dot(attended[0], branch[0])

    fc1[...] += dot(turned_n[image], grad_before[0])
    for k in range(groups):

        @pl.when(d == k)
        def _(k=k):
            fc2[...] += dot(turned_g[image, k * width : (k + 1) * width, :], act[0])

    for k in range(groups):

        @pl.when(finished & (step == k))
        def _(k=k):
            if k:
                pltpu.make_async_copy(ready, outs[k - 1], sem).wait()
            for b in range(plan.wide):
                ready[b, :piece, :] = fc1[b * piece : (b + 1) * piece, :].astype(BF)
                cols = slice(b * 4 * piece, (b + 1) * 4 * piece)
                for side in range(2):
                    lanes = slice(side * 4 * piece, (side + 1) * 4 * piece)
                    upper = fc2[side * piece : (side + 1) * piece, cols]
                    ready[b, piece : 2 * piece, lanes] = upper.astype(BF)
                at = pl.ds(pl.multiple_of(b * piece + d * part, 8), part)
                ready[b, 2 * piece :, :] = out[at, :].astype(BF)
            copy = pltpu.make_async_copy(ready, outs[k], sem)
            copy.start()
            if k == groups - 1:
                copy.wait()


def weight_shares(plan, groups, own, normed, grad_before, g, act, attended, branch):
    rows = 2 * plan.rows
    fold = lambda v: v.reshape(plan.images, rows, v.shape[-1])
    values = [fold(v) for v in (normed, grad_before, g, act, attended, branch)]
    once = pl.BlockSpec((1, rows, D), lambda s, i, o: (jnp.where(s == 0, i, plan.images - 1), 0, 0))
    wide = pl.BlockSpec((1, rows, values[3].shape[-1]), lambda s, i, o: (i, 0, 0))
    column = pl.BlockSpec((1, rows, D), lambda s, i, o: (i, 0, (o[0] + s) % groups))
    block = (plan.wide, 2 * D // plan.wide + D // plan.wide // groups, D)
    return pl.pallas_call(
        partial(shares_kernel, plan, groups),
        out_shape=[shape(block, BF)] * groups,
        grid_spec=pltpu.PrefetchScalarGridSpec(
            num_scalar_prefetch=1,
            grid=(groups, plan.images),
            in_specs=[once, column, once, wide, once, once],
            out_specs=[pl.BlockSpec(memory_space=pl.ANY)] * groups,
            scratch_shapes=[
                pltpu.VMEM((D, D), F32),
                pltpu.VMEM((D // groups, 4 * D), F32),
                pltpu.VMEM((D, D), F32),
                pltpu.VMEM(block, BF),
                pltpu.VMEM((plan.images, D, rows), BF),
                pltpu.VMEM((plan.images, D, rows), BF),
                pltpu.SemaphoreType.DMA,
            ],
        ),
        compiler_params=params("arbitrary", "arbitrary"),
        cost_estimate=pl.CostEstimate(
            flops=15 * 10**9, bytes_accessed=60 << 20, transcendentals=0
        ),
        name="weight_shares",
    )(own, *values)


def collect_kernel(plan, chunk, groups, kinds, own, arrived, normed, wq, wk, wv, *refs):
    before, middle_grad, x, gain = (None,) * 4
    if chunk > 0:
        before, refs = (refs[0], refs[1:])
    if chunk == CHUNKS - 1:
        (middle_grad, x, gain), refs = (refs[:3], refs[3:])
    total, bias_grad = refs[:2]
    outs, (held,) = (refs[2:-1], refs[-1:])
    image = pl.program_id(0)

    @pl.when(image == 0)
    def _():
        held[...] = jnp.zeros_like(held)
        bias_grad[...] = jnp.zeros_like(bias_grad)

    n = normed[0]
    whole = before[0] if chunk > 0 else None
    for p, weight in enumerate((wq, wk, wv)):
        halves = []
        for half in range(2):
            at = p * 128 + half * HDIM
            lanes = [arrived[g, :, at : at + HDIM] for g in range(GROUPS)]
            halves.append(jnp.concatenate(lanes, axis=1))
        y = jnp.concatenate(halves, axis=0)
        made = dot_t(y, weight[...])
        whole = made if whole is None else whole + made
        span = slice(p * 256, (p + 1) * 256)
        held[:, span] += t_dot(n, y)
        bias_grad[0:1, span] += jnp.sum(y.astype(F32), axis=0, keepdims=True)
    if chunk == CHUNKS - 1:
        scaled, spread = norm_rows(x[0].astype(F32))
        total[0] = middle_grad[0] + norm_back(whole * gain[...], scaled, spread)
        bias_grad[0:1, D : 2 * D] += jnp.sum(whole * scaled, axis=0, keepdims=True)
        bias_grad[0:1, 2 * D :] += jnp.sum(whole, axis=0, keepdims=True)
    else:
        total[0] = whole

    @pl.when(image == pl.num_programs(0) - 1)
    def _():
        if len(outs) == 1:
            outs[0][...] = held[...].astype(BF)
            return
        piece = D // plan.wide
        part = piece // groups
        for k in range(groups):
            first = (own[0] + k) % groups * part
            for b in range(plan.wide):
                at = pl.ds(pl.multiple_of(first + b * piece, 8), part)
                outs[k][b] = held[at, :].astype(BF)


def collect(plan, chunk, groups, own, aligned, arrived, normed, weight, *extra):
    rows = pl.BlockSpec((1, 2 * plan.rows, D), lambda i, o: (i, 0, 0))
    columns = [pl.BlockSpec((D, 256), lambda i, o, p=p: (0, p * 3 + chunk)) for p in range(3)]
    last = chunk == CHUNKS - 1
    width = 3 * D if last else D
    fixed = lambda *dims: pl.BlockSpec(dims, lambda i, o: (0,) * len(dims))
    if aligned:
        blocks = [(plan.wide, D // plan.wide // groups, D)] * groups
    else:
        blocks = [(D, D)]
    more = [rows] * (chunk > 0) + ([rows, rows, fixed(1, D)] if last else [])
    total, sums, *outs = pl.pallas_call(
        partial(collect_kernel, plan, chunk, groups, None),
        out_shape=[shape((plan.images, 2 * plan.rows, D), F32), shape((8, width), F32)]
        + [shape(b, BF) for b in blocks],
        grid_spec=pltpu.PrefetchScalarGridSpec(
            num_scalar_prefetch=1,
            grid=(plan.images,),
            in_specs=[pl.BlockSpec((GROUPS, plan.rows, 384), lambda i, o: (i, 0, 0)), rows]
            + columns
            + more,
            out_specs=[rows, fixed(8, width)] + [fixed(*b) for b in blocks],
            scratch_shapes=[pltpu.VMEM((D, D), F32)],
        ),
        compiler_params=params(),
        cost_estimate=pl.CostEstimate(
            flops=8 * 10**9, bytes_accessed=20 << 20, transcendentals=0
        ),
        name="collect",
    )(own, arrived, normed, weight, weight, weight, *extra)
    return (total, sums[0], outs)


def tie(value, *others):
    return lax.optimization_barrier((value, *others))[0]


def exchange(blocks, axis="wide"):
    return lax.all_to_all(blocks, axis, split_axis=0, concat_axis=0, tiled=True)


def share_rows(grad, wide, groups):
    piece = grad.shape[0] // wide // groups
    return grad.astype(BF).reshape(wide, groups, piece, D).transpose(1, 0, 2, 3)


def over_groups(blocks):
    groups = len(blocks)
    got = [blocks[0]]
    for d in range(1, groups):
        pairs = [(i, (i + d) % groups) for i in range(groups)]
        got.append(lax.ppermute(blocks[d], "dp", pairs))
    return got


def turn_groups(low):
    groups = low.shape[0]
    own = lax.axis_index("dp")
    take = lambda i: lax.dynamic_index_in_dim(low, i, 0, keepdims=False)
    return [take((own + d) % groups) for d in range(groups)]


def add_groups(got):
    total = got[0].astype(F32)
    for x in got[1:]:
        total = total + x.astype(F32)
    return total


def add_wide(got):
    return jnp.sum(got.astype(F32), axis=0)


def shards(
    tokens, norm1_gain, norm1_shift, qkv_weight, qv_bias, rel_rows, rel_cols, out_weight, out_bias,
    norm2_gain, norm2_shift, fc1_weight, fc1_bias, fc2_weight, fc2_bias,
    window_place, image_extent, box_mask, out_grad,
):
    wide, groups = (lax.axis_size("wide"), lax.axis_size("dp"))
    me = lax.axis_index("wide").astype(jnp.int32).reshape(1)
    plan = Plan(wide, image_extent.shape[0])
    slots = tokens.shape[0]
    aligned = D // wide // groups % 8 == 0 and D // wide * 4 % 128 == 0
    wide_f = lambda v: v.astype(F32).reshape(1, -1)
    bias = jnp.concatenate([qv_bias[0], jnp.zeros((D,), BF), qv_bias[1]])
    blank = jnp.zeros((1, HDIM), BF)
    table = jnp.concatenate([rel_rows[::-1], blank, rel_cols[::-1], blank], 0)
    table_back = jnp.concatenate([rel_rows[::-1], blank, rel_cols, blank], 0)
    x, normed1, send = enter(
        plan, window_place, me, tokens,
        qkv_weight, wide_f(bias), wide_f(norm1_gain), wide_f(norm1_shift),
    )
    forward = []
    arrived = exchange(send)
    grad_out, *sends = follow(
        plan, window_place, me, out_grad, box_mask, normed1, qkv_weight, wide_f(bias)
    )
    sends = [send, *sends]
    for h in range(CHUNKS):
        if h + 1 < CHUNKS:
            following, arrived = lax.optimization_barrier((sends[h + 1], arrived))
            following = exchange(tie(following, forward[h - 1][2]) if h else following)
        else:
            first, arrived = lax.optimization_barrier((forward[1][0], arrived))
            first = exchange(first)
        earlier = (forward[0][0],) if h == 1 else ()
        forward.append(
            attention_forward(
                plan, slots, window_place, me, image_extent, arrived, table, *earlier
            )
        )
        arrived = following
    last, first = lax.optimization_barrier((forward[2][0], first))
    last = exchange(last)
    rows = plan.images * 2 * plan.rows
    (
        attended, normed2, act_low, grad_before, result, grad_middle, grad_branch,
        send_first, send_last, early,
    ) = middle_part(
        plan, first, last, x, grad_out, out_weight, fc1_weight, fc2_weight,
        wide_f(out_bias), wide_f(fc1_bias), wide_f(fc2_bias), wide_f(norm2_gain), wide_f(norm2_shift),
    )
    grad_middle = grad_middle.reshape(rows, D)
    early = early.reshape(-1)
    grad_arrived = exchange(send_first)
    own = lax.axis_index("dp").astype(jnp.int32).reshape(1)
    if aligned:
        shares = weight_shares(
            plan, groups, own, normed2, grad_before, grad_out, act_low, attended, grad_branch
        )
    else:
        normed2, act_low, attended, _ = lax.optimization_barrier(
            (normed2, act_low, attended, send_first)
        )
        flat = lambda v: v.reshape(rows, v.shape[-1])
        fc1_low = t_dot(flat(normed2), flat(grad_before)).astype(BF)
        fc1_low = fc1_low.reshape(D, groups, D).transpose(1, 0, 2)
        shares = turn_groups(
            jnp.concatenate(
                [
                    fc1_low.reshape(groups, wide, D // wide, D),
                    share_rows(t_dot(flat(act_low), flat(grad_out)), wide, groups),
                    share_rows(t_dot(flat(attended), flat(grad_branch)), wide, groups),
                ],
                axis=2,
            )
        )
    *shares, grad_arrived = lax.optimization_barrier((*shares, grad_arrived))
    shares = over_groups(shares)
    following = exchange(tie(send_last, grad_arrived))

    rel_total = None
    grad_qkv = []
    for h in range(CHUNKS):
        if h == 2:
            *shares, _ = lax.optimization_barrier((*shares, send))
            shares = add_groups(shares)
            grad_arrived, shares = lax.optimization_barrier((grad_arrived, shares))
        send, rel_grad = attention_backward(
            plan, slots, window_place, me, image_extent, grad_arrived, max(h - 1, 0),
            forward[h][1], forward[h][2], table, table_back,
        )
        if h == 0:
            send, grad_arrived = lax.optimization_barrier((send, following))
        rel_total = rel_grad if h == 0 else rel_total + rel_grad
        if h > 0:
            send = tie(send, grad_qkv[-1])
        grad_qkv.append(exchange(send))
        if h + 1 < CHUNKS and h > 0:
            grad_arrived = tie(grad_arrived, grad_qkv[-2])
    shares = lax.psum_scatter(shares.astype(BF), "wide", scatter_dimension=0, tiled=True)[0]
    shares = tie(shares, send)
    shares = lax.all_gather(shares, "dp", axis=0, tiled=False).astype(F32)
    result = tie(result, send)
    tokens_out = leave(
        plan, window_place, me, result.reshape(plan.images, 2 * plan.rows, D), slots, BF
    )
    mid = jnp.concatenate([early, rel_total.reshape(-1), jnp.zeros((512,), F32)]).reshape(-1, D)
    mid = jnp.sum(lax.all_gather(tie(mid, send), "dp", axis=0, tiled=False), axis=0)
    fold = lambda v: v.reshape(plan.images, 2 * plan.rows, D)
    around = lambda b: over_groups(b if aligned else turn_groups(share_rows(b[0], wide, groups)))
    gather = partial(collect, plan)
    fixed = (groups, own, aligned)
    totals, sums0, blocks = gather(0, *fixed, grad_qkv[0], normed1, qkv_weight)
    got0 = around(blocks)
    totals, sums1, blocks = gather(1, *fixed, grad_qkv[1], normed1, qkv_weight, totals)
    got1 = around(blocks)
    *got, _ = lax.optimization_barrier((*got0, *got1, tokens_out))
    ready = [add_groups(got[:groups]).astype(BF), add_groups(got[groups:]).astype(BF)]
    arrived, shares, mid, *ready = lax.optimization_barrier((grad_qkv[2], shares, mid, *ready))
    early_sums = exchange(jnp.concatenate(ready, axis=2))
    totals, sums2, blocks = gather(
        2, *fixed, arrived, normed1, qkv_weight, totals, fold(grad_middle), x, wide_f(norm1_gain)
    )
    weight_grad = add_groups(around(blocks)).astype(BF)
    third = [c[:D].reshape(3, 256) for c in (sums0, sums1, sums2)]
    late = jnp.concatenate([sums2[D:]] + [t[0] for t in third] + [t[2] for t in third])
    small = jnp.concatenate([late.reshape(-1, D), mid], axis=0)
    small = jnp.sum(lax.all_gather(small, "wide", axis=0, tiled=False), axis=0)
    weight_grad, early_sums, small, totals, shares = lax.optimization_barrier(
        (weight_grad, early_sums, small, totals, shares)
    )
    last = exchange(weight_grad)
    share = D // wide
    piece = share // groups
    weight_sums = jnp.concatenate([add_wide(early_sums), add_wide(last)], axis=1)
    last = jnp.concatenate([weight_sums.reshape(-1, D), small[:4]], axis=0)
    last = lax.all_gather(last, "dp", axis=0, tiled=False)
    qkv_weight_grad = last[:, : 3 * piece].reshape(share, CHUNKS, 3, 256)
    qkv_weight_grad = qkv_weight_grad.transpose(0, 2, 1, 3).reshape(share, 3 * D)
    late = jnp.sum(last[:, 3 * piece :], axis=0).reshape(-1)
    sums = small[4:].reshape(-1)
    tokens_grad = leave(plan, window_place, me, totals, slots, F32)
    rel_total = sums[8 * D : 8 * D + HDIM * 256].reshape(HDIM, 256).T
    small = sums[: 8 * D]
    fc2_share = shares[:, share : 2 * share]
    if aligned:
        fc2_share = fc2_share.reshape(groups, share, 2, 4 * share).transpose(3, 0, 2, 1)
    fc2_share = fc2_share.reshape(4 * share, D)
    return (
        tokens_out,
        tokens_grad,
        late[:D],
        late[D : 2 * D],
        qkv_weight_grad,
        late[2 * D :].reshape(2, D),
        rel_total[:127][::-1],
        rel_total[128:255],
        shares[:, 2 * share :].reshape(share, D),
        small[:D],
        small[D : 2 * D],
        small[2 * D : 3 * D],
        shares[:, :share].transpose(1, 0, 2).reshape(share, 4 * D),
        small[3 * D : 7 * D],
        fc2_share,
        small[7 * D :],
    )


def solution(mesh):
    tokens = P(("dp", "wide"), None, None)
    placed = (tokens,) + (P(),) * 14 + (P("dp"), P("dp", None), P(("dp", "wide"), None), tokens)
    shared = P("wide", None)
    return jax.shard_map(
        shards,
        mesh=mesh,
        in_specs=placed,
        out_specs=(
            tokens, tokens, P(), P(), shared, P(), P(), P(), shared, P(), P(), P(), shared, P(),
            shared, P(),
        ),
        check_vma=False,
    )
```

```python
from functools import partial

import jax
import jax.numpy as jnp
from jax import lax
from jax.experimental import pallas as pl
from jax.experimental.pallas import tpu as pltpu
from jax.sharding import PartitionSpec as P

F32 = jnp.float32
BF = jnp.bfloat16
D = 768
HEADS = 12
HDIM = 64
GRID = 64
N = GRID * GRID
WIN = 14
WGRID = 5
WINS = 25
WTOK = 196
HALF = 98
GROUPS = 4
CHUNKS = 3
EPS = 1e-06
NEG = -1e9
VMEM = 60 << 20
KEYS = 512
TILE = 1024


def dot(a, b):
    return jnp.dot(a, b, preferred_element_type=F32)


def dot_t(a, b):
    return lax.dot_general(a, b, (((1,), (1,)), ((), ())), preferred_element_type=F32)


def t_dot(a, b):
    return lax.dot_general(a, b, (((0,), (0,)), ((), ())), preferred_element_type=F32)


def shape(dims, kind):
    return jax.ShapeDtypeStruct(dims, kind)


def params(*semantics):
    return pltpu.CompilerParams(
        dimension_semantics=semantics or ("arbitrary",), vmem_limit_bytes=VMEM
    )


class Plan:
    def __init__(self, wide, images):
        self.wide, self.images = wide, images
        self.corner = WINS % wide == 1 and wide < WINS
        self.full = WINS // wide if self.corner else -(-WINS // wide)
        self.slots = self.full + int(self.corner)
        used = self.full * HALF + 32 * int(self.corner)
        self.rows = max(-(-used // 8) * 8, self.start(self.full - 1) + 112)
        self.tail = self.rows - self.start(self.full)
        self.corner_at = self.full * HALF

    def start(self, m):
        return m * HALF // 16 * 16

    def turn(self, places, slot_count, image):
        return (places[0] // slot_count + WINS * image) % self.wide

    def residue(self, places, slot_count, me, image):
        return (me + 2 * WINS * self.wide - self.turn(places, slot_count, image)) % self.wide

    def slot(self, places, slot_count, me, image, m):
        w = jnp.minimum(self.residue(places, slot_count, me, image) + self.wide * m, WINS - 1)
        return places[image * WINS + w] % slot_count


def norm_rows(values):
    centre = values - jnp.mean(values, axis=-1, keepdims=True)
    spread = lax.rsqrt(jnp.mean(centre * centre, axis=-1, keepdims=True) + EPS)
    return (centre * spread, spread)


def norm_back(weighted, scaled, spread):
    return spread * (
        weighted
        - jnp.mean(weighted, axis=-1, keepdims=True)
        - scaled * jnp.mean(weighted * scaled, axis=-1, keepdims=True)
    )


def place_rows(buffer, values, plan, m):
    if m < plan.full:
        for half in range(2):
            buffer[half, m * HALF : (m + 1) * HALF, :] = values[half * HALF : (half + 1) * HALF, :]
    else:
        for row in range(8):
            at = plan.corner_at + (row % 4) * 8
            buffer[row // 4, at : at + 8, :] = values[row * WIN : row * WIN + 8, :]


def cell_mask(plan, w, live):
    cell = lax.broadcasted_iota(jnp.int32, (WTOK, 1), 0)
    row_end = jnp.where(w // WGRID == WGRID - 1, 8, WIN)
    col_end = jnp.where(w % WGRID == WGRID - 1, 8, WIN)
    return ((cell // WIN < row_end) & (cell % WIN < col_end) & live).astype(F32)


def send_lanes(plan, normed, weights, bias, send):
    for part in range(3):
        at = part * 256
        made = dot(normed, weights[part][...]) + bias[part][...]
        top, low = (made[: plan.rows].astype(BF), made[plan.rows :].astype(BF))
        for g in range(GROUPS):
            own = slice(g * HDIM, (g + 1) * HDIM)
            both = jnp.concatenate([top[:, own], low[:, own]], axis=1)
            send[g, :, part * 128 : (part + 1) * 128] = both


def enter_kernel(plan, places, me, *refs):
    count = plan.slots
    tokens = refs[:count]
    weights, bias = (refs[count : count + 3], refs[count + 3 : count + 6])
    gain, shift, x_out, n_out, send, xbuf = refs[count + 6 :]

    @pl.when(pl.program_id(0) == 0)
    def _():
        xbuf[...] = jnp.zeros_like(xbuf)

    for m in range(count):
        place_rows(xbuf, tokens[m][0].astype(F32), plan, m)
    x = xbuf[...].reshape(2 * plan.rows, D)
    x_out[0] = x.astype(BF)
    scaled, _ = norm_rows(x)
    normed = (scaled * gain[...] + shift[...]).astype(BF)
    n_out[0] = normed
    send_lanes(plan, normed, weights, bias, send)


def follow_kernel(plan, places, me, *refs):
    count = plan.slots
    grads = refs[:count]
    box, normed = refs[count : count + 2]
    weights, bias = (refs[count + 2 : count + 8], refs[count + 8 : count + 14])
    g_out, *sends = refs[count + 14 : count + 17]
    gbuf, turned = refs[count + 17 :]
    image = pl.program_id(0)
    slot_count = box.shape[0]

    @pl.when(image == 0)
    def _():
        gbuf[...] = jnp.zeros_like(gbuf)
        turned[...] = box[...].astype(F32).T

    for h in range(2):
        own = slice(h * 3, h * 3 + 3)
        send_lanes(plan, normed[0], weights[own], bias[own], sends[h])
    residue = plan.residue(places, slot_count, me[0], image)
    for m in range(count):
        w = residue + plan.wide * m
        slot = plan.slot(places, slot_count, me[0], image, m)
        lane = lax.broadcasted_iota(jnp.int32, (WTOK, slot_count), 1)
        inside = jnp.sum(jnp.where(lane == slot, turned[...], 0.0), axis=1, keepdims=True)
        inside = inside * cell_mask(plan, w, w < WINS)
        place_rows(gbuf, grads[m][0].astype(F32) * inside, plan, m)
    g_out[0] = gbuf[...].reshape(2 * plan.rows, D).astype(BF)


def entry_specs(plan, slot_count):
    windows = [
        pl.BlockSpec((1, WTOK, D), lambda i, p, a, m=m: (plan.slot(p, slot_count, a[0], i, m), 0, 0))
        for m in range(plan.slots)
    ]
    column = lambda rows, h: [
        pl.BlockSpec((rows, 256), lambda i, p, a, b=part * CHUNKS + h: (0, b)) for part in range(3)
    ]
    rows = pl.BlockSpec((1, 2 * plan.rows, D), lambda i, p, a: (i, 0, 0))
    send = pl.BlockSpec((GROUPS, plan.rows, 384), lambda i, p, a: (i, 0, 0))
    return (windows, column, rows, send)


def enter(plan, places, me, tokens, weight, bias, gain, shift):
    windows, column, rows, send = entry_specs(plan, tokens.shape[0])
    fixed = pl.BlockSpec((1, D), lambda i, p, a: (0, 0))
    working = shape((plan.images, 2 * plan.rows, D), BF)
    return pl.pallas_call(
        partial(enter_kernel, plan),
        out_shape=[working, working, shape((plan.wide, plan.rows, 384), BF)],
        grid_spec=pltpu.PrefetchScalarGridSpec(
            num_scalar_prefetch=2,
            grid=(plan.images,),
            in_specs=windows + column(D, 0) + column(1, 0) + [fixed, fixed],
            out_specs=[rows, rows, send],
            scratch_shapes=[pltpu.VMEM((2, plan.rows, D), F32)],
        ),
        compiler_params=params(),
        cost_estimate=pl.CostEstimate(
            flops=2 * 10**9, bytes_accessed=10 << 20, transcendentals=0
        ),
        name="enter",
    )(places, me, *([tokens] * plan.slots), *([weight] * 3), *([bias] * 3), gain, shift)


def follow(plan, places, me, out_grad, box_mask, normed, weight, bias):
    slot_count = out_grad.shape[0]
    windows, column, rows, send = entry_specs(plan, slot_count)
    fixed = pl.BlockSpec(box_mask.shape, lambda i, p, a: (0, 0))
    block = shape((plan.wide, plan.rows, 384), BF)
    return pl.pallas_call(
        partial(follow_kernel, plan),
        out_shape=[shape((plan.images, 2 * plan.rows, D), BF), block, block],
        grid_spec=pltpu.PrefetchScalarGridSpec(
            num_scalar_prefetch=2,
            grid=(plan.images,),
            in_specs=windows
            + [fixed, rows]
            + column(D, 1)
            + column(D, 2)
            + column(1, 1)
            + column(1, 2),
            out_specs=[rows, send, send],
            scratch_shapes=[
                pltpu.VMEM((2, plan.rows, D), F32),
                pltpu.VMEM((WTOK, slot_count), F32),
            ],
        ),
        compiler_params=params(),
        cost_estimate=pl.CostEstimate(
            flops=4 * 10**9, bytes_accessed=16 << 20, transcendentals=0
        ),
        name="follow",
    )(places, me, *([out_grad] * plan.slots), box_mask, normed, *([weight] * 6), *([bias] * 6))


def leave_kernel(plan, places, me, values, out, held):
    slot = pl.program_id(0)
    slot_count = pl.num_programs(0)
    held[...] = jnp.zeros_like(held)
    for image in range(plan.images):
        residue = plan.residue(places, slot_count, me[0], image)
        for m in range(plan.slots):
            w = residue + plan.wide * m
            place = places[image * WINS + jnp.minimum(w, WINS - 1)]
            hit = (w < WINS) & (place == me[0] * slot_count + slot)

            @pl.when(hit)
            def _(image=image, m=m, w=w):
                if m < plan.full:
                    keep = cell_mask(plan, w, w < WINS)
                    for half in range(2):
                        at = half * plan.rows + m * HALF
                        part = slice(half * HALF, (half + 1) * HALF)
                        held[part, :] = values[image, at : at + HALF, :] * keep[part]
                else:
                    for row in range(8):
                        at = (row // 4) * plan.rows + plan.corner_at + (row % 4) * 8
                        held[row * WIN : row * WIN + 8, :] = values[image, at : at + 8, :]

    out[0] = held[...].astype(out.dtype)


def leave(plan, places, me, values, slot_count, kind):
    return pl.pallas_call(
        partial(leave_kernel, plan),
        out_shape=shape((slot_count, WTOK, D), kind),
        grid_spec=pltpu.PrefetchScalarGridSpec(
            num_scalar_prefetch=2,
            grid=(slot_count,),
            in_specs=[
                pl.BlockSpec(values.shape, lambda j, p, a: (0, 0, 0), pipeline_mode=pl.Buffered(1))
            ],
            out_specs=pl.BlockSpec((1, WTOK, D), lambda j, p, a: (j, 0, 0)),
            scratch_shapes=[pltpu.VMEM((WTOK, D), F32)],
        ),
        compiler_params=params(),
        cost_estimate=pl.CostEstimate(flops=1 << 20, bytes_accessed=12 << 20, transcendentals=0),
        name="leave",
    )(places, me, values)


def spread_matrix(plan, band, flip):
    dims = (560, 448) if flip else (448, 560)
    cell = lax.broadcasted_iota(jnp.int32, dims, 1 if flip else 0)
    item = lax.broadcasted_iota(jnp.int32, dims, 0 if flip else 1)
    row, col = (cell // GRID, cell % GRID)
    block = col // WIN
    shift = jnp.zeros(dims, jnp.int32)
    for c in range(WGRID):
        m = (band * WGRID + c) // plan.wide
        if m < plan.full:
            shift = jnp.where(block == c, m * HALF - plan.start(m), shift)
        else:
            shift = jnp.where(block == c, -10000, shift)
    return (item == block * 112 + shift + row * WIN + col % WIN).astype(F32).astype(BF)


def corner_matrix(plan, flip):
    dims = (plan.tail, 256) if flip else (256, plan.tail)
    cell = lax.broadcasted_iota(jnp.int32, dims, 1 if flip else 0)
    item = lax.broadcasted_iota(jnp.int32, dims, 0 if flip else 1)
    row, col = (cell // GRID, cell % GRID)
    at = plan.corner_at - plan.start(plan.full)
    hit = (col >= 4 * WIN) & (item == at + row * 8 + col - 4 * WIN)
    return hit.astype(F32).astype(BF)


def gather_grid(plan, turn, arrived, band):
    pieces = []
    for c in range(WGRID):
        w = band * WGRID + c
        m = w // plan.wide
        if m < plan.full:
            source = (w % plan.wide + turn) % plan.wide
            at = plan.start(m)
        else:
            source, at = (0, 0)
        pieces.append(arrived[source, at : at + 112, :])
    found = dot(spread_matrix(plan, band, False), jnp.concatenate(pieces, axis=0))
    return found


def grid_rows(plan, turn, arrived, parts, store):
    for band in range(WGRID):
        found = gather_grid(plan, turn, arrived, band)
        last = band == WGRID - 1
        if last and plan.corner:
            source = ((WINS - 1) % plan.wide + turn) % plan.wide
            at = plan.start(plan.full)
            extra = dot(corner_matrix(plan, False), arrived[source, at : at + plan.tail, :])
        for part in range(parts):
            top = found[:, part * 128 : part * 128 + HDIM]
            low = found[:, part * 128 + HDIM : (part + 1) * 128]
            if last:
                low = low[:GRID]
            whole = jnp.concatenate([top, low], axis=0)
            if last and plan.corner:
                more = jnp.concatenate(
                    [
                        extra[:, part * 128 : part * 128 + HDIM],
                        extra[:, part * 128 + HDIM : (part + 1) * 128],
                    ],
                    axis=0,
                )
                whole = whole + more
            store(part, band * WIN * GRID, whole)


def scatter_grid(plan, turn, out, parts, load, lane=0):
    span = slice(lane, lane + parts * 128)
    out[:, :, span] = jnp.zeros((plan.wide, plan.rows, parts * 128), BF)
    for band in range(WGRID):
        last = band == WGRID - 1
        base = band * WIN * GRID
        lanes = []
        for part in range(parts):
            top = load(part, base, 448)
            if last:
                low = load(part, base + 448, GRID)
                low = jnp.concatenate([low, jnp.zeros((448 - GRID, HDIM), BF)], axis=0)
            else:
                low = load(part, base + 448, 448)
            lanes += [top, low]
        made = dot(spread_matrix(plan, band, True), jnp.concatenate(lanes, axis=1)).astype(BF)
        for c in range(WGRID):
            w = band * WGRID + c
            m = w // plan.wide
            if m < plan.full:
                dest = (w % plan.wide + turn) % plan.wide
                at = plan.start(m)
                out[dest, at : at + 112, span] += made[c * 112 : (c + 1) * 112]
        if last and plan.corner:
            lanes = []
            for part in range(parts):
                lanes += [load(part, base, 256), load(part, base + 256, 256)]
            made = dot(corner_matrix(plan, True), jnp.concatenate(lanes, axis=1)).astype(BF)
            dest = ((WINS - 1) % plan.wide + turn) % plan.wide
            at = plan.start(plan.full)
            out[dest, at : at + plan.tail, span] += made


def split(x):
    high = x.astype(BF)
    return (high, (x - high.astype(F32)).astype(BF))


def key_marks():
    feature = lax.broadcasted_iota(jnp.int32, (192, N // 2), 0)
    key = lax.broadcasted_iota(jnp.int32, (192, N // 2), 1)
    col = (feature % GRID) == (key % GRID)
    row = ((feature - 128) % 32) == (key // GRID)
    return jnp.where(feature < 128, col.astype(F32), row.astype(F32)).astype(BF)


def rel_terms(q, table, extent_rows, extent_cols, first_row, count):
    both = dot_t(q, table)
    lane = lax.broadcasted_iota(jnp.int32, (GRID, 128), 1)
    row_mask = jnp.where(lane < extent_rows, 0.0, NEG)
    col_mask = jnp.where(lane < extent_cols, 0.0, NEG)
    rows, cols = ([], [])
    for i in range(count):
        part = both[i * GRID : (i + 1) * GRID]
        rows.append(pltpu.roll(part[:, :128], (first_row + i + 65) % 128, 1) + row_mask)
        cols.append(pltpu.roll(part[:, 128:], 65, 1, stride=1, stride_axis=0) + col_mask)
    return (jnp.concatenate(rows, 0)[:, :GRID], jnp.concatenate(cols, 0)[:, :GRID])


def query_marks(q, rows, cols):
    rh, rl = split(rows)
    ch, cl = split(cols)
    scaled = (q.astype(F32) * 0.125).astype(BF)
    return [
        jnp.concatenate([scaled, ch, cl, rh[:, i : i + 32], rl[:, i : i + 32]], 1) for i in (0, 32)
    ]


def forward_kernel(plan, tile, slot_count, keep, places, me, extent, arrived, table, *refs):
    refs, (kt, va, held) = (refs[:-3], refs[-3:])
    refs, probs = (refs[:-1], refs[-1]) if keep else (refs, None)
    earlier, (send, kept, saved) = (refs[:-3], refs[-3:])
    step = pl.program_id(0)
    image = me[0] // GROUPS
    turn = plan.turn(places, slot_count, image)

    @pl.when(step == 0)
    def _():
        marks = key_marks()
        kt[HDIM:, : N // 2] = marks
        kt[HDIM:, N // 2 :] = marks
        va[:, HDIM:] = (lax.broadcasted_iota(jnp.int32, (N, HDIM), 1) == 0).astype(F32).astype(BF)

        def store(part, first, values):
            kept[part, first : first + values.shape[0], :] = values.astype(BF)

        grid_rows(plan, turn, arrived, 3, store)
        kt[:HDIM, :] = kept[1].astype(F32).T.astype(BF)
        va[:, :HDIM] = kept[2]

    here = pl.ds(pl.multiple_of(step * tile, tile), tile)
    q = kept[0, here, :]
    count = tile // GRID
    rows, cols = rel_terms(q, table[...], extent[image, 0], extent[image, 1], step * count, count)
    marks = query_marks(q, rows, cols)
    side = N // 2
    score = lambda c: dot(marks[c * KEYS // side], kt[:, c * KEYS : (c + 1) * KEYS])
    total, top, now, tops = (None, None, score(0), [])
    for c in range(N // KEYS):
        following = score(c + 1) if c + 1 < N // KEYS else None
        higher = jnp.max(now, axis=1, keepdims=True)
        if c:
            higher = jnp.maximum(top, higher)
        weights = jnp.exp(now - higher).astype(BF)
        tops.append(higher)
        if keep:
            probs[:, c * KEYS : (c + 1) * KEYS] = weights
        x = dot(weights, va[c * KEYS : (c + 1) * KEYS, :])
        total = total * jnp.exp(top - higher) + x if c else x
        top, now = (higher, following)
    mass = total[:, HDIM : HDIM + 1]
    out = total * (1.0 / mass)
    lane = lax.broadcasted_iota(jnp.int32, (tile, 128), 1)
    level = top + jnp.log(mass)
    if keep:
        for c, higher in enumerate(tops):
            out = jnp.where(lane == HDIM + c, jnp.exp(higher - level), out)
        saved[...] = out
    else:
        saved[...] = jnp.where(lane < HDIM, out, level)
    held[here, :] = out[:, :HDIM].astype(BF)

    @pl.when(step == pl.num_programs(0) - 1)
    def _():
        load = lambda part, first, size: held[first : first + size, :]
        scatter_grid(plan, turn, send, 1, load, 128 * len(earlier))
        for i, block in enumerate(earlier):
            send[:, :, 128 * i : 128 * (i + 1)] = block[...]


def attention_forward(
    plan, slot_count, places, me, extent, arrived, table, *earlier, keep=False, tile=TILE
):
    lanes = 128 * (1 + len(earlier))
    whole = lambda *dims: pl.BlockSpec(dims, lambda t, *_: (0,) * len(dims))
    return pl.pallas_call(
        partial(forward_kernel, plan, tile, slot_count, keep),
        out_shape=(
            shape((plan.wide, plan.rows, lanes), BF),
            shape((3, N, HDIM), BF),
            shape((N, 128), F32),
        )
        + (shape((N, N), BF),) * keep,
        grid_spec=pltpu.PrefetchScalarGridSpec(
            num_scalar_prefetch=3,
            grid=(N // tile,),
            in_specs=[whole(*x.shape) for x in (arrived, table, *earlier)],
            out_specs=[
                whole(plan.wide, plan.rows, lanes),
                whole(3, N, HDIM),
                pl.BlockSpec((tile, 128), lambda t, *_: (t, 0)),
            ]
            + [pl.BlockSpec((tile, N), lambda t, *_: (t, 0))] * keep,
            scratch_shapes=[
                pltpu.VMEM((256, N), BF),
                pltpu.VMEM((N, 128), BF),
                pltpu.VMEM((N, HDIM), BF),
            ],
        ),
        compiler_params=params(),
        cost_estimate=pl.CostEstimate(
            flops=4 * N * N * 256, bytes_accessed=12 << 20, transcendentals=N * N
        ),
        name="attention_forward",
    )(places, me, extent, arrived, table, *earlier)


def backward_kernel(
    plan, tile, slot_count, places, me, extent,
    arrived, kept, saved, table, table_back,
    send, rel_grad,
    kt, vt, ka, dout, dq, dk, dv,
):
    step = pl.program_id(0)
    image = me[0] // GROUPS
    turn = plan.turn(places, slot_count, image)
    side = N // 2

    @pl.when(step == 0)
    def _():
        marks = key_marks()
        kt[HDIM:, :side] = marks
        kt[HDIM:, side:] = marks
        minus = lax.broadcasted_iota(jnp.int32, (HDIM, N), 0) < 2
        vt[HDIM:, :] = jnp.where(minus, -1.0, 0.0).astype(BF)
        key = lax.broadcasted_iota(jnp.int32, (N, 128), 0)
        mark = lax.broadcasted_iota(jnp.int32, (N, 128), 1)
        col = (GRID - 1 - mark) == key % GRID
        row = (mark - GRID) == key // GRID
        ka[:, HDIM:192] = jnp.where(mark < GRID, col.astype(F32), row.astype(F32)).astype(BF)
        ka[:, 192:] = jnp.zeros((N, HDIM), BF)
        rel_grad[...] = jnp.zeros_like(rel_grad)
        dk[...] = jnp.zeros_like(dk)
        dv[...] = jnp.zeros_like(dv)
        keys = kept[1].astype(F32)
        kt[:HDIM, :] = keys.T.astype(BF)
        ka[:, :HDIM] = (keys * 0.125).astype(BF)
        vt[:HDIM, :] = kept[2].astype(F32).T.astype(BF)

        def store(part, first, values):
            dout[first : first + values.shape[0], :] = values.astype(BF)

        grid_rows(plan, turn, arrived, 1, store)

    here = pl.ds(pl.multiple_of(step * tile, tile), tile)
    q = kept[0, here, :]
    do = dout[here, :]
    old = saved[...]
    count = tile // GRID
    inner = jnp.sum(do.astype(F32) * old[:, :HDIM], axis=1, keepdims=True)
    rows, cols = rel_terms(q, table[...], extent[image, 0], extent[image, 1], step * count, count)
    marks = query_marks(q, rows - old[:, HDIM : HDIM + 1], cols)
    high, low = split(inner)
    lane = lax.broadcasted_iota(jnp.int32, (tile, HDIM), 1)
    less = jnp.where(lane == 0, high.astype(F32), jnp.where(lane == 1, low.astype(F32), 0.0))
    do_less = jnp.concatenate([do, less.astype(BF)], 1)
    q_turned = (q.astype(F32) * 0.125).T.astype(BF)
    do_turned = do.astype(F32).T.astype(BF)
    def products(c):
        part = slice(c * KEYS, (c + 1) * KEYS)
        return (dot(marks[c * KEYS // side], kt[:, part]), dot(do_less, vt[:, part]))

    back, now = (None, products(0))
    for c in range(N // KEYS):
        part = slice(c * KEYS, (c + 1) * KEYS)
        following = products(c + 1) if c + 1 < N // KEYS else None
        weights = jnp.exp(now[0])
        dscore = (weights * now[1]).astype(BF)
        dv[:, part] += dot(do_turned, weights.astype(BF))
        dk[:, part] += dot(q_turned, dscore)
        x = dot(dscore, ka[part, :])
        back = x if back is None else back + x
        now = following
    blank = jnp.zeros((GRID, HDIM), F32)
    offsets = []
    for i in range(count):
        own = slice(i * GRID, (i + 1) * GRID)
        row_part = jnp.concatenate([back[own, 128:192], blank], 1)
        col_part = jnp.concatenate([back[own, HDIM:128], blank], 1)
        row_part = pltpu.roll(row_part, (2 * GRID - 1 + GRID - step * count - i) % 128, 1)
        col_part = pltpu.roll(col_part, 0, 1, stride=1, stride_axis=0)
        offsets.append(jnp.concatenate([row_part, col_part], 1))
    high, low = split(jnp.concatenate(offsets, 0))
    rel = table_back[...]
    both = dot(jnp.concatenate([high, low], 1), jnp.concatenate([rel, rel], 0))
    dq[here, :] = (back[:, :HDIM] + both).astype(BF)
    q_whole = q.astype(F32).T.astype(BF)
    rel_grad[...] += dot(q_whole, high) + dot(q_whole, low)

    @pl.when(step == pl.num_programs(0) - 1)
    def _():
        def load(part, first, size):
            if part == 0:
                return dq[first : first + size, :]
            return turned[part - 1][first : first + size, :]

        turned = (dk[...].T.astype(BF), dv[...].T.astype(BF))
        scatter_grid(plan, turn, send, 3, load)


def attention_backward(
    plan, slot_count, places, me, extent, arrived, lane, kept, saved, table, table_back, tile=TILE
):
    whole = lambda *dims: pl.BlockSpec(dims, lambda t, *_: (0,) * len(dims))
    return pl.pallas_call(
        partial(backward_kernel, plan, tile, slot_count),
        out_shape=(shape((plan.wide, plan.rows, 384), BF), shape((HDIM, 256), F32)),
        grid_spec=pltpu.PrefetchScalarGridSpec(
            num_scalar_prefetch=3,
            grid=(N // tile,),
            in_specs=[
                pl.BlockSpec((plan.wide, plan.rows, 128), lambda t, *_: (0, 0, lane)),
                whole(3, N, HDIM),
                pl.BlockSpec((tile, 128), lambda t, *_: (t, 0)),
                whole(*table.shape),
                whole(*table_back.shape),
            ],
            out_specs=[whole(plan.wide, plan.rows, 384), whole(HDIM, 256)],
            scratch_shapes=[
                pltpu.VMEM((256, N), BF),
                pltpu.VMEM((128, N), BF),
                pltpu.VMEM((N, 256), BF),
                pltpu.VMEM((N, HDIM), BF),
                pltpu.VMEM((N, HDIM), BF),
                pltpu.VMEM((HDIM, N), F32),
                pltpu.VMEM((HDIM, N), F32),
            ],
        ),
        compiler_params=params(),
        cost_estimate=pl.CostEstimate(
            flops=10 * N * N * 256, bytes_accessed=12 << 20, transcendentals=N * N
        ),
        name="attention_backward",
    )(places, me, extent, arrived, kept, saved, table, table_back)


def replay_kernel(
    plan, tile, slot_count, places, me,
    arrived, kept, saved, probs, table_back,
    send, rel_grad,
    vt, ka, dout, dq, dk, dv,
):
    step = pl.program_id(0)
    image = me[0] // GROUPS
    turn = plan.turn(places, slot_count, image)

    @pl.when(step == 0)
    def _():
        minus = lax.broadcasted_iota(jnp.int32, (HDIM, N), 0) < 2
        vt[HDIM:, :] = jnp.where(minus, -1.0, 0.0).astype(BF)
        key = lax.broadcasted_iota(jnp.int32, (N, 128), 0)
        mark = lax.broadcasted_iota(jnp.int32, (N, 128), 1)
        col = (GRID - 1 - mark) == key % GRID
        row = (mark - GRID) == key // GRID
        ka[:, HDIM:192] = jnp.where(mark < GRID, col.astype(F32), row.astype(F32)).astype(BF)
        ka[:, 192:] = jnp.zeros((N, HDIM), BF)
        rel_grad[...] = jnp.zeros_like(rel_grad)
        dk[...] = jnp.zeros_like(dk)
        dv[...] = jnp.zeros_like(dv)
        ka[:, :HDIM] = (kept[1].astype(F32) * 0.125).astype(BF)
        vt[:HDIM, :] = kept[2].astype(F32).T.astype(BF)

        def store(part, first, values):
            dout[first : first + values.shape[0], :] = values.astype(BF)

        grid_rows(plan, turn, arrived, 1, store)

    here = pl.ds(pl.multiple_of(step * tile, tile), tile)
    q = kept[0, here, :]
    do = dout[here, :].astype(F32)
    old = saved[...]
    count = tile // GRID
    inner = jnp.sum(do * old[:, :HDIM], axis=1, keepdims=True)
    lane = lax.broadcasted_iota(jnp.int32, (tile, HDIM), 1)
    q_turned = (q.astype(F32) * 0.125).T.astype(BF)
    do_turned = do.T
    factors = old[:, HDIM:].T

    def products(c):
        part = slice(c * KEYS, (c + 1) * KEYS)
        factor = old[:, HDIM + c : HDIM + c + 1]
        high, low = split(inner * factor)
        less = jnp.where(lane == 0, high.astype(F32), jnp.where(lane == 1, low.astype(F32), 0.0))
        do_less = jnp.concatenate([(do * factor).astype(BF), less.astype(BF)], 1)
        return dot(do_less, vt[:, part])

    back, now = (None, products(0))
    for c in range(N // KEYS):
        part = slice(c * KEYS, (c + 1) * KEYS)
        following = products(c + 1) if c + 1 < N // KEYS else None
        weights = probs[:, part]
        dscore = (weights.astype(F32) * now).astype(BF)
        dv[:, part] += dot((do_turned * factors[c : c + 1, :]).astype(BF), weights)
        dk[:, part] += dot(q_turned, dscore)
        x = dot(dscore, ka[part, :])
        back = x if back is None else back + x
        now = following
    blank = jnp.zeros((GRID, HDIM), F32)
    offsets = []
    for i in range(count):
        own = slice(i * GRID, (i + 1) * GRID)
        row_part = jnp.concatenate([back[own, 128:192], blank], 1)
        col_part = jnp.concatenate([back[own, HDIM:128], blank], 1)
        row_part = pltpu.roll(row_part, (2 * GRID - 1 + GRID - step * count - i) % 128, 1)
        col_part = pltpu.roll(col_part, 0, 1, stride=1, stride_axis=0)
        offsets.append(jnp.concatenate([row_part, col_part], 1))
    high, low = split(jnp.concatenate(offsets, 0))
    rel = table_back[...]
    both = dot(jnp.concatenate([high, low], 1), jnp.concatenate([rel, rel], 0))
    dq[here, :] = (back[:, :HDIM] + both).astype(BF)
    q_whole = q.astype(F32).T.astype(BF)
    rel_grad[...] += dot(q_whole, high) + dot(q_whole, low)

    @pl.when(step == pl.num_programs(0) - 1)
    def _():
        def load(part, first, size):
            if part == 0:
                return dq[first : first + size, :]
            return turned[part - 1][first : first + size, :]

        turned = (dk[...].T.astype(BF), dv[...].T.astype(BF))
        scatter_grid(plan, turn, send, 3, load)


def attention_replay(
    plan, slot_count, places, me, arrived, lane, kept, saved, probs, table_back, tile=TILE
):
    whole = lambda *dims: pl.BlockSpec(dims, lambda t, *_: (0,) * len(dims))
    return pl.pallas_call(
        partial(replay_kernel, plan, tile, slot_count),
        out_shape=(shape((plan.wide, plan.rows, 384), BF), shape((HDIM, 256), F32)),
        grid_spec=pltpu.PrefetchScalarGridSpec(
            num_scalar_prefetch=2,
            grid=(N // tile,),
            in_specs=[
                pl.BlockSpec((plan.wide, plan.rows, 128), lambda t, *_: (0, 0, lane)),
                whole(3, N, HDIM),
                pl.BlockSpec((tile, 128), lambda t, *_: (t, 0)),
                pl.BlockSpec((tile, N), lambda t, *_: (t, 0)),
                whole(*table_back.shape),
            ],
            out_specs=[whole(plan.wide, plan.rows, 384), whole(HDIM, 256)],
            scratch_shapes=[
                pltpu.VMEM((128, N), BF),
                pltpu.VMEM((N, 256), BF),
                pltpu.VMEM((N, HDIM), BF),
                pltpu.VMEM((N, HDIM), BF),
                pltpu.VMEM((HDIM, N), F32),
                pltpu.VMEM((HDIM, N), F32),
            ],
        ),
        compiler_params=params(),
        cost_estimate=pl.CostEstimate(
            flops=10 * N * N * 256, bytes_accessed=44 << 20, transcendentals=0
        ),
        name="attention_replay",
    )(places, me, arrived, kept, saved, probs, table_back)


def middle_kernel(
    plan, first, last, x, g, out_weight, fc1_weight, fc2_weight,
    out_bias, fc1_bias, fc2_bias, gain, shift,
    attended, normed, act, grad_before, result, grad_middle, grad_branch, send_first, send_last, sums,
    grads,
):
    step = pl.program_id(0)
    half = step % 2
    blocks = [first.at[:, :, :128], first.at[:, :, 128:], last]
    for side in range(2):

        @pl.when(half == side)
        def _(side=side):
            lanes = [
                blocks[h][k, :, side * HDIM : (side + 1) * HDIM]
                for h in range(CHUNKS)
                for k in range(GROUPS)
            ]
            attended[0] = jnp.concatenate(lanes, axis=1)

    @pl.when(step == 0)
    def _():
        sums[...] = jnp.zeros_like(sums)

    middle = x[0].astype(F32) + (dot(attended[0], out_weight[...]) + out_bias[...])
    scaled, spread = norm_rows(middle)
    n = (scaled * gain[...] + shift[...]).astype(BF)
    normed[0] = n
    grad = g[0]
    total, grad_normed = (None, None)
    add = lambda old, new: new if old is None else old + new

    def products(c):
        span = slice(c * D, (c + 1) * D)
        return (dot(n, fc1_weight[:, span]), dot_t(grad, fc2_weight[span, :]))

    now = products(0)
    for c in range(4):
        span = slice(c * D, (c + 1) * D)
        following = products(c + 1) if c < 3 else None
        before = now[0] + fc1_bias[:, span]
        share = 0.5 + 0.5 * lax.erf(before * (0.5**0.5))
        low = (before * share).astype(BF)
        act[0, :, span] = low
        slope = share + before * (jnp.exp(before * before * -0.5) * 0.3989422804014327)
        back = (now[1] * slope).astype(BF)
        grad_before[0, :, span] = back
        sums[:, (3 + c) * D : (4 + c) * D] += jnp.sum(back.astype(F32), axis=0, keepdims=True)
        total = add(total, dot(low, fc2_weight[span, :]))
        grad_normed = add(grad_normed, dot_t(back, fc1_weight[:, span]))
        now = following
    result[0] = middle + total + fc2_bias[...]
    full = grad.astype(F32) + norm_back(grad_normed * gain[...], scaled, spread)
    grad_middle[0] = full
    branch = full.astype(BF)
    grad_branch[0] = branch
    for place, value in (
        (0, branch.astype(F32)), (1, grad_normed * scaled), (2, grad_normed), (7, grad.astype(F32))
    ):
        sums[:, place * D : (place + 1) * D] += jnp.sum(value, axis=0, keepdims=True)
    grads[...] = dot_t(branch, out_weight[...]).astype(BF)
    targets = [send_first, send_last.at[:, :, :128], send_last.at[:, :, 128:]]
    for side in range(2):

        @pl.when(half == side)
        def _(side=side):
            for h in range(CHUNKS):
                for k in range(GROUPS):
                    at = (h * GROUPS + k) * HDIM
                    made = grads[:, at : at + HDIM]
                    targets[h][k, :, side * HDIM : (side + 1) * HDIM] = made


def middle_part(plan, first, last, x, g, out_weight, fc1_weight, fc2_weight, *vectors):
    rows, hidden = (plan.rows, fc1_weight.shape[1])
    halves = 2 * plan.images
    x, g = (v.reshape(halves, rows, D) for v in (x, g))
    row = lambda width: pl.BlockSpec((1, rows, width), lambda i: (i, 0, 0))
    whole = lambda v: pl.BlockSpec(v.shape, lambda i: (0, 0), pipeline_mode=pl.Buffered(1))
    block = lambda lanes: pl.BlockSpec((GROUPS, rows, lanes), lambda i: (i // 2, 0, 0))
    made = lambda width, kind: shape((halves, rows, width), kind)
    fixed = (out_weight, fc1_weight, fc2_weight, *vectors)
    return pl.pallas_call(
        partial(middle_kernel, plan),
        out_shape=(
            made(D, BF), made(D, BF), made(hidden, BF), made(hidden, BF),
            made(D, F32), made(D, F32), made(D, BF),
            shape((plan.wide, rows, 128), BF), shape((plan.wide, rows, 256), BF),
            shape((1, 8 * D), F32),
        ),
        grid=(halves,),
        in_specs=[block(256), block(128), row(D), row(D)] + [whole(v) for v in fixed],
        out_specs=(
            row(D), row(D), row(hidden), row(hidden), row(D), row(D), row(D),
            block(128), block(256), pl.BlockSpec((1, 8 * D), lambda i: (0, 0)),
        ),
        scratch_shapes=[pltpu.VMEM((rows, D), BF)],
        compiler_params=params(),
        cost_estimate=pl.CostEstimate(
            flops=30 * 10**9, bytes_accessed=40 << 20, transcendentals=8 << 20
        ),
        name="middle",
    )(first, last, x, g, *fixed)


def shares_kernel(
    plan, groups, own, normed, grad_before, g, act, attended, branch,
    o0, o1, o2, o3, fc1, fc2, out, ready, turned_n, turned_g, sem,
):
    step, image = (pl.program_id(0), pl.program_id(1))
    finished = image == pl.num_programs(1) - 1
    outs = (o0, o1, o2, o3)
    d = (own[0] + step) % groups
    piece = D // plan.wide
    part = piece // groups
    width = D // groups

    @pl.when(image == 0)
    def _():
        fc1[...] = jnp.zeros_like(fc1)
        fc2[...] = jnp.zeros_like(fc2)

    @pl.when((image == 0) & (step == 0))
    def _():
        out[...] = jnp.zeros_like(out)

    @pl.when(step == 0)
    def _():
        turned_n[image] = normed[0].astype(F32).T.astype(BF)
        turned_g[image] = g[0].astype(F32).T.astype(BF)
        out[...] += t_dot(attended[0], branch[0])

    fc1[...] += dot(turned_n[image], grad_before[0])
    for k in range(groups):

        @pl.when(d == k)
        def _(k=k):
            fc2[...] += dot(turned_g[image, k * width : (k + 1) * width, :], act[0])

    for k in range(groups):

        @pl.when(finished & (step == k))
        def _(k=k):
            if k:
                pltpu.make_async_copy(ready, outs[k - 1], sem).wait()
            for b in range(plan.wide):
                ready[b, :piece, :] = fc1[b * piece : (b + 1) * piece, :].astype(BF)
                cols = slice(b * 4 * piece, (b + 1) * 4 * piece)
                for side in range(2):
                    lanes = slice(side * 4 * piece, (side + 1) * 4 * piece)
                    upper = fc2[side * piece : (side + 1) * piece, cols]
                    ready[b, piece : 2 * piece, lanes] = upper.astype(BF)
                at = pl.ds(pl.multiple_of(b * piece + d * part, 8), part)
                ready[b, 2 * piece :, :] = out[at, :].astype(BF)
            copy = pltpu.make_async_copy(ready, outs[k], sem)
            copy.start()
            if k == groups - 1:
                copy.wait()


def weight_shares(plan, groups, own, normed, grad_before, g, act, attended, branch):
    rows = 2 * plan.rows
    fold = lambda v: v.reshape(plan.images, rows, v.shape[-1])
    values = [fold(v) for v in (normed, grad_before, g, act, attended, branch)]
    once = pl.BlockSpec((1, rows, D), lambda s, i, o: (jnp.where(s == 0, i, plan.images - 1), 0, 0))
    wide = pl.BlockSpec((1, rows, values[3].shape[-1]), lambda s, i, o: (i, 0, 0))
    column = pl.BlockSpec((1, rows, D), lambda s, i, o: (i, 0, (o[0] + s) % groups))
    block = (plan.wide, 2 * D // plan.wide + D // plan.wide // groups, D)
    return pl.pallas_call(
        partial(shares_kernel, plan, groups),
        out_shape=[shape(block, BF)] * groups,
        grid_spec=pltpu.PrefetchScalarGridSpec(
            num_scalar_prefetch=1,
            grid=(groups, plan.images),
            in_specs=[once, column, once, wide, once, once],
            out_specs=[pl.BlockSpec(memory_space=pl.ANY)] * groups,
            scratch_shapes=[
                pltpu.VMEM((D, D), F32),
                pltpu.VMEM((D // groups, 4 * D), F32),
                pltpu.VMEM((D, D), F32),
                pltpu.VMEM(block, BF),
                pltpu.VMEM((plan.images, D, rows), BF),
                pltpu.VMEM((plan.images, D, rows), BF),
                pltpu.SemaphoreType.DMA,
            ],
        ),
        compiler_params=params("arbitrary", "arbitrary"),
        cost_estimate=pl.CostEstimate(
            flops=15 * 10**9, bytes_accessed=60 << 20, transcendentals=0
        ),
        name="weight_shares",
    )(own, *values)


def collect_kernel(plan, chunk, groups, kinds, own, arrived, normed, wq, wk, wv, *refs):
    before, middle_grad, x, gain = (None,) * 4
    if chunk > 0:
        before, refs = (refs[0], refs[1:])
    if chunk == CHUNKS - 1:
        (middle_grad, x, gain), refs = (refs[:3], refs[3:])
    total, bias_grad = refs[:2]
    outs, (held,) = (refs[2:-1], refs[-1:])
    image = pl.program_id(0)

    @pl.when(image == 0)
    def _():
        held[...] = jnp.zeros_like(held)
        bias_grad[...] = jnp.zeros_like(bias_grad)

    halves = []
    for half in range(2):
        lanes = [
            arrived[g, :, p * 128 + half * HDIM : p * 128 + (half + 1) * HDIM]
            for p in range(3)
            for g in range(GROUPS)
        ]
        halves.append(jnp.concatenate(lanes, axis=1))
    y = jnp.concatenate(halves, axis=0)
    held[...] += t_dot(normed[0], y)
    bias_grad[0:1, :D] += jnp.sum(y.astype(F32), axis=0, keepdims=True)
    whole = dot_t(y, jnp.concatenate([wq[...], wk[...], wv[...]], axis=1))
    if chunk > 0:
        whole = whole + before[0]
    if chunk == CHUNKS - 1:
        scaled, spread = norm_rows(x[0].astype(F32))
        total[0] = middle_grad[0] + norm_back(whole * gain[...], scaled, spread)
        bias_grad[0:1, D : 2 * D] += jnp.sum(whole * scaled, axis=0, keepdims=True)
        bias_grad[0:1, 2 * D :] += jnp.sum(whole, axis=0, keepdims=True)
    else:
        total[0] = whole

    @pl.when(image == pl.num_programs(0) - 1)
    def _():
        if len(outs) == 1:
            outs[0][...] = held[...].astype(BF)
            return
        piece = D // plan.wide
        part = piece // groups
        for k in range(groups):
            first = (own[0] + k) % groups * part
            for b in range(plan.wide):
                at = pl.ds(pl.multiple_of(first + b * piece, 8), part)
                outs[k][b] = held[at, :].astype(BF)


def collect(plan, chunk, groups, own, aligned, arrived, normed, weight, *extra):
    rows = pl.BlockSpec((1, 2 * plan.rows, D), lambda i, o: (i, 0, 0))
    columns = [pl.BlockSpec((D, 256), lambda i, o, p=p: (0, p * 3 + chunk)) for p in range(3)]
    last = chunk == CHUNKS - 1
    width = 3 * D if last else D
    fixed = lambda *dims: pl.BlockSpec(dims, lambda i, o: (0,) * len(dims))
    if aligned:
        blocks = [(plan.wide, D // plan.wide // groups, D)] * groups
    else:
        blocks = [(D, D)]
    more = [rows] * (chunk > 0) + ([rows, rows, fixed(1, D)] if last else [])
    total, sums, *outs = pl.pallas_call(
        partial(collect_kernel, plan, chunk, groups, None),
        out_shape=[shape((plan.images, 2 * plan.rows, D), F32), shape((8, width), F32)]
        + [shape(b, BF) for b in blocks],
        grid_spec=pltpu.PrefetchScalarGridSpec(
            num_scalar_prefetch=1,
            grid=(plan.images,),
            in_specs=[pl.BlockSpec((GROUPS, plan.rows, 384), lambda i, o: (i, 0, 0)), rows]
            + columns
            + more,
            out_specs=[rows, fixed(8, width)] + [fixed(*b) for b in blocks],
            scratch_shapes=[pltpu.VMEM((D, D), F32)],
        ),
        compiler_params=params(),
        cost_estimate=pl.CostEstimate(
            flops=8 * 10**9, bytes_accessed=20 << 20, transcendentals=0
        ),
        name="collect",
    )(own, arrived, normed, weight, weight, weight, *extra)
    return (total, sums[0], outs)


def tie(value, *others):
    return lax.optimization_barrier((value, *others))[0]


def exchange(blocks, axis="wide"):
    return lax.all_to_all(blocks, axis, split_axis=0, concat_axis=0, tiled=True)


def share_rows(grad, wide, groups):
    piece = grad.shape[0] // wide // groups
    return grad.astype(BF).reshape(wide, groups, piece, D).transpose(1, 0, 2, 3)


def over_groups(blocks):
    groups = len(blocks)
    got = [blocks[0]]
    for d in range(1, groups):
        pairs = [(i, (i + d) % groups) for i in range(groups)]
        got.append(lax.ppermute(blocks[d], "dp", pairs))
    return got


def turn_groups(low):
    groups = low.shape[0]
    own = lax.axis_index("dp")
    take = lambda i: lax.dynamic_index_in_dim(low, i, 0, keepdims=False)
    return [take((own + d) % groups) for d in range(groups)]


def add_groups(got):
    total = got[0].astype(F32)
    for x in got[1:]:
        total = total + x.astype(F32)
    return total


def add_wide(got):
    return jnp.sum(got.astype(F32), axis=0)


def shards(
    tokens, norm1_gain, norm1_shift, qkv_weight, qv_bias, rel_rows, rel_cols, out_weight, out_bias,
    norm2_gain, norm2_shift, fc1_weight, fc1_bias, fc2_weight, fc2_bias,
    window_place, image_extent, box_mask, out_grad,
):
    wide, groups = (lax.axis_size("wide"), lax.axis_size("dp"))
    me = lax.axis_index("wide").astype(jnp.int32).reshape(1)
    plan = Plan(wide, image_extent.shape[0])
    slots = tokens.shape[0]
    aligned = D // wide // groups % 8 == 0 and D // wide * 4 % 128 == 0
    wide_f = lambda v: v.astype(F32).reshape(1, -1)
    bias = jnp.concatenate([qv_bias[0], jnp.zeros((D,), BF), qv_bias[1]])
    blank = jnp.zeros((1, HDIM), BF)
    table = jnp.concatenate([rel_rows[::-1], blank, rel_cols[::-1], blank], 0)
    table_back = jnp.concatenate([rel_rows[::-1], blank, rel_cols, blank], 0)
    x, normed1, send = enter(
        plan, window_place, me, tokens,
        qkv_weight, wide_f(bias), wide_f(norm1_gain), wide_f(norm1_shift),
    )
    forward = []
    arrived = exchange(send)
    grad_out, *sends = follow(
        plan, window_place, me, out_grad, box_mask, normed1, qkv_weight, wide_f(bias)
    )
    sends = [send, *sends]
    for h in range(CHUNKS):
        if h + 1 < CHUNKS:
            following, arrived = lax.optimization_barrier((sends[h + 1], arrived))
            following = exchange(tie(following, forward[h - 1][2]) if h else following)
        else:
            first, arrived = lax.optimization_barrier((forward[1][0], arrived))
            first = exchange(first)
        earlier = (forward[0][0],) if h == 1 else ()
        forward.append(
            attention_forward(
                plan, slots, window_place, me, image_extent, arrived, table, *earlier,
                keep=h < CHUNKS - 1,
            )
        )
        arrived = following
    last, first = lax.optimization_barrier((forward[2][0], first))
    last = exchange(last)
    rows = plan.images * 2 * plan.rows
    (
        attended, normed2, act_low, grad_before, result, grad_middle, grad_branch,
        send_first, send_last, early,
    ) = middle_part(
        plan, first, last, x, grad_out, out_weight, fc1_weight, fc2_weight,
        wide_f(out_bias), wide_f(fc1_bias), wide_f(fc2_bias), wide_f(norm2_gain), wide_f(norm2_shift),
    )
    grad_middle = grad_middle.reshape(rows, D)
    early = early.reshape(-1)
    grad_arrived = exchange(send_first)
    own = lax.axis_index("dp").astype(jnp.int32).reshape(1)
    if aligned:
        shares = weight_shares(
            plan, groups, own, normed2, grad_before, grad_out, act_low, attended, grad_branch
        )
    else:
        normed2, act_low, attended, _ = lax.optimization_barrier(
            (normed2, act_low, attended, send_first)
        )
        flat = lambda v: v.reshape(rows, v.shape[-1])
        fc1_low = t_dot(flat(normed2), flat(grad_before)).astype(BF)
        fc1_low = fc1_low.reshape(D, groups, D).transpose(1, 0, 2)
        shares = turn_groups(
            jnp.concatenate(
                [
                    fc1_low.reshape(groups, wide, D // wide, D),
                    share_rows(t_dot(flat(act_low), flat(grad_out)), wide, groups),
                    share_rows(t_dot(flat(attended), flat(grad_branch)), wide, groups),
                ],
                axis=2,
            )
        )
    *shares, grad_arrived = lax.optimization_barrier((*shares, grad_arrived))
    shares = over_groups(shares)
    following = exchange(tie(send_last, grad_arrived))

    rel_total = None
    grad_qkv = []
    for h in range(CHUNKS):
        if h == 2:
            *shares, _ = lax.optimization_barrier((*shares, send))
            shares = add_groups(shares)
            grad_arrived, shares = lax.optimization_barrier((grad_arrived, shares))
        lane = max(h - 1, 0)
        if h < CHUNKS - 1:
            send, rel_grad = attention_replay(
                plan, slots, window_place, me, grad_arrived, lane, *forward[h][1:], table_back
            )
        else:
            send, rel_grad = attention_backward(
                plan, slots, window_place, me, image_extent, grad_arrived, lane,
                forward[h][1], forward[h][2], table, table_back,
            )
        if h == 0:
            send, grad_arrived = lax.optimization_barrier((send, following))
        rel_total = rel_grad if h == 0 else rel_total + rel_grad
        if h > 0:
            send = tie(send, grad_qkv[-1])
        grad_qkv.append(exchange(send))
        if h + 1 < CHUNKS and h > 0:
            grad_arrived = tie(grad_arrived, grad_qkv[-2])
    shares = lax.psum_scatter(shares.astype(BF), "wide", scatter_dimension=0, tiled=True)[0]
    shares = tie(shares, send)
    shares = lax.all_gather(shares, "dp", axis=0, tiled=False).astype(F32)
    result = tie(result, send)
    tokens_out = leave(
        plan, window_place, me, result.reshape(plan.images, 2 * plan.rows, D), slots, BF
    )
    mid = jnp.concatenate([early, rel_total.reshape(-1), jnp.zeros((512,), F32)]).reshape(-1, D)
    fold = lambda v: v.reshape(plan.images, 2 * plan.rows, D)
    around = lambda b: over_groups(b if aligned else turn_groups(share_rows(b[0], wide, groups)))
    gather = partial(collect, plan)
    fixed = (groups, own, aligned)
    totals, sums0, blocks = gather(0, *fixed, grad_qkv[0], normed1, qkv_weight)
    got0 = around(blocks)
    totals, sums1, blocks = gather(1, *fixed, grad_qkv[1], normed1, qkv_weight, totals)
    got1 = around(blocks)
    *got, _ = lax.optimization_barrier((*got0, *got1, tokens_out))
    ready = [add_groups(got[:groups]).astype(BF), add_groups(got[groups:]).astype(BF)]
    arrived, shares, *ready = lax.optimization_barrier((grad_qkv[2], shares, *ready))
    early_sums = exchange(jnp.concatenate(ready, axis=2))
    totals, sums2, blocks = gather(
        2, *fixed, arrived, normed1, qkv_weight, totals, fold(grad_middle), x, wide_f(norm1_gain)
    )
    weight_grad = add_groups(around(blocks)).astype(BF)
    third = [c[:D].reshape(3, 256) for c in (sums0, sums1, sums2)]
    late = jnp.concatenate([sums2[D:]] + [t[0] for t in third] + [t[2] for t in third])
    weight_grad, early_sums, late, totals, shares = lax.optimization_barrier(
        (weight_grad, early_sums, late, totals, shares)
    )
    last = exchange(weight_grad)
    small = jnp.concatenate([late.reshape(-1, D), mid], axis=0)
    small = jnp.sum(lax.all_gather(small, "wide", axis=0, tiled=False), axis=0)
    share = D // wide
    piece = share // groups
    weight_sums = jnp.concatenate([add_wide(early_sums), add_wide(last)], axis=1)
    last = jnp.concatenate([weight_sums.reshape(-1, D), small], axis=0)
    totals, shares, last = lax.optimization_barrier((totals, shares, last))
    last = lax.all_gather(last, "dp", axis=0, tiled=False)
    qkv_weight_grad = last[:, : 3 * piece].reshape(share, CHUNKS, 3, 256)
    qkv_weight_grad = qkv_weight_grad.transpose(0, 2, 1, 3).reshape(share, 3 * D)
    sums = jnp.sum(last[:, 3 * piece :], axis=0).reshape(-1)
    late, sums = (sums[: 4 * D], sums[4 * D :])
    tokens_grad = leave(plan, window_place, me, totals, slots, F32)
    rel_total = sums[8 * D : 8 * D + HDIM * 256].reshape(HDIM, 256).T
    small = sums[: 8 * D]
    fc2_share = shares[:, share : 2 * share]
    if aligned:
        fc2_share = fc2_share.reshape(groups, share, 2, 4 * share).transpose(3, 0, 2, 1)
    fc2_share = fc2_share.reshape(4 * share, D)
    return (
        tokens_out,
        tokens_grad,
        late[:D],
        late[D : 2 * D],
        qkv_weight_grad,
        late[2 * D :].reshape(2, D),
        rel_total[:127][::-1],
        rel_total[128:255],
        shares[:, 2 * share :].reshape(share, D),
        small[:D],
        small[D : 2 * D],
        small[2 * D : 3 * D],
        shares[:, :share].transpose(1, 0, 2).reshape(share, 4 * D),
        small[3 * D : 7 * D],
        fc2_share,
        small[7 * D :],
    )


def solution(mesh):
    tokens = P(("dp", "wide"), None, None)
    placed = (tokens,) + (P(),) * 14 + (P("dp"), P("dp", None), P(("dp", "wide"), None), tokens)
    shared = P("wide", None)
    return jax.shard_map(
        shards,
        mesh=mesh,
        in_specs=placed,
        out_specs=(
            tokens, tokens, P(), P(), shared, P(), P(), P(), shared, P(), P(), P(), shared, P(),
            shared, P(),
        ),
        check_vma=False,
    )
```

```python
from functools import partial

import jax
import jax.numpy as jnp
from jax import lax
from jax.experimental import pallas as pl
from jax.experimental.pallas import tpu as pltpu
from jax.sharding import PartitionSpec as P

F32 = jnp.float32
BF = jnp.bfloat16
D = 768
HEADS = 12
HDIM = 64
GRID = 64
N = GRID * GRID
WIN = 14
WGRID = 5
WINS = 25
WTOK = 196
HALF = 98
GROUPS = 4
CHUNKS = 3
EPS = 1e-06
NEG = -1e9
VMEM = 60 << 20
KEYS = 512
TILE = 1024


def dot(a, b):
    return jnp.dot(a, b, preferred_element_type=F32)


def dot_t(a, b):
    return lax.dot_general(a, b, (((1,), (1,)), ((), ())), preferred_element_type=F32)


def t_dot(a, b):
    return lax.dot_general(a, b, (((0,), (0,)), ((), ())), preferred_element_type=F32)


def shape(dims, kind):
    return jax.ShapeDtypeStruct(dims, kind)


def params(*semantics):
    return pltpu.CompilerParams(
        dimension_semantics=semantics or ("arbitrary",), vmem_limit_bytes=VMEM
    )


class Plan:
    def __init__(self, wide, images):
        self.wide, self.images = wide, images
        self.corner = WINS % wide == 1 and wide < WINS
        self.full = WINS // wide if self.corner else -(-WINS // wide)
        self.slots = self.full + int(self.corner)
        used = self.full * HALF + 32 * int(self.corner)
        self.rows = max(-(-used // 8) * 8, self.start(self.full - 1) + 112)
        self.tail = self.rows - self.start(self.full)
        self.corner_at = self.full * HALF

    def start(self, m):
        return m * HALF // 16 * 16

    def turn(self, places, slot_count, image):
        return (places[0] // slot_count + WINS * image) % self.wide

    def residue(self, places, slot_count, me, image):
        return (me + 2 * WINS * self.wide - self.turn(places, slot_count, image)) % self.wide

    def slot(self, places, slot_count, me, image, m):
        w = jnp.minimum(self.residue(places, slot_count, me, image) + self.wide * m, WINS - 1)
        return places[image * WINS + w] % slot_count


def norm_rows(values):
    centre = values - jnp.mean(values, axis=-1, keepdims=True)
    spread = lax.rsqrt(jnp.mean(centre * centre, axis=-1, keepdims=True) + EPS)
    return (centre * spread, spread)


def norm_back(weighted, scaled, spread):
    return spread * (
        weighted
        - jnp.mean(weighted, axis=-1, keepdims=True)
        - scaled * jnp.mean(weighted * scaled, axis=-1, keepdims=True)
    )


def place_rows(buffer, values, plan, m):
    if m < plan.full:
        for half in range(2):
            buffer[half, m * HALF : (m + 1) * HALF, :] = values[half * HALF : (half + 1) * HALF, :]
    else:
        for row in range(8):
            at = plan.corner_at + (row % 4) * 8
            buffer[row // 4, at : at + 8, :] = values[row * WIN : row * WIN + 8, :]


def cell_mask(plan, w, live):
    cell = lax.broadcasted_iota(jnp.int32, (WTOK, 1), 0)
    row_end = jnp.where(w // WGRID == WGRID - 1, 8, WIN)
    col_end = jnp.where(w % WGRID == WGRID - 1, 8, WIN)
    return ((cell // WIN < row_end) & (cell % WIN < col_end) & live).astype(F32)


def send_lanes(plan, normed, weights, bias, send):
    for part in range(3):
        at = part * 256
        made = dot(normed, weights[part][...]) + bias[part][...]
        top, low = (made[: plan.rows].astype(BF), made[plan.rows :].astype(BF))
        for g in range(GROUPS):
            own = slice(g * HDIM, (g + 1) * HDIM)
            both = jnp.concatenate([top[:, own], low[:, own]], axis=1)
            send[g, :, part * 128 : (part + 1) * 128] = both


def enter_kernel(plan, places, me, *refs):
    count = plan.slots
    tokens = refs[:count]
    weights, bias = (refs[count : count + 3], refs[count + 3 : count + 6])
    gain, shift, x_out, n_out, send, xbuf = refs[count + 6 :]

    @pl.when(pl.program_id(0) == 0)
    def _():
        xbuf[...] = jnp.zeros_like(xbuf)

    for m in range(count):
        place_rows(xbuf, tokens[m][0].astype(F32), plan, m)
    x = xbuf[...].reshape(2 * plan.rows, D)
    x_out[0] = x.astype(BF)
    scaled, _ = norm_rows(x)
    normed = (scaled * gain[...] + shift[...]).astype(BF)
    n_out[0] = normed
    send_lanes(plan, normed, weights, bias, send)


def follow_kernel(plan, places, me, *refs):
    count = plan.slots
    grads = refs[:count]
    box, normed = refs[count : count + 2]
    weights, bias = (refs[count + 2 : count + 8], refs[count + 8 : count + 14])
    g_out, *sends = refs[count + 14 : count + 17]
    gbuf, turned = refs[count + 17 :]
    image = pl.program_id(0)
    slot_count = box.shape[0]

    @pl.when(image == 0)
    def _():
        gbuf[...] = jnp.zeros_like(gbuf)
        turned[...] = box[...].astype(F32).T

    for h in range(2):
        own = slice(h * 3, h * 3 + 3)
        send_lanes(plan, normed[0], weights[own], bias[own], sends[h])
    residue = plan.residue(places, slot_count, me[0], image)
    for m in range(count):
        w = residue + plan.wide * m
        slot = plan.slot(places, slot_count, me[0], image, m)
        lane = lax.broadcasted_iota(jnp.int32, (WTOK, slot_count), 1)
        inside = jnp.sum(jnp.where(lane == slot, turned[...], 0.0), axis=1, keepdims=True)
        inside = inside * cell_mask(plan, w, w < WINS)
        place_rows(gbuf, grads[m][0].astype(F32) * inside, plan, m)
    g_out[0] = gbuf[...].reshape(2 * plan.rows, D).astype(BF)


def entry_specs(plan, slot_count):
    windows = [
        pl.BlockSpec((1, WTOK, D), lambda i, p, a, m=m: (plan.slot(p, slot_count, a[0], i, m), 0, 0))
        for m in range(plan.slots)
    ]
    column = lambda rows, h: [
        pl.BlockSpec((rows, 256), lambda i, p, a, b=part * CHUNKS + h: (0, b)) for part in range(3)
    ]
    rows = pl.BlockSpec((1, 2 * plan.rows, D), lambda i, p, a: (i, 0, 0))
    send = pl.BlockSpec((GROUPS, plan.rows, 384), lambda i, p, a: (i, 0, 0))
    return (windows, column, rows, send)


def enter(plan, places, me, tokens, weight, bias, gain, shift):
    windows, column, rows, send = entry_specs(plan, tokens.shape[0])
    fixed = pl.BlockSpec((1, D), lambda i, p, a: (0, 0))
    working = shape((plan.images, 2 * plan.rows, D), BF)
    return pl.pallas_call(
        partial(enter_kernel, plan),
        out_shape=[working, working, shape((plan.wide, plan.rows, 384), BF)],
        grid_spec=pltpu.PrefetchScalarGridSpec(
            num_scalar_prefetch=2,
            grid=(plan.images,),
            in_specs=windows + column(D, 0) + column(1, 0) + [fixed, fixed],
            out_specs=[rows, rows, send],
            scratch_shapes=[pltpu.VMEM((2, plan.rows, D), F32)],
        ),
        compiler_params=params(),
        cost_estimate=pl.CostEstimate(
            flops=2 * 10**9, bytes_accessed=10 << 20, transcendentals=0
        ),
        name="enter",
    )(places, me, *([tokens] * plan.slots), *([weight] * 3), *([bias] * 3), gain, shift)


def follow(plan, places, me, out_grad, box_mask, normed, weight, bias):
    slot_count = out_grad.shape[0]
    windows, column, rows, send = entry_specs(plan, slot_count)
    fixed = pl.BlockSpec(box_mask.shape, lambda i, p, a: (0, 0))
    block = shape((plan.wide, plan.rows, 384), BF)
    return pl.pallas_call(
        partial(follow_kernel, plan),
        out_shape=[shape((plan.images, 2 * plan.rows, D), BF), block, block],
        grid_spec=pltpu.PrefetchScalarGridSpec(
            num_scalar_prefetch=2,
            grid=(plan.images,),
            in_specs=windows
            + [fixed, rows]
            + column(D, 1)
            + column(D, 2)
            + column(1, 1)
            + column(1, 2),
            out_specs=[rows, send, send],
            scratch_shapes=[
                pltpu.VMEM((2, plan.rows, D), F32),
                pltpu.VMEM((WTOK, slot_count), F32),
            ],
        ),
        compiler_params=params(),
        cost_estimate=pl.CostEstimate(
            flops=4 * 10**9, bytes_accessed=16 << 20, transcendentals=0
        ),
        name="follow",
    )(places, me, *([out_grad] * plan.slots), box_mask, normed, *([weight] * 6), *([bias] * 6))


def leave_kernel(plan, places, me, values, out, held):
    slot = pl.program_id(0)
    slot_count = pl.num_programs(0)
    held[...] = jnp.zeros_like(held)
    for image in range(plan.images):
        residue = plan.residue(places, slot_count, me[0], image)
        for m in range(plan.slots):
            w = residue + plan.wide * m
            place = places[image * WINS + jnp.minimum(w, WINS - 1)]
            hit = (w < WINS) & (place == me[0] * slot_count + slot)

            @pl.when(hit)
            def _(image=image, m=m, w=w):
                if m < plan.full:
                    keep = cell_mask(plan, w, w < WINS)
                    for half in range(2):
                        at = half * plan.rows + m * HALF
                        part = slice(half * HALF, (half + 1) * HALF)
                        held[part, :] = values[image, at : at + HALF, :] * keep[part]
                else:
                    for row in range(8):
                        at = (row // 4) * plan.rows + plan.corner_at + (row % 4) * 8
                        held[row * WIN : row * WIN + 8, :] = values[image, at : at + 8, :]

    out[0] = held[...].astype(out.dtype)


def leave(plan, places, me, values, slot_count, kind):
    return pl.pallas_call(
        partial(leave_kernel, plan),
        out_shape=shape((slot_count, WTOK, D), kind),
        grid_spec=pltpu.PrefetchScalarGridSpec(
            num_scalar_prefetch=2,
            grid=(slot_count,),
            in_specs=[
                pl.BlockSpec(values.shape, lambda j, p, a: (0, 0, 0), pipeline_mode=pl.Buffered(1))
            ],
            out_specs=pl.BlockSpec((1, WTOK, D), lambda j, p, a: (j, 0, 0)),
            scratch_shapes=[pltpu.VMEM((WTOK, D), F32)],
        ),
        compiler_params=params(),
        cost_estimate=pl.CostEstimate(flops=1 << 20, bytes_accessed=12 << 20, transcendentals=0),
        name="leave",
    )(places, me, values)


def spread_matrix(plan, band, flip):
    dims = (560, 448) if flip else (448, 560)
    cell = lax.broadcasted_iota(jnp.int32, dims, 1 if flip else 0)
    item = lax.broadcasted_iota(jnp.int32, dims, 0 if flip else 1)
    row, col = (cell // GRID, cell % GRID)
    block = col // WIN
    shift = jnp.zeros(dims, jnp.int32)
    for c in range(WGRID):
        m = (band * WGRID + c) // plan.wide
        if m < plan.full:
            shift = jnp.where(block == c, m * HALF - plan.start(m), shift)
        else:
            shift = jnp.where(block == c, -10000, shift)
    return (item == block * 112 + shift + row * WIN + col % WIN).astype(F32).astype(BF)


def corner_matrix(plan, flip):
    dims = (plan.tail, 256) if flip else (256, plan.tail)
    cell = lax.broadcasted_iota(jnp.int32, dims, 1 if flip else 0)
    item = lax.broadcasted_iota(jnp.int32, dims, 0 if flip else 1)
    row, col = (cell // GRID, cell % GRID)
    at = plan.corner_at - plan.start(plan.full)
    hit = (col >= 4 * WIN) & (item == at + row * 8 + col - 4 * WIN)
    return hit.astype(F32).astype(BF)


def gather_grid(plan, turn, arrived, band):
    pieces = []
    for c in range(WGRID):
        w = band * WGRID + c
        m = w // plan.wide
        if m < plan.full:
            source = (w % plan.wide + turn) % plan.wide
            at = plan.start(m)
        else:
            source, at = (0, 0)
        pieces.append(arrived[source, at : at + 112, :])
    found = dot(spread_matrix(plan, band, False), jnp.concatenate(pieces, axis=0))
    return found


def grid_rows(plan, turn, arrived, parts, store):
    for band in range(WGRID):
        found = gather_grid(plan, turn, arrived, band)
        last = band == WGRID - 1
        if last and plan.corner:
            source = ((WINS - 1) % plan.wide + turn) % plan.wide
            at = plan.start(plan.full)
            extra = dot(corner_matrix(plan, False), arrived[source, at : at + plan.tail, :])
        for part in range(parts):
            top = found[:, part * 128 : part * 128 + HDIM]
            low = found[:, part * 128 + HDIM : (part + 1) * 128]
            if last:
                low = low[:GRID]
            whole = jnp.concatenate([top, low], axis=0)
            if last and plan.corner:
                more = jnp.concatenate(
                    [
                        extra[:, part * 128 : part * 128 + HDIM],
                        extra[:, part * 128 + HDIM : (part + 1) * 128],
                    ],
                    axis=0,
                )
                whole = whole + more
            store(part, band * WIN * GRID, whole)


def scatter_grid(plan, turn, out, parts, load, lane=0):
    span = slice(lane, lane + parts * 128)
    out[:, :, span] = jnp.zeros((plan.wide, plan.rows, parts * 128), BF)
    for band in range(WGRID):
        last = band == WGRID - 1
        base = band * WIN * GRID
        lanes = []
        for part in range(parts):
            top = load(part, base, 448)
            if last:
                low = load(part, base + 448, GRID)
                low = jnp.concatenate([low, jnp.zeros((448 - GRID, HDIM), BF)], axis=0)
            else:
                low = load(part, base + 448, 448)
            lanes += [top, low]
        made = dot(spread_matrix(plan, band, True), jnp.concatenate(lanes, axis=1)).astype(BF)
        for c in range(WGRID):
            w = band * WGRID + c
            m = w // plan.wide
            if m < plan.full:
                dest = (w % plan.wide + turn) % plan.wide
                at = plan.start(m)
                out[dest, at : at + 112, span] += made[c * 112 : (c + 1) * 112]
        if last and plan.corner:
            lanes = []
            for part in range(parts):
                lanes += [load(part, base, 256), load(part, base + 256, 256)]
            made = dot(corner_matrix(plan, True), jnp.concatenate(lanes, axis=1)).astype(BF)
            dest = ((WINS - 1) % plan.wide + turn) % plan.wide
            at = plan.start(plan.full)
            out[dest, at : at + plan.tail, span] += made


def split(x):
    high = x.astype(BF)
    return (high, (x - high.astype(F32)).astype(BF))


def key_marks():
    feature = lax.broadcasted_iota(jnp.int32, (192, N // 2), 0)
    key = lax.broadcasted_iota(jnp.int32, (192, N // 2), 1)
    col = (feature % GRID) == (key % GRID)
    row = ((feature - 128) % 32) == (key // GRID)
    return jnp.where(feature < 128, col.astype(F32), row.astype(F32)).astype(BF)


def rel_terms(q, table, extent_rows, extent_cols, first_row, count):
    both = dot_t(q, table)
    lane = lax.broadcasted_iota(jnp.int32, (GRID, 128), 1)
    row_mask = jnp.where(lane < extent_rows, 0.0, NEG)
    col_mask = jnp.where(lane < extent_cols, 0.0, NEG)
    rows, cols = ([], [])
    for i in range(count):
        part = both[i * GRID : (i + 1) * GRID]
        rows.append(pltpu.roll(part[:, :128], (first_row + i + 65) % 128, 1) + row_mask)
        cols.append(pltpu.roll(part[:, 128:], 65, 1, stride=1, stride_axis=0) + col_mask)
    return (jnp.concatenate(rows, 0)[:, :GRID], jnp.concatenate(cols, 0)[:, :GRID])


def query_marks(q, rows, cols):
    rh, rl = split(rows)
    ch, cl = split(cols)
    scaled = (q.astype(F32) * 0.125).astype(BF)
    return [
        jnp.concatenate([scaled, ch, cl, rh[:, i : i + 32], rl[:, i : i + 32]], 1) for i in (0, 32)
    ]


def forward_kernel(plan, tile, slot_count, keep, places, me, extent, arrived, table, *refs):
    refs, (kt, va, held) = (refs[:-3], refs[-3:])
    refs, probs = (refs[:-1], refs[-1]) if keep else (refs, None)
    earlier, (send, kept, saved) = (refs[:-3], refs[-3:])
    step = pl.program_id(0)
    image = me[0] // GROUPS
    turn = plan.turn(places, slot_count, image)

    @pl.when(step == 0)
    def _():
        marks = key_marks()
        kt[HDIM:, : N // 2] = marks
        kt[HDIM:, N // 2 :] = marks
        va[:, HDIM:] = (lax.broadcasted_iota(jnp.int32, (N, HDIM), 1) == 0).astype(F32).astype(BF)

        def store(part, first, values):
            kept[part, first : first + values.shape[0], :] = values.astype(BF)

        grid_rows(plan, turn, arrived, 3, store)
        kt[:HDIM, :] = kept[1].astype(F32).T.astype(BF)
        va[:, :HDIM] = kept[2]

    here = pl.ds(pl.multiple_of(step * tile, tile), tile)
    q = kept[0, here, :]
    count = tile // GRID
    rows, cols = rel_terms(q, table[...], extent[image, 0], extent[image, 1], step * count, count)
    marks = query_marks(q, rows, cols)
    side = N // 2
    score = lambda c: dot(marks[c * KEYS // side], kt[:, c * KEYS : (c + 1) * KEYS])
    total, top, now, tops = (None, None, score(0), [])
    for c in range(N // KEYS):
        following = score(c + 1) if c + 1 < N // KEYS else None
        higher = jnp.max(now, axis=1, keepdims=True)
        if c:
            higher = jnp.maximum(top, higher)
        weights = jnp.exp(now - higher).astype(BF)
        tops.append(higher)
        if keep:
            probs[:, c * KEYS : (c + 1) * KEYS] = weights
        x = dot(weights, va[c * KEYS : (c + 1) * KEYS, :])
        total = total * jnp.exp(top - higher) + x if c else x
        top, now = (higher, following)
    mass = total[:, HDIM : HDIM + 1]
    out = total * (1.0 / mass)
    lane = lax.broadcasted_iota(jnp.int32, (tile, 128), 1)
    level = top + jnp.log(mass)
    if keep:
        for c, higher in enumerate(tops):
            out = jnp.where(lane == HDIM + c, jnp.exp(higher - level), out)
        saved[...] = out
    else:
        saved[...] = jnp.where(lane < HDIM, out, level)
    held[here, :] = out[:, :HDIM].astype(BF)

    @pl.when(step == pl.num_programs(0) - 1)
    def _():
        load = lambda part, first, size: held[first : first + size, :]
        scatter_grid(plan, turn, send, 1, load, 128 * len(earlier))
        for i, block in enumerate(earlier):
            send[:, :, 128 * i : 128 * (i + 1)] = block[...]


def attention_forward(
    plan, slot_count, places, me, extent, arrived, table, *earlier, keep=False, tile=TILE
):
    lanes = 128 * (1 + len(earlier))
    whole = lambda *dims: pl.BlockSpec(dims, lambda t, *_: (0,) * len(dims))
    return pl.pallas_call(
        partial(forward_kernel, plan, tile, slot_count, keep),
        out_shape=(
            shape((plan.wide, plan.rows, lanes), BF),
            shape((3, N, HDIM), BF),
            shape((N, 128), F32),
        )
        + (shape((N, N), BF),) * keep,
        grid_spec=pltpu.PrefetchScalarGridSpec(
            num_scalar_prefetch=3,
            grid=(N // tile,),
            in_specs=[whole(*x.shape) for x in (arrived, table, *earlier)],
            out_specs=[
                whole(plan.wide, plan.rows, lanes),
                whole(3, N, HDIM),
                pl.BlockSpec((tile, 128), lambda t, *_: (t, 0)),
            ]
            + [pl.BlockSpec((tile, N), lambda t, *_: (t, 0))] * keep,
            scratch_shapes=[
                pltpu.VMEM((256, N), BF),
                pltpu.VMEM((N, 128), BF),
                pltpu.VMEM((N, HDIM), BF),
            ],
        ),
        compiler_params=params(),
        cost_estimate=pl.CostEstimate(
            flops=4 * N * N * 256, bytes_accessed=12 << 20, transcendentals=N * N
        ),
        name="attention_forward",
    )(places, me, extent, arrived, table, *earlier)


def backward_kernel(
    plan, tile, slot_count, places, me, extent,
    arrived, kept, saved, table, table_back,
    send, rel_grad,
    kt, vt, ka, dout, dq, dk, dv,
):
    step = pl.program_id(0)
    image = me[0] // GROUPS
    turn = plan.turn(places, slot_count, image)
    side = N // 2

    @pl.when(step == 0)
    def _():
        marks = key_marks()
        kt[HDIM:, :side] = marks
        kt[HDIM:, side:] = marks
        minus = lax.broadcasted_iota(jnp.int32, (HDIM, N), 0) < 2
        vt[HDIM:, :] = jnp.where(minus, -1.0, 0.0).astype(BF)
        key = lax.broadcasted_iota(jnp.int32, (N, 128), 0)
        mark = lax.broadcasted_iota(jnp.int32, (N, 128), 1)
        col = (GRID - 1 - mark) == key % GRID
        row = (mark - GRID) == key // GRID
        ka[:, HDIM:192] = jnp.where(mark < GRID, col.astype(F32), row.astype(F32)).astype(BF)
        ka[:, 192:] = jnp.zeros((N, HDIM), BF)
        rel_grad[...] = jnp.zeros_like(rel_grad)
        dk[...] = jnp.zeros_like(dk)
        dv[...] = jnp.zeros_like(dv)
        keys = kept[1].astype(F32)
        kt[:HDIM, :] = keys.T.astype(BF)
        ka[:, :HDIM] = (keys * 0.125).astype(BF)
        vt[:HDIM, :] = kept[2].astype(F32).T.astype(BF)

        def store(part, first, values):
            dout[first : first + values.shape[0], :] = values.astype(BF)

        grid_rows(plan, turn, arrived, 1, store)

    here = pl.ds(pl.multiple_of(step * tile, tile), tile)
    q = kept[0, here, :]
    do = dout[here, :]
    old = saved[...]
    count = tile // GRID
    inner = jnp.sum(do.astype(F32) * old[:, :HDIM], axis=1, keepdims=True)
    rows, cols = rel_terms(q, table[...], extent[image, 0], extent[image, 1], step * count, count)
    marks = query_marks(q, rows - old[:, HDIM : HDIM + 1], cols)
    high, low = split(inner)
    lane = lax.broadcasted_iota(jnp.int32, (tile, HDIM), 1)
    less = jnp.where(lane == 0, high.astype(F32), jnp.where(lane == 1, low.astype(F32), 0.0))
    do_less = jnp.concatenate([do, less.astype(BF)], 1)
    q_turned = (q.astype(F32) * 0.125).T.astype(BF)
    do_turned = do.astype(F32).T.astype(BF)
    def products(c):
        part = slice(c * KEYS, (c + 1) * KEYS)
        return (dot(marks[c * KEYS // side], kt[:, part]), dot(do_less, vt[:, part]))

    back, now = (None, products(0))
    for c in range(N // KEYS):
        part = slice(c * KEYS, (c + 1) * KEYS)
        following = products(c + 1) if c + 1 < N // KEYS else None
        weights = jnp.exp(now[0])
        dscore = (weights * now[1]).astype(BF)
        dv[:, part] += dot(do_turned, weights.astype(BF))
        dk[:, part] += dot(q_turned, dscore)
        x = dot(dscore, ka[part, :])
        back = x if back is None else back + x
        now = following
    blank = jnp.zeros((GRID, HDIM), F32)
    offsets = []
    for i in range(count):
        own = slice(i * GRID, (i + 1) * GRID)
        row_part = jnp.concatenate([back[own, 128:192], blank], 1)
        col_part = jnp.concatenate([back[own, HDIM:128], blank], 1)
        row_part = pltpu.roll(row_part, (2 * GRID - 1 + GRID - step * count - i) % 128, 1)
        col_part = pltpu.roll(col_part, 0, 1, stride=1, stride_axis=0)
        offsets.append(jnp.concatenate([row_part, col_part], 1))
    high, low = split(jnp.concatenate(offsets, 0))
    rel = table_back[...]
    both = dot(jnp.concatenate([high, low], 1), jnp.concatenate([rel, rel], 0))
    dq[here, :] = (back[:, :HDIM] + both).astype(BF)
    q_whole = q.astype(F32).T.astype(BF)
    rel_grad[...] += dot(q_whole, high) + dot(q_whole, low)

    @pl.when(step == pl.num_programs(0) - 1)
    def _():
        def load(part, first, size):
            if part == 0:
                return dq[first : first + size, :]
            return turned[part - 1][first : first + size, :]

        turned = (dk[...].T.astype(BF), dv[...].T.astype(BF))
        scatter_grid(plan, turn, send, 3, load)


def attention_backward(
    plan, slot_count, places, me, extent, arrived, lane, kept, saved, table, table_back, tile=TILE
):
    whole = lambda *dims: pl.BlockSpec(dims, lambda t, *_: (0,) * len(dims))
    return pl.pallas_call(
        partial(backward_kernel, plan, tile, slot_count),
        out_shape=(shape((plan.wide, plan.rows, 384), BF), shape((HDIM, 256), F32)),
        grid_spec=pltpu.PrefetchScalarGridSpec(
            num_scalar_prefetch=3,
            grid=(N // tile,),
            in_specs=[
                pl.BlockSpec((plan.wide, plan.rows, 128), lambda t, *_: (0, 0, lane)),
                whole(3, N, HDIM),
                pl.BlockSpec((tile, 128), lambda t, *_: (t, 0)),
                whole(*table.shape),
                whole(*table_back.shape),
            ],
            out_specs=[whole(plan.wide, plan.rows, 384), whole(HDIM, 256)],
            scratch_shapes=[
                pltpu.VMEM((256, N), BF),
                pltpu.VMEM((128, N), BF),
                pltpu.VMEM((N, 256), BF),
                pltpu.VMEM((N, HDIM), BF),
                pltpu.VMEM((N, HDIM), BF),
                pltpu.VMEM((HDIM, N), F32),
                pltpu.VMEM((HDIM, N), F32),
            ],
        ),
        compiler_params=params(),
        cost_estimate=pl.CostEstimate(
            flops=10 * N * N * 256, bytes_accessed=12 << 20, transcendentals=N * N
        ),
        name="attention_backward",
    )(places, me, extent, arrived, kept, saved, table, table_back)


def replay_kernel(
    plan, tile, slot_count, places, me,
    arrived, kept, saved, probs, table_back,
    send, rel_grad,
    vt, ka, dout, dq, dk, dv,
):
    step = pl.program_id(0)
    image = me[0] // GROUPS
    turn = plan.turn(places, slot_count, image)

    @pl.when(step == 0)
    def _():
        minus = lax.broadcasted_iota(jnp.int32, (HDIM, N), 0) < 2
        vt[HDIM:, :] = jnp.where(minus, -1.0, 0.0).astype(BF)
        key = lax.broadcasted_iota(jnp.int32, (N, 128), 0)
        mark = lax.broadcasted_iota(jnp.int32, (N, 128), 1)
        col = (GRID - 1 - mark) == key % GRID
        row = (mark - GRID) == key // GRID
        ka[:, HDIM:192] = jnp.where(mark < GRID, col.astype(F32), row.astype(F32)).astype(BF)
        ka[:, 192:] = jnp.zeros((N, HDIM), BF)
        rel_grad[...] = jnp.zeros_like(rel_grad)
        dk[...] = jnp.zeros_like(dk)
        dv[...] = jnp.zeros_like(dv)
        ka[:, :HDIM] = (kept[1].astype(F32) * 0.125).astype(BF)
        vt[:HDIM, :] = kept[2].astype(F32).T.astype(BF)

        def store(part, first, values):
            dout[first : first + values.shape[0], :] = values.astype(BF)

        grid_rows(plan, turn, arrived, 1, store)

    here = pl.ds(pl.multiple_of(step * tile, tile), tile)
    q = kept[0, here, :]
    do = dout[here, :].astype(F32)
    old = saved[...]
    count = tile // GRID
    inner = jnp.sum(do * old[:, :HDIM], axis=1, keepdims=True)
    lane = lax.broadcasted_iota(jnp.int32, (tile, HDIM), 1)
    q_turned = (q.astype(F32) * 0.125).T.astype(BF)
    do_turned = do.T
    factors = old[:, HDIM:].T

    def products(c):
        part = slice(c * KEYS, (c + 1) * KEYS)
        factor = old[:, HDIM + c : HDIM + c + 1]
        high, low = split(inner * factor)
        less = jnp.where(lane == 0, high.astype(F32), jnp.where(lane == 1, low.astype(F32), 0.0))
        do_less = jnp.concatenate([(do * factor).astype(BF), less.astype(BF)], 1)
        return dot(do_less, vt[:, part])

    back, now = (None, products(0))
    for c in range(N // KEYS):
        part = slice(c * KEYS, (c + 1) * KEYS)
        following = products(c + 1) if c + 1 < N // KEYS else None
        weights = probs[:, part]
        dscore = (weights.astype(F32) * now).astype(BF)
        dv[:, part] += dot((do_turned * factors[c : c + 1, :]).astype(BF), weights)
        dk[:, part] += dot(q_turned, dscore)
        x = dot(dscore, ka[part, :])
        back = x if back is None else back + x
        now = following
    blank = jnp.zeros((GRID, HDIM), F32)
    offsets = []
    for i in range(count):
        own = slice(i * GRID, (i + 1) * GRID)
        row_part = jnp.concatenate([back[own, 128:192], blank], 1)
        col_part = jnp.concatenate([back[own, HDIM:128], blank], 1)
        row_part = pltpu.roll(row_part, (2 * GRID - 1 + GRID - step * count - i) % 128, 1)
        col_part = pltpu.roll(col_part, 0, 1, stride=1, stride_axis=0)
        offsets.append(jnp.concatenate([row_part, col_part], 1))
    high, low = split(jnp.concatenate(offsets, 0))
    rel = table_back[...]
    both = dot(jnp.concatenate([high, low], 1), jnp.concatenate([rel, rel], 0))
    dq[here, :] = (back[:, :HDIM] + both).astype(BF)
    q_whole = q.astype(F32).T.astype(BF)
    rel_grad[...] += dot(q_whole, high) + dot(q_whole, low)

    @pl.when(step == pl.num_programs(0) - 1)
    def _():
        def load(part, first, size):
            if part == 0:
                return dq[first : first + size, :]
            return turned[part - 1][first : first + size, :]

        turned = (dk[...].T.astype(BF), dv[...].T.astype(BF))
        scatter_grid(plan, turn, send, 3, load)


def attention_replay(
    plan, slot_count, places, me, arrived, lane, kept, saved, probs, table_back, tile=TILE
):
    whole = lambda *dims: pl.BlockSpec(dims, lambda t, *_: (0,) * len(dims))
    return pl.pallas_call(
        partial(replay_kernel, plan, tile, slot_count),
        out_shape=(shape((plan.wide, plan.rows, 384), BF), shape((HDIM, 256), F32)),
        grid_spec=pltpu.PrefetchScalarGridSpec(
            num_scalar_prefetch=2,
            grid=(N // tile,),
            in_specs=[
                pl.BlockSpec((plan.wide, plan.rows, 128), lambda t, *_: (0, 0, lane)),
                whole(3, N, HDIM),
                pl.BlockSpec((tile, 128), lambda t, *_: (t, 0)),
                pl.BlockSpec((tile, N), lambda t, *_: (t, 0)),
                whole(*table_back.shape),
            ],
            out_specs=[whole(plan.wide, plan.rows, 384), whole(HDIM, 256)],
            scratch_shapes=[
                pltpu.VMEM((128, N), BF),
                pltpu.VMEM((N, 256), BF),
                pltpu.VMEM((N, HDIM), BF),
                pltpu.VMEM((N, HDIM), BF),
                pltpu.VMEM((HDIM, N), F32),
                pltpu.VMEM((HDIM, N), F32),
            ],
        ),
        compiler_params=params(),
        cost_estimate=pl.CostEstimate(
            flops=10 * N * N * 256, bytes_accessed=44 << 20, transcendentals=0
        ),
        name="attention_replay",
    )(places, me, arrived, kept, saved, probs, table_back)


def middle_kernel(
    plan, first, last, x, g, out_weight, fc1_weight, fc2_weight,
    out_bias, fc1_bias, fc2_bias, gain, shift,
    attended, normed, act, grad_before, result, grad_middle, grad_branch, send_first, send_last, sums,
    grads,
):
    step = pl.program_id(0)
    half = step % 2
    blocks = [first.at[:, :, :128], first.at[:, :, 128:], last]
    for side in range(2):

        @pl.when(half == side)
        def _(side=side):
            lanes = [
                blocks[h][k, :, side * HDIM : (side + 1) * HDIM]
                for h in range(CHUNKS)
                for k in range(GROUPS)
            ]
            attended[0] = jnp.concatenate(lanes, axis=1)

    @pl.when(step == 0)
    def _():
        sums[...] = jnp.zeros_like(sums)

    middle = x[0].astype(F32) + (dot(attended[0], out_weight[...]) + out_bias[...])
    scaled, spread = norm_rows(middle)
    n = (scaled * gain[...] + shift[...]).astype(BF)
    normed[0] = n
    grad = g[0]
    total, grad_normed = (None, None)
    add = lambda old, new: new if old is None else old + new

    def products(c):
        span = slice(c * D, (c + 1) * D)
        return (dot(n, fc1_weight[:, span]), dot_t(grad, fc2_weight[span, :]))

    now = products(0)
    for c in range(4):
        span = slice(c * D, (c + 1) * D)
        following = products(c + 1) if c < 3 else None
        before = now[0] + fc1_bias[:, span]
        share = 0.5 + 0.5 * lax.erf(before * (0.5**0.5))
        low = (before * share).astype(BF)
        act[0, :, span] = low
        slope = share + before * (jnp.exp(before * before * -0.5) * 0.3989422804014327)
        back = (now[1] * slope).astype(BF)
        grad_before[0, :, span] = back
        sums[:, (3 + c) * D : (4 + c) * D] += jnp.sum(back.astype(F32), axis=0, keepdims=True)
        total = add(total, dot(low, fc2_weight[span, :]))
        grad_normed = add(grad_normed, dot_t(back, fc1_weight[:, span]))
        now = following
    result[0] = middle + total + fc2_bias[...]
    full = grad.astype(F32) + norm_back(grad_normed * gain[...], scaled, spread)
    grad_middle[0] = full
    branch = full.astype(BF)
    grad_branch[0] = branch
    for place, value in (
        (0, branch.astype(F32)), (1, grad_normed * scaled), (2, grad_normed), (7, grad.astype(F32))
    ):
        sums[:, place * D : (place + 1) * D] += jnp.sum(value, axis=0, keepdims=True)
    grads[...] = dot_t(branch, out_weight[...]).astype(BF)
    targets = [send_first, send_last.at[:, :, :128], send_last.at[:, :, 128:]]
    for side in range(2):

        @pl.when(half == side)
        def _(side=side):
            for h in range(CHUNKS):
                for k in range(GROUPS):
                    at = (h * GROUPS + k) * HDIM
                    made = grads[:, at : at + HDIM]
                    targets[h][k, :, side * HDIM : (side + 1) * HDIM] = made


def middle_part(plan, first, last, x, g, out_weight, fc1_weight, fc2_weight, *vectors):
    rows, hidden = (plan.rows, fc1_weight.shape[1])
    halves = 2 * plan.images
    x, g = (v.reshape(halves, rows, D) for v in (x, g))
    row = lambda width: pl.BlockSpec((1, rows, width), lambda i: (i, 0, 0))
    whole = lambda v: pl.BlockSpec(v.shape, lambda i: (0, 0), pipeline_mode=pl.Buffered(1))
    block = lambda lanes: pl.BlockSpec((GROUPS, rows, lanes), lambda i: (i // 2, 0, 0))
    made = lambda width, kind: shape((halves, rows, width), kind)
    fixed = (out_weight, fc1_weight, fc2_weight, *vectors)
    return pl.pallas_call(
        partial(middle_kernel, plan),
        out_shape=(
            made(D, BF), made(D, BF), made(hidden, BF), made(hidden, BF),
            made(D, F32), made(D, F32), made(D, BF),
            shape((plan.wide, rows, 128), BF), shape((plan.wide, rows, 256), BF),
            shape((1, 8 * D), F32),
        ),
        grid=(halves,),
        in_specs=[block(256), block(128), row(D), row(D)] + [whole(v) for v in fixed],
        out_specs=(
            row(D), row(D), row(hidden), row(hidden), row(D), row(D), row(D),
            block(128), block(256), pl.BlockSpec((1, 8 * D), lambda i: (0, 0)),
        ),
        scratch_shapes=[pltpu.VMEM((rows, D), BF)],
        compiler_params=params(),
        cost_estimate=pl.CostEstimate(
            flops=30 * 10**9, bytes_accessed=40 << 20, transcendentals=8 << 20
        ),
        name="middle",
    )(first, last, x, g, *fixed)


def shares_kernel(
    plan, groups, own, normed, grad_before, g, act, attended, branch,
    o0, o1, o2, o3, fc1, fc2, out, ready, turned_n, turned_g, sem,
):
    step, image = (pl.program_id(0), pl.program_id(1))
    finished = image == pl.num_programs(1) - 1
    outs = (o0, o1, o2, o3)
    d = (own[0] + step) % groups
    piece = D // plan.wide
    part = piece // groups
    width = D // groups

    @pl.when(image == 0)
    def _():
        fc1[...] = jnp.zeros_like(fc1)
        fc2[...] = jnp.zeros_like(fc2)

    @pl.when((image == 0) & (step == 0))
    def _():
        out[...] = jnp.zeros_like(out)

    @pl.when(step == 0)
    def _():
        turned_n[image] = normed[0].astype(F32).T.astype(BF)
        turned_g[image] = g[0].astype(F32).T.astype(BF)
        out[...] += t_dot(attended[0], branch[0])

    fc1[...] += dot(turned_n[image], grad_before[0])
    for k in range(groups):

        @pl.when(d == k)
        def _(k=k):
            fc2[...] += dot(turned_g[image, k * width : (k + 1) * width, :], act[0])

    for k in range(groups):

        @pl.when(finished & (step == k))
        def _(k=k):
            if k:
                pltpu.make_async_copy(ready, outs[k - 1], sem).wait()
            for b in range(plan.wide):
                ready[b, :piece, :] = fc1[b * piece : (b + 1) * piece, :].astype(BF)
                cols = slice(b * 4 * piece, (b + 1) * 4 * piece)
                for side in range(2):
                    lanes = slice(side * 4 * piece, (side + 1) * 4 * piece)
                    upper = fc2[side * piece : (side + 1) * piece, cols]
                    ready[b, piece : 2 * piece, lanes] = upper.astype(BF)
                at = pl.ds(pl.multiple_of(b * piece + d * part, 8), part)
                ready[b, 2 * piece :, :] = out[at, :].astype(BF)
            copy = pltpu.make_async_copy(ready, outs[k], sem)
            copy.start()
            if k == groups - 1:
                copy.wait()


def weight_shares(plan, groups, own, normed, grad_before, g, act, attended, branch):
    rows = 2 * plan.rows
    fold = lambda v: v.reshape(plan.images, rows, v.shape[-1])
    values = [fold(v) for v in (normed, grad_before, g, act, attended, branch)]
    once = pl.BlockSpec((1, rows, D), lambda s, i, o: (jnp.where(s == 0, i, plan.images - 1), 0, 0))
    wide = pl.BlockSpec((1, rows, values[3].shape[-1]), lambda s, i, o: (i, 0, 0))
    column = pl.BlockSpec((1, rows, D), lambda s, i, o: (i, 0, (o[0] + s) % groups))
    block = (plan.wide, 2 * D // plan.wide + D // plan.wide // groups, D)
    return pl.pallas_call(
        partial(shares_kernel, plan, groups),
        out_shape=[shape(block, BF)] * groups,
        grid_spec=pltpu.PrefetchScalarGridSpec(
            num_scalar_prefetch=1,
            grid=(groups, plan.images),
            in_specs=[once, column, once, wide, once, once],
            out_specs=[pl.BlockSpec(memory_space=pl.ANY)] * groups,
            scratch_shapes=[
                pltpu.VMEM((D, D), F32),
                pltpu.VMEM((D // groups, 4 * D), F32),
                pltpu.VMEM((D, D), F32),
                pltpu.VMEM(block, BF),
                pltpu.VMEM((plan.images, D, rows), BF),
                pltpu.VMEM((plan.images, D, rows), BF),
                pltpu.SemaphoreType.DMA,
            ],
        ),
        compiler_params=params("arbitrary", "arbitrary"),
        cost_estimate=pl.CostEstimate(
            flops=15 * 10**9, bytes_accessed=60 << 20, transcendentals=0
        ),
        name="weight_shares",
    )(own, *values)


def collect_kernel(plan, chunk, groups, kinds, own, arrived, normed, wq, wk, wv, *refs):
    before, middle_grad, x, gain = (None,) * 4
    if chunk > 0:
        before, refs = (refs[0], refs[1:])
    if chunk == CHUNKS - 1:
        (middle_grad, x, gain), refs = (refs[:3], refs[3:])
    total, bias_grad = refs[:2]
    outs, (held,) = (refs[2:-1], refs[-1:])
    image = pl.program_id(0)

    @pl.when(image == 0)
    def _():
        held[...] = jnp.zeros_like(held)
        bias_grad[...] = jnp.zeros_like(bias_grad)

    halves = []
    for half in range(2):
        lanes = [
            arrived[g, :, p * 128 + half * HDIM : p * 128 + (half + 1) * HDIM]
            for p in range(3)
            for g in range(GROUPS)
        ]
        halves.append(jnp.concatenate(lanes, axis=1))
    y = jnp.concatenate(halves, axis=0)
    held[...] += t_dot(normed[0], y)
    bias_grad[0:1, :D] += jnp.sum(y.astype(F32), axis=0, keepdims=True)
    whole = dot_t(y, jnp.concatenate([wq[...], wk[...], wv[...]], axis=1))
    if chunk > 0:
        whole = whole + before[0]
    if chunk == CHUNKS - 1:
        scaled, spread = norm_rows(x[0].astype(F32))
        total[0] = middle_grad[0] + norm_back(whole * gain[...], scaled, spread)
        bias_grad[0:1, D : 2 * D] += jnp.sum(whole * scaled, axis=0, keepdims=True)
        bias_grad[0:1, 2 * D :] += jnp.sum(whole, axis=0, keepdims=True)
    else:
        total[0] = whole

    @pl.when(image == pl.num_programs(0) - 1)
    def _():
        if len(outs) == 1:
            outs[0][...] = held[...].astype(BF)
            return
        piece = D // plan.wide
        part = piece // groups
        for k in range(groups):
            first = (own[0] + k) % groups * part
            for b in range(plan.wide):
                at = pl.ds(pl.multiple_of(first + b * piece, 8), part)
                outs[k][b] = held[at, :].astype(BF)


def collect(plan, chunk, groups, own, aligned, arrived, normed, weight, *extra):
    rows = pl.BlockSpec((1, 2 * plan.rows, D), lambda i, o: (i, 0, 0))
    columns = [pl.BlockSpec((D, 256), lambda i, o, p=p: (0, p * 3 + chunk)) for p in range(3)]
    last = chunk == CHUNKS - 1
    width = 3 * D if last else D
    fixed = lambda *dims: pl.BlockSpec(dims, lambda i, o: (0,) * len(dims))
    if aligned:
        blocks = [(plan.wide, D // plan.wide // groups, D)] * groups
    else:
        blocks = [(D, D)]
    more = [rows] * (chunk > 0) + ([rows, rows, fixed(1, D)] if last else [])
    total, sums, *outs = pl.pallas_call(
        partial(collect_kernel, plan, chunk, groups, None),
        out_shape=[shape((plan.images, 2 * plan.rows, D), F32), shape((8, width), F32)]
        + [shape(b, BF) for b in blocks],
        grid_spec=pltpu.PrefetchScalarGridSpec(
            num_scalar_prefetch=1,
            grid=(plan.images,),
            in_specs=[pl.BlockSpec((GROUPS, plan.rows, 384), lambda i, o: (i, 0, 0)), rows]
            + columns
            + more,
            out_specs=[rows, fixed(8, width)] + [fixed(*b) for b in blocks],
            scratch_shapes=[pltpu.VMEM((D, D), F32)],
        ),
        compiler_params=params(),
        cost_estimate=pl.CostEstimate(
            flops=8 * 10**9, bytes_accessed=20 << 20, transcendentals=0
        ),
        name="collect",
    )(own, arrived, normed, weight, weight, weight, *extra)
    return (total, sums[0], outs)


def tie(value, *others):
    return lax.optimization_barrier((value, *others))[0]


def exchange(blocks, axis="wide"):
    return lax.all_to_all(blocks, axis, split_axis=0, concat_axis=0, tiled=True)


def share_rows(grad, wide, groups):
    piece = grad.shape[0] // wide // groups
    return grad.astype(BF).reshape(wide, groups, piece, D).transpose(1, 0, 2, 3)


def over_groups(blocks):
    groups = len(blocks)
    got = [blocks[0]]
    for d in range(1, groups):
        pairs = [(i, (i + d) % groups) for i in range(groups)]
        got.append(lax.ppermute(blocks[d], "dp", pairs))
    return got


def turn_groups(low):
    groups = low.shape[0]
    own = lax.axis_index("dp")
    take = lambda i: lax.dynamic_index_in_dim(low, i, 0, keepdims=False)
    return [take((own + d) % groups) for d in range(groups)]


def add_groups(got):
    total = got[0].astype(F32)
    for x in got[1:]:
        total = total + x.astype(F32)
    return total


def add_wide(got):
    return jnp.sum(got.astype(F32), axis=0)


def shards(
    tokens, norm1_gain, norm1_shift, qkv_weight, qv_bias, rel_rows, rel_cols, out_weight, out_bias,
    norm2_gain, norm2_shift, fc1_weight, fc1_bias, fc2_weight, fc2_bias,
    window_place, image_extent, box_mask, out_grad,
):
    wide, groups = (lax.axis_size("wide"), lax.axis_size("dp"))
    me = lax.axis_index("wide").astype(jnp.int32).reshape(1)
    plan = Plan(wide, image_extent.shape[0])
    slots = tokens.shape[0]
    aligned = D // wide // groups % 8 == 0 and D // wide * 4 % 128 == 0
    wide_f = lambda v: v.astype(F32).reshape(1, -1)
    bias = jnp.concatenate([qv_bias[0], jnp.zeros((D,), BF), qv_bias[1]])
    blank = jnp.zeros((1, HDIM), BF)
    table = jnp.concatenate([rel_rows[::-1], blank, rel_cols[::-1], blank], 0)
    table_back = jnp.concatenate([rel_rows[::-1], blank, rel_cols, blank], 0)
    x, normed1, send = enter(
        plan, window_place, me, tokens,
        qkv_weight, wide_f(bias), wide_f(norm1_gain), wide_f(norm1_shift),
    )
    forward = []
    arrived = exchange(send)
    grad_out, *sends = follow(
        plan, window_place, me, out_grad, box_mask, normed1, qkv_weight, wide_f(bias)
    )
    sends = [send, *sends]
    for h in range(CHUNKS):
        if h + 1 < CHUNKS:
            following, arrived = lax.optimization_barrier((sends[h + 1], arrived))
            following = exchange(tie(following, forward[h - 1][2]) if h else following)
        else:
            first, arrived = lax.optimization_barrier((forward[1][0], arrived))
            first = exchange(first)
        earlier = (forward[0][0],) if h == 1 else ()
        forward.append(
            attention_forward(
                plan, slots, window_place, me, image_extent, arrived, table, *earlier,
                keep=h < CHUNKS - 1,
            )
        )
        arrived = following
    last, first = lax.optimization_barrier((forward[2][0], first))
    last = exchange(last)
    rows = plan.images * 2 * plan.rows
    (
        attended, normed2, act_low, grad_before, result, grad_middle, grad_branch,
        send_first, send_last, early,
    ) = middle_part(
        plan, first, last, x, grad_out, out_weight, fc1_weight, fc2_weight,
        wide_f(out_bias), wide_f(fc1_bias), wide_f(fc2_bias), wide_f(norm2_gain), wide_f(norm2_shift),
    )
    grad_middle = grad_middle.reshape(rows, D)
    early = early.reshape(-1)
    grad_arrived = exchange(send_first)
    own = lax.axis_index("dp").astype(jnp.int32).reshape(1)
    if aligned:
        shares = weight_shares(
            plan, groups, own, normed2, grad_before, grad_out, act_low, attended, grad_branch
        )
    else:
        normed2, act_low, attended, _ = lax.optimization_barrier(
            (normed2, act_low, attended, send_first)
        )
        flat = lambda v: v.reshape(rows, v.shape[-1])
        fc1_low = t_dot(flat(normed2), flat(grad_before)).astype(BF)
        fc1_low = fc1_low.reshape(D, groups, D).transpose(1, 0, 2)
        shares = turn_groups(
            jnp.concatenate(
                [
                    fc1_low.reshape(groups, wide, D // wide, D),
                    share_rows(t_dot(flat(act_low), flat(grad_out)), wide, groups),
                    share_rows(t_dot(flat(attended), flat(grad_branch)), wide, groups),
                ],
                axis=2,
            )
        )
    *shares, grad_arrived = lax.optimization_barrier((*shares, grad_arrived))
    shares = over_groups(shares)
    following = exchange(tie(send_last, grad_arrived))

    rel_total = None
    grad_qkv = []
    for h in range(CHUNKS):
        if h == 2:
            *shares, _ = lax.optimization_barrier((*shares, send))
            shares = add_groups(shares)
            grad_arrived, shares = lax.optimization_barrier((grad_arrived, shares))
        lane = max(h - 1, 0)
        if h < CHUNKS - 1:
            send, rel_grad = attention_replay(
                plan, slots, window_place, me, grad_arrived, lane, *forward[h][1:], table_back
            )
        else:
            send, rel_grad = attention_backward(
                plan, slots, window_place, me, image_extent, grad_arrived, lane,
                forward[h][1], forward[h][2], table, table_back,
            )
        if h == 0:
            send, grad_arrived = lax.optimization_barrier((send, following))
        rel_total = rel_grad if h == 0 else rel_total + rel_grad
        if h > 0:
            send = tie(send, grad_qkv[-1])
        grad_qkv.append(exchange(send))
        if h + 1 < CHUNKS and h > 0:
            grad_arrived = tie(grad_arrived, grad_qkv[-2])
    shares = lax.psum_scatter(shares.astype(BF), "wide", scatter_dimension=0, tiled=True)[0]
    shares = tie(shares, send)
    shares = lax.all_gather(shares, "dp", axis=0, tiled=False).astype(F32)
    result = tie(result, send)
    tokens_out = leave(
        plan, window_place, me, result.reshape(plan.images, 2 * plan.rows, D), slots, BF
    )
    mid = jnp.concatenate([early, rel_total.reshape(-1), jnp.zeros((512,), F32)]).reshape(-1, D)
    fold = lambda v: v.reshape(plan.images, 2 * plan.rows, D)
    around = lambda b: over_groups(b if aligned else turn_groups(share_rows(b[0], wide, groups)))
    gather = partial(collect, plan)
    fixed = (groups, own, aligned)
    totals, sums0, blocks = gather(0, *fixed, grad_qkv[0], normed1, qkv_weight)
    got0 = around(blocks)
    totals, sums1, blocks = gather(1, *fixed, grad_qkv[1], normed1, qkv_weight, totals)
    got1 = around(blocks)
    *got, _ = lax.optimization_barrier((*got0, *got1, tokens_out))
    ready = [add_groups(got[:groups]).astype(BF), add_groups(got[groups:]).astype(BF)]
    arrived, shares, *ready = lax.optimization_barrier((grad_qkv[2], shares, *ready))
    early_sums = exchange(jnp.concatenate(ready, axis=2))
    totals, sums2, blocks = gather(
        2, *fixed, arrived, normed1, qkv_weight, totals, fold(grad_middle), x, wide_f(norm1_gain)
    )
    got2 = around(blocks)
    share = D // wide
    piece = share // groups
    tokens_grad = leave(plan, window_place, me, totals, slots, F32)
    fc1_share = shares[:, :share].transpose(1, 0, 2).reshape(share, 4 * D)
    fc2_share = shares[:, share : 2 * share]
    if aligned:
        fc2_share = fc2_share.reshape(groups, share, 2, 4 * share).transpose(3, 0, 2, 1)
    fc2_share = fc2_share.reshape(4 * share, D)
    out_share = shares[:, 2 * share :].reshape(share, D)
    third = [c[:D].reshape(3, 256) for c in (sums0, sums1, sums2)]
    late = jnp.concatenate([sums2[D:]] + [t[0] for t in third] + [t[2] for t in third])
    small = jnp.concatenate([late.reshape(-1, D), mid], axis=0)
    *got2, tokens_grad, fc1_share, fc2_share, out_share, small = lax.optimization_barrier(
        (*got2, tokens_grad, fc1_share, fc2_share, out_share, small)
    )
    weight_grad = add_groups(got2).astype(BF)
    weight_grad, early_sums, small = lax.optimization_barrier((weight_grad, early_sums, small))
    last = exchange(weight_grad)
    small = jnp.sum(lax.all_gather(small, "wide", axis=0, tiled=False), axis=0)
    small = jnp.sum(lax.all_gather(small, "dp", axis=0, tiled=False), axis=0).reshape(-1)
    weight_sums = jnp.concatenate([add_wide(early_sums), add_wide(last)], axis=1)
    last = lax.all_gather(weight_sums, "dp", axis=0, tiled=True)
    qkv_weight_grad = last.reshape(share, CHUNKS, 3, 256)
    qkv_weight_grad = qkv_weight_grad.transpose(0, 2, 1, 3).reshape(share, 3 * D)
    late, sums = (small[: 4 * D], small[4 * D :])
    rel_total = sums[8 * D : 8 * D + HDIM * 256].reshape(HDIM, 256).T
    small = sums[: 8 * D]
    return (
        tokens_out,
        tokens_grad,
        late[:D],
        late[D : 2 * D],
        qkv_weight_grad,
        late[2 * D :].reshape(2, D),
        rel_total[:127][::-1],
        rel_total[128:255],
        out_share,
        small[:D],
        small[D : 2 * D],
        small[2 * D : 3 * D],
        fc1_share,
        small[3 * D : 7 * D],
        fc2_share,
        small[7 * D :],
    )


def solution(mesh):
    tokens = P(("dp", "wide"), None, None)
    placed = (tokens,) + (P(),) * 14 + (P("dp"), P("dp", None), P(("dp", "wide"), None), tokens)
    shared = P("wide", None)
    return jax.shard_map(
        shards,
        mesh=mesh,
        in_specs=placed,
        out_specs=(
            tokens, tokens, P(), P(), shared, P(), P(), P(), shared, P(), P(), P(), shared, P(),
            shared, P(),
        ),
        check_vma=False,
    )
```
